128 devices in a mesh: row: 16 (over y, z), col: 8 (over x, core).
Axes of the slice: x: 4, y: 4, z: 4, core: 2. Of those that a mesh axis runs over, the one named last changes fastest.
Arguments:
- tokens: bfloat16 [2048, 4096], P('row', 'col'), may hold values from -6 to 6
- w_in: bfloat16 [4096, 16384], P('col', 'row'), may hold values from -0.09375 to 0.09375
- w_out: bfloat16 [16384, 4096], P('row', 'col'), may hold values from -0.046875 to 0.046875
- cotangent: bfloat16 [2048, 4096], P('row', 'col'), may hold values from -6 to 6
Outputs:
- block_out: bfloat16 [2048, 4096], P(('row', 'col'))
- grad_tokens: bfloat16 [2048, 4096], P('row', 'col')
- grad_in: float32 [4096, 16384], P('col', 'row')
- grad_out: float32 [16384, 4096], P('row', 'col')
The draws below stay inside these ranges and needn't reach their ends.
All inputs are finite; a program needn't handle non-finite values.
Results may differ from the reference program's by a relative error of at most 0.015.
Values may be sent and summed in bfloat16 or wider, within the bound.
A program may use at most 128 MiB of HBM per device.

```python
import jax
import jax.numpy as jnp
from jax import lax

D = 4096
F = 16384
TOKENS = 2048
N_ROW = 16
N_COL = 8


def level_of(key, extent, cuts, least, high):
    level, own = 1.0, jax.random.fold_in(key, 6)
    for position, blocks in cuts:
        steps = jnp.exp(jax.random.uniform(jax.random.fold_in(own, position), (blocks,), jnp.float32, least / len(cuts), high / len(cuts)))
        level = level * jnp.repeat(steps, extent[position] // blocks).reshape([-1 if axis == position else 1 for axis in range(len(extent))])
    return level


def centred(stream_key, extent, scale, limit, pieces=(), dtype=jnp.bfloat16):
    gain = level_of(stream_key, extent, pieces, -0.22, 0.18) if pieces else 1.0
    result = jax.random.normal(stream_key, extent, jnp.float32) * scale * gain
    return jnp.minimum(jnp.maximum(result, -limit), limit).astype(dtype)


def setup_inputs(seed: int = 0) -> dict:
    keys = jax.random.split(jax.random.key(seed), 5)
    return {
        "tokens": centred(keys[0], (TOKENS, D), 1.0, 6.0, ((0, 16), (1, 8))),
        "w_in": centred(keys[1], (D, F), D ** -0.5, 0.09375, ((0, 8), (1, 16))),
        "w_out": centred(keys[2], (F, D), F ** -0.5, 0.046875, ((0, 16), (1, 8))),
        "cotangent": centred(keys[3], (TOKENS, D), 1.0, 6.0, ((0, 16), (1, 8))),
    }


def block_sum(left, right, parts):
    width = left.shape[1] // parts
    total = jnp.zeros((left.shape[0], right.shape[1]), jnp.float32)
    for index in range(parts):
        piece = jnp.dot(left[:, index * width:(index + 1) * width], right[index * width:(index + 1) * width], preferred_element_type=jnp.float32)
        rounded = lax.optimization_barrier(piece.astype(jnp.bfloat16))
        total = total + rounded.astype(jnp.float32)
    return total

def gelu_grad(value):
    cdf = 0.5 * (1.0 + jax.scipy.special.erf(value * 0.7071067811865476))
    pdf = jnp.exp(-0.5 * value * value) * 0.3989422804014327
    return cdf + value * pdf

def reference(tokens, w_in, w_out, cotangent):
    pre = block_sum(tokens, w_in, N_COL)
    act = jax.nn.gelu(pre, approximate=False).astype(jnp.bfloat16)
    block_out = (tokens.astype(jnp.float32) + block_sum(act, w_out, N_ROW)).astype(jnp.bfloat16)
    dact = block_sum(cotangent, w_out.T, N_COL)
    dpre = (dact * gelu_grad(pre)).astype(jnp.bfloat16)
    grad_out = jnp.dot(act.T, cotangent, preferred_element_type=jnp.float32)
    grad_in = jnp.dot(tokens.T, dpre, preferred_element_type=jnp.float32)
    grad_tokens = (cotangent.astype(jnp.float32) + block_sum(dpre, w_in.T, N_ROW)).astype(jnp.bfloat16)
    return (block_out, grad_tokens, grad_in, grad_out)
```

```python
import jax
import jax.numpy as jnp
from jax import lax
from jax.sharding import PartitionSpec as P


def gelu_grad(value):
    cdf = 0.5 * (1.0 + jax.scipy.special.erf(value * 0.7071067811865476))
    pdf = jnp.exp(-0.5 * value * value) * 0.3989422804014327
    return cdf + value * pdf


def token_panel(local_rows):
    return lax.all_gather(local_rows, "row", axis=0, tiled=True)


def token_panel_a2a(local_rows):
    n = lax.axis_size("row")
    copies = jnp.broadcast_to(local_rows[None], (n,) + local_rows.shape)
    copies = copies.reshape(n * local_rows.shape[0], local_rows.shape[1])
    return lax.all_to_all(copies, "row", split_axis=0, concat_axis=0, tiled=True)


def hidden_panel(local_rows):
    return lax.all_gather(local_rows, "col", axis=0, tiled=True)


def contract_last(left, right):
    return lax.dot_general(
        left, right, (((1,), (1,)), ((), ())), preferred_element_type=jnp.float32
    )


def width_split(left_all, right, transposed):
    if transposed:
        term = contract_last(left_all, right)
    else:
        term = jnp.dot(left_all, right, preferred_element_type=jnp.float32)
    return lax.psum_scatter(
        term.astype(jnp.bfloat16), "col", scatter_dimension=0, tiled=True
    ).astype(jnp.float32)


def unit_sum(left_all, right, transposed):
    n = lax.axis_size("row")
    if transposed:
        term = contract_last(left_all, right)
    else:
        term = jnp.dot(left_all, right, preferred_element_type=jnp.float32)
    pieces = term.astype(jnp.bfloat16).reshape(n, term.shape[0] // n, term.shape[1])
    pieces = lax.all_to_all(pieces, "row", split_axis=0, concat_axis=0, tiled=True)
    return jnp.sum(pieces.astype(jnp.float32), axis=0)


def local(tokens, w_in, w_out, cotangent):
    tokens_all = token_panel(tokens)
    upstream_all = token_panel_a2a(cotangent)
    pre_part = width_split(tokens_all, w_in, False)
    act_all = hidden_panel(jax.nn.gelu(pre_part, approximate=False).astype(jnp.bfloat16))
    dact_part = width_split(upstream_all, w_out, True)
    dpre_all = hidden_panel((dact_part * gelu_grad(pre_part)).astype(jnp.bfloat16))
    mixed = unit_sum(act_all, w_out, False)
    block_rows = (tokens.astype(jnp.float32) + mixed).astype(jnp.bfloat16)
    block_out = lax.all_to_all(block_rows, "col", split_axis=0, concat_axis=1, tiled=True)
    grad_out = lax.dot_general(
        act_all, upstream_all, (((0,), (0,)), ((), ())), preferred_element_type=jnp.float32
    )
    grad_in = lax.dot_general(
        tokens_all, dpre_all, (((0,), (0,)), ((), ())), preferred_element_type=jnp.float32
    )
    back = unit_sum(dpre_all, w_in, True)
    grad_tokens = (cotangent.astype(jnp.float32) + back).astype(jnp.bfloat16)
    return (block_out, grad_tokens, grad_in, grad_out)


def solution(mesh):
    in_specs = (P("row", "col"), P("col", "row"), P("row", "col"), P("row", "col"))
    out_specs = (P(("row", "col"), None), P("row", "col"), P("col", "row"), P("row", "col"))
    return jax.shard_map(local, mesh=mesh, in_specs=in_specs, out_specs=out_specs, check_vma=False)
```

```python
import jax
import jax.numpy as jnp
from jax import lax
from jax.sharding import PartitionSpec as P


def gelu_grad(value):
    cdf = 0.5 * (1.0 + jax.scipy.special.erf(value * 0.7071067811865476))
    pdf = jnp.exp(-0.5 * value * value) * 0.3989422804014327
    return cdf + value * pdf


def token_panel(local_rows):
    return lax.all_gather(local_rows, "row", axis=0, tiled=True)


def token_panel_a2a(local_rows):
    n = lax.axis_size("row")
    copies = jnp.broadcast_to(local_rows[None], (n,) + local_rows.shape)
    copies = copies.reshape(n * local_rows.shape[0], local_rows.shape[1])
    return lax.all_to_all(copies, "row", split_axis=0, concat_axis=0, tiled=True)


def hidden_panel(local_rows):
    return lax.all_gather(local_rows, "col", axis=0, tiled=True)


def hidden_panel_a2a(local_rows):
    n = lax.axis_size("col")
    copies = jnp.broadcast_to(local_rows[None], (n,) + local_rows.shape)
    copies = copies.reshape(n * local_rows.shape[0], local_rows.shape[1])
    return lax.all_to_all(copies, "col", split_axis=0, concat_axis=0, tiled=True)


def width_split_a2a(left_all, right, transposed):
    n = lax.axis_size("col")
    if transposed:
        term = contract_last(left_all, right)
    else:
        term = jnp.dot(left_all, right, preferred_element_type=jnp.float32)
    pieces = term.astype(jnp.bfloat16).reshape(n, term.shape[0] // n, term.shape[1])
    pieces = lax.all_to_all(pieces, "col", split_axis=0, concat_axis=0, tiled=True)
    return jnp.sum(pieces.astype(jnp.float32), axis=0)


def contract_last(left, right):
    return lax.dot_general(
        left, right, (((1,), (1,)), ((), ())), preferred_element_type=jnp.float32
    )


def width_split(left_all, right, transposed):
    if transposed:
        term = contract_last(left_all, right)
    else:
        term = jnp.dot(left_all, right, preferred_element_type=jnp.float32)
    return lax.psum_scatter(
        term.astype(jnp.bfloat16), "col", scatter_dimension=0, tiled=True
    ).astype(jnp.float32)


def unit_sum(left_all, right, transposed):
    n = lax.axis_size("row")
    if transposed:
        term = contract_last(left_all, right)
    else:
        term = jnp.dot(left_all, right, preferred_element_type=jnp.float32)
    pieces = term.astype(jnp.bfloat16).reshape(n, term.shape[0] // n, term.shape[1])
    pieces = lax.all_to_all(pieces, "row", split_axis=0, concat_axis=0, tiled=True)
    return jnp.sum(pieces.astype(jnp.float32), axis=0)


def local(tokens, w_in, w_out, cotangent):
    both_all = token_panel_a2a(jnp.stack([tokens, cotangent], axis=1).reshape(2 * tokens.shape[0], tokens.shape[1]))
    both_all = both_all.reshape(-1, 2, tokens.shape[1])
    tokens_all = both_all[:, 0]
    upstream_all = both_all[:, 1]
    pre_part = width_split(tokens_all, w_in, False)
    act_all = hidden_panel(jax.nn.gelu(pre_part, approximate=False).astype(jnp.bfloat16))
    dact_part = width_split_a2a(upstream_all, w_out, True)
    dpre_all = hidden_panel_a2a((dact_part * gelu_grad(pre_part)).astype(jnp.bfloat16))
    mixed = unit_sum(act_all, w_out, False)
    block_rows = (tokens.astype(jnp.float32) + mixed).astype(jnp.bfloat16)
    block_out = lax.all_to_all(block_rows, "col", split_axis=0, concat_axis=1, tiled=True)
    grad_out = lax.dot_general(
        act_all, upstream_all, (((0,), (0,)), ((), ())), preferred_element_type=jnp.float32
    )
    grad_in = lax.dot_general(
        tokens_all, dpre_all, (((0,), (0,)), ((), ())), preferred_element_type=jnp.float32
    )
    back = unit_sum(dpre_all, w_in, True)
    grad_tokens = (cotangent.astype(jnp.float32) + back).astype(jnp.bfloat16)
    return (block_out, grad_tokens, grad_in, grad_out)


def solution(mesh):
    in_specs = (P("row", "col"), P("col", "row"), P("row", "col"), P("row", "col"))
    out_specs = (P(("row", "col"), None), P("row", "col"), P("col", "row"), P("row", "col"))
    return jax.shard_map(local, mesh=mesh, in_specs=in_specs, out_specs=out_specs, check_vma=False)
```

```python
import jax
import jax.numpy as jnp
from jax import lax
from jax.sharding import PartitionSpec as P
import functools
from jax.experimental import pallas as pl
from jax.experimental.pallas import tpu as pltpu

MESH = pl.DeviceIdType.MESH


def _col_ids(nx):
    me = lax.axis_index("col")
    x = me // 2
    k = me % 2
    d = 1 - 2 * k
    nxt = lax.rem(x + nx + d, nx)
    prv = lax.rem(x + nx - d, nx)
    return x, k, d, nxt, prv


def _greet(row, k, x, nxt, prv):
    barrier = pltpu.get_barrier_semaphore()
    for peer in (2 * x + 1 - k, 2 * nxt + k, 2 * prv + k):
        pl.semaphore_signal(barrier, inc=1, device_id=(row, peer), device_id_type=MESH)
    pl.semaphore_wait(barrier, 3)


def _rs_kernel(nx, narr, *refs):
    parts = refs[:narr]
    outs = refs[narr:2 * narr]
    recv1, vsum, sendbuf, recv2, s1, r1, s2, r2 = refs[2 * narr:]
    row = lax.axis_index("row")
    x, k, d, nxt, prv = _col_ids(nx)
    _greet(row, k, x, nxt, prv)
    partner = (row, 2 * x + 1 - k)
    nextdev = (row, 2 * nxt + k)
    first = []
    for a in range(narr):
        for i in range(nx):
            cp = pltpu.make_async_remote_copy(
                src_ref=parts[a].at[2 * i + 1 - k], dst_ref=recv1.at[a, i],
                send_sem=s1.at[a, i], recv_sem=r1.at[a, i],
                device_id=partner, device_id_type=MESH)
            cp.start()
            first.append(cp)
    for cp in first:
        cp.wait()
    for a in range(narr):
        for i in range(nx):
            vsum[a, i] = parts[a][2 * i + k].astype(jnp.float32) + recv1[a, i].astype(jnp.float32)
    ring = []
    for step in range(nx - 1):
        for a in range(narr):
            src_idx = lax.rem(x + 4 * nx - d * (step + 1), nx)
            if step == 0:
                sendbuf[a, step] = vsum[a, src_idx].astype(sendbuf.dtype)
            else:
                prevcp = ring[(step - 1) * narr + a]
                prevcp.wait_recv()
                sendbuf[a, step] = (recv2[a, step - 1].astype(jnp.float32) + vsum[a, src_idx]).astype(sendbuf.dtype)
            cp = pltpu.make_async_remote_copy(
                src_ref=sendbuf.at[a, step], dst_ref=recv2.at[a, step],
                send_sem=s2.at[a, step], recv_sem=r2.at[a, step],
                device_id=nextdev, device_id_type=MESH)
            cp.start()
            ring.append(cp)
    for a in range(narr):
        last = ring[(nx - 2) * narr + a]
        last.wait_recv()
        outs[a][...] = recv2[a, nx - 2].astype(jnp.float32) + vsum[a, x]
    for cp in ring:
        cp.wait_send()


def col_reduce_scatter(arrays, cid):
    n = lax.axis_size("col")
    nx = n // 2
    narr = len(arrays)
    rows = arrays[0].shape[0] // n
    cols = arrays[0].shape[1]
    parts = [a.reshape(n, rows, cols) for a in arrays]
    return pl.pallas_call(
        functools.partial(_rs_kernel, nx, narr),
        out_shape=[jax.ShapeDtypeStruct((rows, cols), jnp.float32)] * narr,
        in_specs=[pl.BlockSpec(memory_space=pltpu.VMEM)] * narr,
        out_specs=[pl.BlockSpec(memory_space=pltpu.VMEM)] * narr,
        scratch_shapes=[
            pltpu.VMEM((narr, nx, rows, cols), jnp.bfloat16),
            pltpu.VMEM((narr, nx, rows, cols), jnp.float32),
            pltpu.VMEM((narr, nx - 1, rows, cols), jnp.bfloat16),
            pltpu.VMEM((narr, nx - 1, rows, cols), jnp.bfloat16),
            pltpu.SemaphoreType.DMA((narr, nx)),
            pltpu.SemaphoreType.DMA((narr, nx)),
            pltpu.SemaphoreType.DMA((narr, nx - 1)),
            pltpu.SemaphoreType.DMA((narr, nx - 1)),
        ],
        compiler_params=pltpu.CompilerParams(collective_id=cid, has_side_effects=True,
                                             vmem_limit_bytes=64 * 1024 * 1024),
    )(*parts)


def _ag_kernel(nx, narr, *refs):
    chunks = refs[:narr]
    outs = refs[narr:2 * narr]
    sr, rr, sc, rc = refs[2 * narr:]
    row = lax.axis_index("row")
    x, k, d, nxt, prv = _col_ids(nx)
    _greet(row, k, x, nxt, prv)
    me = 2 * x + k
    partner = (row, 2 * x + 1 - k)
    nextdev = (row, 2 * nxt + k)
    for a in range(narr):
        outs[a][me] = chunks[a][...]
    ring, core = [], []
    for step in range(nx):
        for a in range(narr):
            src_x = lax.rem(x + 4 * nx - d * step, nx)
            slot = 2 * src_x + k
            if step > 0:
                ring[(step - 1) * narr + a].wait_recv()
            src = chunks[a] if step == 0 else outs[a].at[slot]
            if step < nx - 1:
                cp = pltpu.make_async_remote_copy(
                    src_ref=src, dst_ref=outs[a].at[slot],
                    send_sem=sr.at[a, step], recv_sem=rr.at[a, step],
                    device_id=nextdev, device_id_type=MESH)
                cp.start()
                ring.append(cp)
            cc = pltpu.make_async_remote_copy(
                src_ref=src, dst_ref=outs[a].at[slot],
                send_sem=sc.at[a, step], recv_sem=rc.at[a, step],
                device_id=partner, device_id_type=MESH)
            cc.start()
            core.append(cc)
    for cp in ring:
        cp.wait_send()
    for cc in core:
        cc.wait()


def col_all_gather(arrays, cid):
    n = lax.axis_size("col")
    nx = n // 2
    narr = len(arrays)
    rows, cols = arrays[0].shape
    outs = pl.pallas_call(
        functools.partial(_ag_kernel, nx, narr),
        out_shape=[jax.ShapeDtypeStruct((n, rows, cols), arrays[0].dtype)] * narr,
        in_specs=[pl.BlockSpec(memory_space=pltpu.VMEM)] * narr,
        out_specs=[pl.BlockSpec(memory_space=pltpu.VMEM)] * narr,
        scratch_shapes=[
            pltpu.SemaphoreType.DMA((narr, nx)),
            pltpu.SemaphoreType.DMA((narr, nx)),
            pltpu.SemaphoreType.DMA((narr, nx)),
            pltpu.SemaphoreType.DMA((narr, nx)),
        ],
        compiler_params=pltpu.CompilerParams(collective_id=cid, has_side_effects=True,
                                             vmem_limit_bytes=64 * 1024 * 1024),
    )(*arrays)
    return [o.reshape(n * rows, cols) for o in outs]


def gelu_grad(value):
    cdf = 0.5 * (1.0 + jax.scipy.special.erf(value * 0.7071067811865476))
    pdf = jnp.exp(-0.5 * value * value) * 0.3989422804014327
    return cdf + value * pdf


def token_panel(local_rows):
    return lax.all_gather(local_rows, "row", axis=0, tiled=True)


def token_panel_a2a(local_rows):
    n = lax.axis_size("row")
    copies = jnp.broadcast_to(local_rows[None], (n,) + local_rows.shape)
    copies = copies.reshape(n * local_rows.shape[0], local_rows.shape[1])
    return lax.all_to_all(copies, "row", split_axis=0, concat_axis=0, tiled=True)


def hidden_panel(local_rows):
    return lax.all_gather(local_rows, "col", axis=0, tiled=True)


def contract_last(left, right):
    return lax.dot_general(
        left, right, (((1,), (1,)), ((), ())), preferred_element_type=jnp.float32
    )


def width_split(left_all, right, transposed):
    if transposed:
        term = contract_last(left_all, right)
    else:
        term = jnp.dot(left_all, right, preferred_element_type=jnp.float32)
    return lax.psum_scatter(
        term.astype(jnp.bfloat16), "col", scatter_dimension=0, tiled=True
    ).astype(jnp.float32)


def unit_sum(left_all, right, transposed):
    n = lax.axis_size("row")
    if transposed:
        term = contract_last(left_all, right)
    else:
        term = jnp.dot(left_all, right, preferred_element_type=jnp.float32)
    pieces = term.astype(jnp.bfloat16).reshape(n, term.shape[0] // n, term.shape[1])
    pieces = lax.all_to_all(pieces, "row", split_axis=0, concat_axis=0, tiled=True)
    return jnp.sum(pieces.astype(jnp.float32), axis=0)


def local(tokens, w_in, w_out, cotangent):
    tokens_all = token_panel(tokens)
    upstream_all = token_panel_a2a(cotangent)
    pre_term = jnp.dot(tokens_all, w_in, preferred_element_type=jnp.float32).astype(jnp.bfloat16)
    dact_term = contract_last(upstream_all, w_out).astype(jnp.bfloat16)
    pre_part, dact_part = col_reduce_scatter([pre_term, dact_term], 1)
    act = jax.nn.gelu(pre_part, approximate=False).astype(jnp.bfloat16)
    dpre = (dact_part * gelu_grad(pre_part)).astype(jnp.bfloat16)
    act_all, dpre_all = col_all_gather([act, dpre], 2)
    mixed = unit_sum(act_all, w_out, False)
    block_rows = (tokens.astype(jnp.float32) + mixed).astype(jnp.bfloat16)
    block_out = lax.all_to_all(block_rows, "col", split_axis=0, concat_axis=1, tiled=True)
    grad_out = lax.dot_general(
        act_all, upstream_all, (((0,), (0,)), ((), ())), preferred_element_type=jnp.float32
    )
    grad_in = lax.dot_general(
        tokens_all, dpre_all, (((0,), (0,)), ((), ())), preferred_element_type=jnp.float32
    )
    back = unit_sum(dpre_all, w_in, True)
    grad_tokens = (cotangent.astype(jnp.float32) + back).astype(jnp.bfloat16)
    return (block_out, grad_tokens, grad_in, grad_out)


def solution(mesh):
    in_specs = (P("row", "col"), P("col", "row"), P("row", "col"), P("row", "col"))
    out_specs = (P(("row", "col"), None), P("row", "col"), P("col", "row"), P("row", "col"))
    return jax.shard_map(local, mesh=mesh, in_specs=in_specs, out_specs=out_specs, check_vma=False)
```

```python
import jax
import jax.numpy as jnp
from jax import lax
from jax.sharding import PartitionSpec as P
import functools
from jax.experimental import pallas as pl
from jax.experimental.pallas import tpu as pltpu

MESH = pl.DeviceIdType.MESH


def _col_ids(nx):
    me = lax.axis_index("col")
    x = me // 2
    k = me % 2
    d = 1 - 2 * k
    nxt = lax.rem(x + nx + d, nx)
    prv = lax.rem(x + nx - d, nx)
    return x, k, d, nxt, prv


def _greet(row, k, x, nxt, prv):
    barrier = pltpu.get_barrier_semaphore()
    for peer in (2 * x + 1 - k, 2 * nxt + k, 2 * prv + k):
        pl.semaphore_signal(barrier, inc=1, device_id=(row, peer), device_id_type=MESH)
    pl.semaphore_wait(barrier, 3)


def _rs_kernel(nx, narr, *refs):
    parts = refs[:narr]
    outs = refs[narr:2 * narr]
    recv1, vsum, sendbuf, recv2, s1, r1, s2, r2 = refs[2 * narr:]
    row = lax.axis_index("row")
    x, k, d, nxt, prv = _col_ids(nx)
    _greet(row, k, x, nxt, prv)
    partner = (row, 2 * x + 1 - k)
    nextdev = (row, 2 * nxt + k)
    first = []
    for a in range(narr):
        for i in range(nx):
            cp = pltpu.make_async_remote_copy(
                src_ref=parts[a].at[2 * i + 1 - k], dst_ref=recv1.at[a, i],
                send_sem=s1.at[a, i], recv_sem=r1.at[a, i],
                device_id=partner, device_id_type=MESH)
            cp.start()
            first.append(cp)
    for cp in first:
        cp.wait()
    for a in range(narr):
        for i in range(nx):
            vsum[a, i] = parts[a][2 * i + k].astype(jnp.float32) + recv1[a, i].astype(jnp.float32)
    ring = []
    for step in range(nx - 1):
        for a in range(narr):
            src_idx = lax.rem(x + 4 * nx - d * (step + 1), nx)
            if step == 0:
                sendbuf[a, step] = vsum[a, src_idx].astype(sendbuf.dtype)
            else:
                prevcp = ring[(step - 1) * narr + a]
                prevcp.wait_recv()
                sendbuf[a, step] = (recv2[a, step - 1].astype(jnp.float32) + vsum[a, src_idx]).astype(sendbuf.dtype)
            cp = pltpu.make_async_remote_copy(
                src_ref=sendbuf.at[a, step], dst_ref=recv2.at[a, step],
                send_sem=s2.at[a, step], recv_sem=r2.at[a, step],
                device_id=nextdev, device_id_type=MESH)
            cp.start()
            ring.append(cp)
    for a in range(narr):
        last = ring[(nx - 2) * narr + a]
        last.wait_recv()
        outs[a][...] = recv2[a, nx - 2].astype(jnp.float32) + vsum[a, x]
    for cp in ring:
        cp.wait_send()


def col_reduce_scatter(arrays, cid):
    n = lax.axis_size("col")
    nx = n // 2
    narr = len(arrays)
    rows = arrays[0].shape[0] // n
    cols = arrays[0].shape[1]
    parts = [a.reshape(n, rows, cols) for a in arrays]
    return pl.pallas_call(
        functools.partial(_rs_kernel, nx, narr),
        out_shape=[jax.ShapeDtypeStruct((rows, cols), jnp.float32)] * narr,
        in_specs=[pl.BlockSpec(memory_space=pltpu.VMEM)] * narr,
        out_specs=[pl.BlockSpec(memory_space=pltpu.VMEM)] * narr,
        scratch_shapes=[
            pltpu.VMEM((narr, nx, rows, cols), jnp.bfloat16),
            pltpu.VMEM((narr, nx, rows, cols), jnp.float32),
            pltpu.VMEM((narr, nx - 1, rows, cols), jnp.bfloat16),
            pltpu.VMEM((narr, nx - 1, rows, cols), jnp.bfloat16),
            pltpu.SemaphoreType.DMA((narr, nx)),
            pltpu.SemaphoreType.DMA((narr, nx)),
            pltpu.SemaphoreType.DMA((narr, nx - 1)),
            pltpu.SemaphoreType.DMA((narr, nx - 1)),
        ],
        compiler_params=pltpu.CompilerParams(collective_id=cid, has_side_effects=True,
                                             vmem_limit_bytes=64 * 1024 * 1024),
    )(*parts)


def _ag_kernel(nx, narr, *refs):
    chunks = refs[:narr]
    outs = refs[narr:2 * narr]
    sr, rr, sc, rc = refs[2 * narr:]
    row = lax.axis_index("row")
    x, k, d, nxt, prv = _col_ids(nx)
    _greet(row, k, x, nxt, prv)
    me = 2 * x + k
    partner = (row, 2 * x + 1 - k)
    nextdev = (row, 2 * nxt + k)
    for a in range(narr):
        outs[a][me] = chunks[a][...]
    ring, core = [], []
    for step in range(nx):
        for a in range(narr):
            src_x = lax.rem(x + 4 * nx - d * step, nx)
            slot = 2 * src_x + k
            if step > 0:
                ring[(step - 1) * narr + a].wait_recv()
            src = chunks[a] if step == 0 else outs[a].at[slot]
            if step < nx - 1:
                cp = pltpu.make_async_remote_copy(
                    src_ref=src, dst_ref=outs[a].at[slot],
                    send_sem=sr.at[a, step], recv_sem=rr.at[a, step],
                    device_id=nextdev, device_id_type=MESH)
                cp.start()
                ring.append(cp)
            cc = pltpu.make_async_remote_copy(
                src_ref=src, dst_ref=outs[a].at[slot],
                send_sem=sc.at[a, step], recv_sem=rc.at[a, step],
                device_id=partner, device_id_type=MESH)
            cc.start()
            core.append(cc)
    for cp in ring:
        cp.wait_send()
    for cc in core:
        cc.wait()


def col_all_gather(arrays, cid):
    n = lax.axis_size("col")
    nx = n // 2
    narr = len(arrays)
    rows, cols = arrays[0].shape
    outs = pl.pallas_call(
        functools.partial(_ag_kernel, nx, narr),
        out_shape=[jax.ShapeDtypeStruct((n, rows, cols), arrays[0].dtype)] * narr,
        in_specs=[pl.BlockSpec(memory_space=pltpu.VMEM)] * narr,
        out_specs=[pl.BlockSpec(memory_space=pltpu.VMEM)] * narr,
        scratch_shapes=[
            pltpu.SemaphoreType.DMA((narr, nx)),
            pltpu.SemaphoreType.DMA((narr, nx)),
            pltpu.SemaphoreType.DMA((narr, nx)),
            pltpu.SemaphoreType.DMA((narr, nx)),
        ],
        compiler_params=pltpu.CompilerParams(collective_id=cid, has_side_effects=True,
                                             vmem_limit_bytes=64 * 1024 * 1024),
    )(*arrays)
    return [o.reshape(n * rows, cols) for o in outs]


def gelu_grad(value):
    cdf = 0.5 * (1.0 + jax.scipy.special.erf(value * 0.7071067811865476))
    pdf = jnp.exp(-0.5 * value * value) * 0.3989422804014327
    return cdf + value * pdf


def token_panel(local_rows):
    return lax.all_gather(local_rows, "row", axis=0, tiled=True)


def token_panel_a2a(local_rows):
    n = lax.axis_size("row")
    copies = jnp.broadcast_to(local_rows[None], (n,) + local_rows.shape)
    copies = copies.reshape(n * local_rows.shape[0], local_rows.shape[1])
    return lax.all_to_all(copies, "row", split_axis=0, concat_axis=0, tiled=True)


def hidden_panel(local_rows):
    return lax.all_gather(local_rows, "col", axis=0, tiled=True)


def contract_last(left, right):
    return lax.dot_general(
        left, right, (((1,), (1,)), ((), ())), preferred_element_type=jnp.float32
    )


def width_split(left_all, right, transposed):
    if transposed:
        term = contract_last(left_all, right)
    else:
        term = jnp.dot(left_all, right, preferred_element_type=jnp.float32)
    return lax.psum_scatter(
        term.astype(jnp.bfloat16), "col", scatter_dimension=0, tiled=True
    ).astype(jnp.float32)


def unit_sum(left_all, right, transposed):
    n = lax.axis_size("row")
    if transposed:
        term = contract_last(left_all, right)
    else:
        term = jnp.dot(left_all, right, preferred_element_type=jnp.float32)
    pieces = term.astype(jnp.bfloat16).reshape(n, term.shape[0] // n, term.shape[1])
    pieces = lax.all_to_all(pieces, "row", split_axis=0, concat_axis=0, tiled=True)
    return jnp.sum(pieces.astype(jnp.float32), axis=0)


def local(tokens, w_in, w_out, cotangent):
    tokens_all = token_panel_a2a(tokens)
    upstream_all = token_panel(cotangent)
    pre_term = jnp.dot(tokens_all, w_in, preferred_element_type=jnp.float32).astype(jnp.bfloat16)
    (pre_part,) = col_reduce_scatter([pre_term], 1)
    act = jax.nn.gelu(pre_part, approximate=False).astype(jnp.bfloat16)
    (act_all,) = col_all_gather([act], 2)
    mixed = unit_sum(act_all, w_out, False)
    dact_term = contract_last(upstream_all, w_out).astype(jnp.bfloat16)
    (dact_part,) = col_reduce_scatter([dact_term], 3)
    dpre = (dact_part * gelu_grad(pre_part)).astype(jnp.bfloat16)
    (dpre_all,) = col_all_gather([dpre], 4)
    block_rows = (tokens.astype(jnp.float32) + mixed).astype(jnp.bfloat16)
    block_out = lax.all_to_all(block_rows, "col", split_axis=0, concat_axis=1, tiled=True)
    grad_out = lax.dot_general(
        act_all, upstream_all, (((0,), (0,)), ((), ())), preferred_element_type=jnp.float32
    )
    grad_in = lax.dot_general(
        tokens_all, dpre_all, (((0,), (0,)), ((), ())), preferred_element_type=jnp.float32
    )
    back = unit_sum(dpre_all, w_in, True)
    grad_tokens = (cotangent.astype(jnp.float32) + back).astype(jnp.bfloat16)
    return (block_out, grad_tokens, grad_in, grad_out)


def solution(mesh):
    in_specs = (P("row", "col"), P("col", "row"), P("row", "col"), P("row", "col"))
    out_specs = (P(("row", "col"), None), P("row", "col"), P("col", "row"), P("row", "col"))
    return jax.shard_map(local, mesh=mesh, in_specs=in_specs, out_specs=out_specs, check_vma=False)
```

```python
import jax
import jax.numpy as jnp
from jax import lax
from jax.sharding import PartitionSpec as P
import functools
from jax.experimental import pallas as pl
from jax.experimental.pallas import tpu as pltpu

MESH = pl.DeviceIdType.MESH


def _col_ids(nx):
    me = lax.axis_index("col")
    x = me // 2
    k = me % 2
    d = 1 - 2 * k
    nxt = lax.rem(x + nx + d, nx)
    prv = lax.rem(x + nx - d, nx)
    return x, k, d, nxt, prv


def _greet(row, k, x, nxt, prv):
    barrier = pltpu.get_barrier_semaphore()
    for peer in (2 * x + 1 - k, 2 * nxt + k, 2 * prv + k):
        pl.semaphore_signal(barrier, inc=1, device_id=(row, peer), device_id_type=MESH)
    pl.semaphore_wait(barrier, 3)


def _rs_kernel(nx, narr, *refs):
    parts = refs[:narr]
    outs = refs[narr:2 * narr]
    recv1, vsum, sendbuf, recv2, s1, r1, s2, r2 = refs[2 * narr:]
    row = lax.axis_index("row")
    x, k, d, nxt, prv = _col_ids(nx)
    _greet(row, k, x, nxt, prv)
    partner = (row, 2 * x + 1 - k)
    nextdev = (row, 2 * nxt + k)
    first = []
    for a in range(narr):
        for i in range(nx):
            cp = pltpu.make_async_remote_copy(
                src_ref=parts[a].at[2 * i + 1 - k], dst_ref=recv1.at[a, i],
                send_sem=s1.at[a, i], recv_sem=r1.at[a, i],
                device_id=partner, device_id_type=MESH)
            cp.start()
            first.append(cp)
    for cp in first:
        cp.wait()
    for a in range(narr):
        for i in range(nx):
            vsum[a, i] = parts[a][2 * i + k].astype(jnp.float32) + recv1[a, i].astype(jnp.float32)
    ring = []
    for step in range(nx - 1):
        for a in range(narr):
            src_idx = lax.rem(x + 4 * nx - d * (step + 1), nx)
            if step == 0:
                sendbuf[a, step] = vsum[a, src_idx].astype(sendbuf.dtype)
            else:
                prevcp = ring[(step - 1) * narr + a]
                prevcp.wait_recv()
                sendbuf[a, step] = (recv2[a, step - 1].astype(jnp.float32) + vsum[a, src_idx]).astype(sendbuf.dtype)
            cp = pltpu.make_async_remote_copy(
                src_ref=sendbuf.at[a, step], dst_ref=recv2.at[a, step],
                send_sem=s2.at[a, step], recv_sem=r2.at[a, step],
                device_id=nextdev, device_id_type=MESH)
            cp.start()
            ring.append(cp)
    for a in range(narr):
        last = ring[(nx - 2) * narr + a]
        last.wait_recv()
        outs[a][...] = recv2[a, nx - 2].astype(jnp.float32) + vsum[a, x]
    for cp in ring:
        cp.wait_send()


def col_reduce_scatter(arrays, cid):
    n = lax.axis_size("col")
    nx = n // 2
    narr = len(arrays)
    rows = arrays[0].shape[0] // n
    cols = arrays[0].shape[1]
    parts = [a.reshape(n, rows, cols) for a in arrays]
    return pl.pallas_call(
        functools.partial(_rs_kernel, nx, narr),
        out_shape=[jax.ShapeDtypeStruct((rows, cols), jnp.float32)] * narr,
        in_specs=[pl.BlockSpec(memory_space=pltpu.VMEM)] * narr,
        out_specs=[pl.BlockSpec(memory_space=pltpu.VMEM)] * narr,
        scratch_shapes=[
            pltpu.VMEM((narr, nx, rows, cols), jnp.bfloat16),
            pltpu.VMEM((narr, nx, rows, cols), jnp.float32),
            pltpu.VMEM((narr, nx - 1, rows, cols), jnp.bfloat16),
            pltpu.VMEM((narr, nx - 1, rows, cols), jnp.bfloat16),
            pltpu.SemaphoreType.DMA((narr, nx)),
            pltpu.SemaphoreType.DMA((narr, nx)),
            pltpu.SemaphoreType.DMA((narr, nx - 1)),
            pltpu.SemaphoreType.DMA((narr, nx - 1)),
        ],
        compiler_params=pltpu.CompilerParams(collective_id=cid, has_side_effects=True,
                                             vmem_limit_bytes=64 * 1024 * 1024),
    )(*parts)


def _ag_kernel(nx, narr, *refs):
    chunks = refs[:narr]
    weights = refs[narr:2 * narr]
    outs = refs[2 * narr:3 * narr]
    prods = refs[3 * narr:4 * narr]
    sr, rr, sc, rc = refs[4 * narr:]
    row = lax.axis_index("row")
    x, k, d, nxt, prv = _col_ids(nx)
    _greet(row, k, x, nxt, prv)
    me = 2 * x + k
    partner = (row, 2 * x + 1 - k)
    nextdev = (row, 2 * nxt + k)

    def product(a, slot):
        prods[a][slot] = jnp.dot(outs[a][slot], weights[a][...],
                                 preferred_element_type=jnp.float32).astype(prods[a].dtype)

    for a in range(narr):
        outs[a][me] = chunks[a][...]
    ring, core = [], []
    for step in range(nx):
        for a in range(narr):
            src_x = lax.rem(x + 4 * nx - d * step, nx)
            slot = 2 * src_x + k
            if step > 0:
                ring[(step - 1) * narr + a].wait_recv()
            src = chunks[a] if step == 0 else outs[a].at[slot]
            if step < nx - 1:
                cp = pltpu.make_async_remote_copy(
                    src_ref=src, dst_ref=outs[a].at[slot],
                    send_sem=sr.at[a, step], recv_sem=rr.at[a, step],
                    device_id=nextdev, device_id_type=MESH)
                cp.start()
                ring.append(cp)
            cc = pltpu.make_async_remote_copy(
                src_ref=src, dst_ref=outs[a].at[slot],
                send_sem=sc.at[a, step], recv_sem=rc.at[a, step],
                device_id=partner, device_id_type=MESH)
            cc.start()
            core.append(cc)
        for a in range(narr):
            product(a, 2 * lax.rem(x + 4 * nx - d * step, nx) + k)
    for cp in ring:
        cp.wait_send()
    for step in range(nx):
        for a in range(narr):
            core[step * narr + a].wait()
        for a in range(narr):
            product(a, 2 * lax.rem(x + 4 * nx + d * step, nx) + 1 - k)


def col_all_gather(arrays, weights, cid):
    n = lax.axis_size("col")
    nx = n // 2
    narr = len(arrays)
    rows, cols = arrays[0].shape
    width = weights[0].shape[1]
    res = pl.pallas_call(
        functools.partial(_ag_kernel, nx, narr),
        out_shape=[jax.ShapeDtypeStruct((n, rows, cols), arrays[0].dtype)] * narr
        + [jax.ShapeDtypeStruct((n, rows, width), jnp.bfloat16)] * narr,
        in_specs=[pl.BlockSpec(memory_space=pltpu.VMEM)] * (2 * narr),
        out_specs=[pl.BlockSpec(memory_space=pltpu.VMEM)] * (2 * narr),
        scratch_shapes=[
            pltpu.SemaphoreType.DMA((narr, nx)),
            pltpu.SemaphoreType.DMA((narr, nx)),
            pltpu.SemaphoreType.DMA((narr, nx)),
            pltpu.SemaphoreType.DMA((narr, nx)),
        ],
        compiler_params=pltpu.CompilerParams(collective_id=cid, has_side_effects=True,
                                             vmem_limit_bytes=64 * 1024 * 1024),
    )(*arrays, *weights)
    gathered = [o.reshape(n * rows, cols) for o in res[:narr]]
    products = [o.reshape(n * rows, width) for o in res[narr:]]
    return gathered, products


def gelu_grad(value):
    cdf = 0.5 * (1.0 + jax.scipy.special.erf(value * 0.7071067811865476))
    pdf = jnp.exp(-0.5 * value * value) * 0.3989422804014327
    return cdf + value * pdf


def token_panel(local_rows):
    return lax.all_gather(local_rows, "row", axis=0, tiled=True)


def token_panel_a2a(local_rows):
    n = lax.axis_size("row")
    copies = jnp.broadcast_to(local_rows[None], (n,) + local_rows.shape)
    copies = copies.reshape(n * local_rows.shape[0], local_rows.shape[1])
    return lax.all_to_all(copies, "row", split_axis=0, concat_axis=0, tiled=True)


def hidden_panel(local_rows):
    return lax.all_gather(local_rows, "col", axis=0, tiled=True)


def contract_last(left, right):
    return lax.dot_general(
        left, right, (((1,), (1,)), ((), ())), preferred_element_type=jnp.float32
    )


def width_split(left_all, right, transposed):
    if transposed:
        term = contract_last(left_all, right)
    else:
        term = jnp.dot(left_all, right, preferred_element_type=jnp.float32)
    return lax.psum_scatter(
        term.astype(jnp.bfloat16), "col", scatter_dimension=0, tiled=True
    ).astype(jnp.float32)


def unit_sum(left_all, right, transposed):
    n = lax.axis_size("row")
    if transposed:
        term = contract_last(left_all, right)
    else:
        term = jnp.dot(left_all, right, preferred_element_type=jnp.float32)
    pieces = term.astype(jnp.bfloat16).reshape(n, term.shape[0] // n, term.shape[1])
    pieces = lax.all_to_all(pieces, "row", split_axis=0, concat_axis=0, tiled=True)
    return jnp.sum(pieces.astype(jnp.float32), axis=0)


def row_sum(term):
    n = lax.axis_size("row")
    pieces = term.reshape(n, term.shape[0] // n, term.shape[1])
    pieces = lax.all_to_all(pieces, "row", split_axis=0, concat_axis=0, tiled=True)
    return jnp.sum(pieces.astype(jnp.float32), axis=0)


def local(tokens, w_in, w_out, cotangent):
    tokens_all = token_panel(tokens)
    upstream_all = token_panel_a2a(cotangent)
    pre_term = jnp.dot(tokens_all, w_in, preferred_element_type=jnp.float32).astype(jnp.bfloat16)
    dact_term = contract_last(upstream_all, w_out).astype(jnp.bfloat16)
    pre_part, dact_part = col_reduce_scatter([pre_term, dact_term], 1)
    act = jax.nn.gelu(pre_part, approximate=False).astype(jnp.bfloat16)
    dpre = (dact_part * gelu_grad(pre_part)).astype(jnp.bfloat16)
    (act_all, dpre_all), (mixed_term, back_term) = col_all_gather([act, dpre], [w_out, w_in.T], 2)
    mixed = row_sum(mixed_term)
    block_rows = (tokens.astype(jnp.float32) + mixed).astype(jnp.bfloat16)
    block_out = lax.all_to_all(block_rows, "col", split_axis=0, concat_axis=1, tiled=True)
    grad_out = lax.dot_general(
        act_all, upstream_all, (((0,), (0,)), ((), ())), preferred_element_type=jnp.float32
    )
    grad_in = lax.dot_general(
        tokens_all, dpre_all, (((0,), (0,)), ((), ())), preferred_element_type=jnp.float32
    )
    back = row_sum(back_term)
    grad_tokens = (cotangent.astype(jnp.float32) + back).astype(jnp.bfloat16)
    return (block_out, grad_tokens, grad_in, grad_out)


def solution(mesh):
    in_specs = (P("row", "col"), P("col", "row"), P("row", "col"), P("row", "col"))
    out_specs = (P(("row", "col"), None), P("row", "col"), P("col", "row"), P("row", "col"))
    return jax.shard_map(local, mesh=mesh, in_specs=in_specs, out_specs=out_specs, check_vma=False)
```

```python
import jax
import jax.numpy as jnp
from jax import lax
from jax.sharding import PartitionSpec as P
import functools
from jax.experimental import pallas as pl
from jax.experimental.pallas import tpu as pltpu

MESH = pl.DeviceIdType.MESH


def _col_ids(nx):
    me = lax.axis_index("col")
    x = me // 2
    k = me % 2
    d = 1 - 2 * k
    nxt = lax.rem(x + nx + d, nx)
    prv = lax.rem(x + nx - d, nx)
    return x, k, d, nxt, prv


def _greet(row, k, x, nxt, prv):
    barrier = pltpu.get_barrier_semaphore()
    for peer in (2 * x + 1 - k, 2 * nxt + k, 2 * prv + k):
        pl.semaphore_signal(barrier, inc=1, device_id=(row, peer), device_id_type=MESH)
    pl.semaphore_wait(barrier, 3)


def _rs_kernel(nx, narr, *refs):
    parts = refs[:narr]
    outs = refs[narr:2 * narr]
    recv1, vsum, sendbuf, recv2, s1, r1, s2, r2 = refs[2 * narr:]
    row = lax.axis_index("row")
    x, k, d, nxt, prv = _col_ids(nx)
    _greet(row, k, x, nxt, prv)
    partner = (row, 2 * x + 1 - k)
    nextdev = (row, 2 * nxt + k)
    first = []
    for a in range(narr):
        for i in range(nx):
            cp = pltpu.make_async_remote_copy(
                src_ref=parts[a].at[2 * i + 1 - k], dst_ref=recv1.at[a, i],
                send_sem=s1.at[a, i], recv_sem=r1.at[a, i],
                device_id=partner, device_id_type=MESH)
            cp.start()
            first.append(cp)
    for cp in first:
        cp.wait()
    for a in range(narr):
        for i in range(nx):
            vsum[a, i] = parts[a][2 * i + k].astype(jnp.float32) + recv1[a, i].astype(jnp.float32)
    ring = []
    for step in range(nx - 1):
        for a in range(narr):
            src_idx = lax.rem(x + 4 * nx - d * (step + 1), nx)
            if step == 0:
                sendbuf[a, step] = vsum[a, src_idx].astype(sendbuf.dtype)
            else:
                prevcp = ring[(step - 1) * narr + a]
                prevcp.wait_recv()
                sendbuf[a, step] = (recv2[a, step - 1].astype(jnp.float32) + vsum[a, src_idx]).astype(sendbuf.dtype)
            cp = pltpu.make_async_remote_copy(
                src_ref=sendbuf.at[a, step], dst_ref=recv2.at[a, step],
                send_sem=s2.at[a, step], recv_sem=r2.at[a, step],
                device_id=nextdev, device_id_type=MESH)
            cp.start()
            ring.append(cp)
    for a in range(narr):
        last = ring[(nx - 2) * narr + a]
        last.wait_recv()
        outs[a][...] = recv2[a, nx - 2].astype(jnp.float32) + vsum[a, x]
    for cp in ring:
        cp.wait_send()


def col_reduce_scatter(arrays, cid):
    n = lax.axis_size("col")
    nx = n // 2
    narr = len(arrays)
    rows = arrays[0].shape[0] // n
    cols = arrays[0].shape[1]
    parts = [a.reshape(n, rows, cols) for a in arrays]
    return pl.pallas_call(
        functools.partial(_rs_kernel, nx, narr),
        out_shape=[jax.ShapeDtypeStruct((rows, cols), jnp.float32)] * narr,
        in_specs=[pl.BlockSpec(memory_space=pltpu.VMEM)] * narr,
        out_specs=[pl.BlockSpec(memory_space=pltpu.VMEM)] * narr,
        scratch_shapes=[
            pltpu.VMEM((narr, nx, rows, cols), jnp.bfloat16),
            pltpu.VMEM((narr, nx, rows, cols), jnp.float32),
            pltpu.VMEM((narr, nx - 1, rows, cols), jnp.bfloat16),
            pltpu.VMEM((narr, nx - 1, rows, cols), jnp.bfloat16),
            pltpu.SemaphoreType.DMA((narr, nx)),
            pltpu.SemaphoreType.DMA((narr, nx)),
            pltpu.SemaphoreType.DMA((narr, nx - 1)),
            pltpu.SemaphoreType.DMA((narr, nx - 1)),
        ],
        compiler_params=pltpu.CompilerParams(collective_id=cid, has_side_effects=True,
                                             vmem_limit_bytes=64 * 1024 * 1024),
    )(*parts)


def _ag_kernel(nx, narr, *refs):
    chunks = refs[:narr]
    weights = refs[narr:2 * narr]
    outs = refs[2 * narr:3 * narr]
    prods = refs[3 * narr:3 * narr + 1]
    sr, rr, sc, rc = refs[3 * narr + 1:]
    row = lax.axis_index("row")
    x, k, d, nxt, prv = _col_ids(nx)
    _greet(row, k, x, nxt, prv)
    me = 2 * x + k
    partner = (row, 2 * x + 1 - k)
    nextdev = (row, 2 * nxt + k)

    width = weights[0].shape[1]

    def product(a, slot):
        prods[0][slot, :, a * width:(a + 1) * width] = jnp.dot(
            outs[a][slot], weights[a][...], preferred_element_type=jnp.float32
        ).astype(prods[0].dtype)

    for a in range(narr):
        outs[a][me] = chunks[a][...]
    ring, core = [], []
    for step in range(nx):
        for a in range(narr):
            src_x = lax.rem(x + 4 * nx - d * step, nx)
            slot = 2 * src_x + k
            if step > 0:
                ring[(step - 1) * narr + a].wait_recv()
            src = chunks[a] if step == 0 else outs[a].at[slot]
            if step < nx - 1:
                cp = pltpu.make_async_remote_copy(
                    src_ref=src, dst_ref=outs[a].at[slot],
                    send_sem=sr.at[a, step], recv_sem=rr.at[a, step],
                    device_id=nextdev, device_id_type=MESH)
                cp.start()
                ring.append(cp)
            cc = pltpu.make_async_remote_copy(
                src_ref=src, dst_ref=outs[a].at[slot],
                send_sem=sc.at[a, step], recv_sem=rc.at[a, step],
                device_id=partner, device_id_type=MESH)
            cc.start()
            core.append(cc)
        for a in range(narr):
            product(a, 2 * lax.rem(x + 4 * nx - d * step, nx) + k)
    for cp in ring:
        cp.wait_send()
    for step in range(nx):
        for a in range(narr):
            core[step * narr + a].wait()
        for a in range(narr):
            product(a, 2 * lax.rem(x + 4 * nx + d * step, nx) + 1 - k)


def col_all_gather(arrays, weights, cid):
    n = lax.axis_size("col")
    nx = n // 2
    narr = len(arrays)
    rows, cols = arrays[0].shape
    width = weights[0].shape[1]
    res = pl.pallas_call(
        functools.partial(_ag_kernel, nx, narr),
        out_shape=[jax.ShapeDtypeStruct((n, rows, cols), arrays[0].dtype)] * narr
        + [jax.ShapeDtypeStruct((n, rows, narr * width), jnp.bfloat16)],
        in_specs=[pl.BlockSpec(memory_space=pltpu.VMEM)] * (2 * narr),
        out_specs=[pl.BlockSpec(memory_space=pltpu.VMEM)] * (narr + 1),
        scratch_shapes=[
            pltpu.SemaphoreType.DMA((narr, nx)),
            pltpu.SemaphoreType.DMA((narr, nx)),
            pltpu.SemaphoreType.DMA((narr, nx)),
            pltpu.SemaphoreType.DMA((narr, nx)),
        ],
        compiler_params=pltpu.CompilerParams(collective_id=cid, has_side_effects=True,
                                             vmem_limit_bytes=64 * 1024 * 1024),
    )(*arrays, *weights)
    gathered = [o.reshape(n * rows, cols) for o in res[:narr]]
    return gathered, res[narr].reshape(n * rows, narr * width)


def gelu_grad(value):
    cdf = 0.5 * (1.0 + jax.scipy.special.erf(value * 0.7071067811865476))
    pdf = jnp.exp(-0.5 * value * value) * 0.3989422804014327
    return cdf + value * pdf


def token_panel(local_rows):
    return lax.all_gather(local_rows, "row", axis=0, tiled=True)


def token_panel_a2a(local_rows):
    n = lax.axis_size("row")
    copies = jnp.broadcast_to(local_rows[None], (n,) + local_rows.shape)
    copies = copies.reshape(n * local_rows.shape[0], local_rows.shape[1])
    return lax.all_to_all(copies, "row", split_axis=0, concat_axis=0, tiled=True)


def hidden_panel(local_rows):
    return lax.all_gather(local_rows, "col", axis=0, tiled=True)


def contract_last(left, right):
    return lax.dot_general(
        left, right, (((1,), (1,)), ((), ())), preferred_element_type=jnp.float32
    )


def width_split(left_all, right, transposed):
    if transposed:
        term = contract_last(left_all, right)
    else:
        term = jnp.dot(left_all, right, preferred_element_type=jnp.float32)
    return lax.psum_scatter(
        term.astype(jnp.bfloat16), "col", scatter_dimension=0, tiled=True
    ).astype(jnp.float32)


def unit_sum(left_all, right, transposed):
    n = lax.axis_size("row")
    if transposed:
        term = contract_last(left_all, right)
    else:
        term = jnp.dot(left_all, right, preferred_element_type=jnp.float32)
    pieces = term.astype(jnp.bfloat16).reshape(n, term.shape[0] // n, term.shape[1])
    pieces = lax.all_to_all(pieces, "row", split_axis=0, concat_axis=0, tiled=True)
    return jnp.sum(pieces.astype(jnp.float32), axis=0)


def row_sum(term):
    n = lax.axis_size("row")
    pieces = term.reshape(n, term.shape[0] // n, term.shape[1])
    pieces = lax.all_to_all(pieces, "row", split_axis=0, concat_axis=0, tiled=True)
    return jnp.sum(pieces.astype(jnp.float32), axis=0)


def local(tokens, w_in, w_out, cotangent):
    tokens_all = token_panel(tokens)
    upstream_all = token_panel_a2a(cotangent)
    pre_term = jnp.dot(tokens_all, w_in, preferred_element_type=jnp.float32).astype(jnp.bfloat16)
    dact_term = contract_last(upstream_all, w_out).astype(jnp.bfloat16)
    pre_part, dact_part = col_reduce_scatter([pre_term, dact_term], 1)
    act = jax.nn.gelu(pre_part, approximate=False).astype(jnp.bfloat16)
    dpre = (dact_part * gelu_grad(pre_part)).astype(jnp.bfloat16)
    (act_all, dpre_all), both_terms = col_all_gather([act, dpre], [w_out, w_in.T], 2)
    both_sums = row_sum(both_terms)
    mixed = both_sums[:, :tokens.shape[1]]
    block_rows = (tokens.astype(jnp.float32) + mixed).astype(jnp.bfloat16)
    block_out = lax.all_to_all(block_rows, "col", split_axis=0, concat_axis=1, tiled=True)
    grad_out = lax.dot_general(
        act_all, upstream_all, (((0,), (0,)), ((), ())), preferred_element_type=jnp.float32
    )
    grad_in = lax.dot_general(
        tokens_all, dpre_all, (((0,), (0,)), ((), ())), preferred_element_type=jnp.float32
    )
    back = both_sums[:, tokens.shape[1]:]
    grad_tokens = (cotangent.astype(jnp.float32) + back).astype(jnp.bfloat16)
    return (block_out, grad_tokens, grad_in, grad_out)


def solution(mesh):
    in_specs = (P("row", "col"), P("col", "row"), P("row", "col"), P("row", "col"))
    out_specs = (P(("row", "col"), None), P("row", "col"), P("col", "row"), P("row", "col"))
    return jax.shard_map(local, mesh=mesh, in_specs=in_specs, out_specs=out_specs, check_vma=False)
```

```python
import jax
import jax.numpy as jnp
from jax import lax
from jax.sharding import PartitionSpec as P
import functools
from jax.experimental import pallas as pl
from jax.experimental.pallas import tpu as pltpu

MESH = pl.DeviceIdType.MESH


def _col_ids(nx):
    me = lax.axis_index("col")
    x = me // 2
    k = me % 2
    d = 1 - 2 * k
    nxt = lax.rem(x + nx + d, nx)
    prv = lax.rem(x + nx - d, nx)
    return x, k, d, nxt, prv


def _greet(row, k, x, nxt, prv):
    barrier = pltpu.get_barrier_semaphore()
    for peer in (2 * x + 1 - k, 2 * nxt + k, 2 * prv + k):
        pl.semaphore_signal(barrier, inc=1, device_id=(row, peer), device_id_type=MESH)
    pl.semaphore_wait(barrier, 3)


def _rs_kernel(nx, narr, *refs):
    parts = refs[:narr]
    outs = refs[narr:2 * narr]
    recv1, vsum, sendbuf, recv2, s1, r1, s2, r2 = refs[2 * narr:]
    row = lax.axis_index("row")
    x, k, d, nxt, prv = _col_ids(nx)
    _greet(row, k, x, nxt, prv)
    partner = (row, 2 * x + 1 - k)
    nextdev = (row, 2 * nxt + k)
    first = []
    for a in range(narr):
        for i in range(nx):
            cp = pltpu.make_async_remote_copy(
                src_ref=parts[a].at[2 * i + 1 - k], dst_ref=recv1.at[a, i],
                send_sem=s1.at[a, i], recv_sem=r1.at[a, i],
                device_id=partner, device_id_type=MESH)
            cp.start()
            first.append(cp)
    for cp in first:
        cp.wait()
    for a in range(narr):
        for i in range(nx):
            vsum[a, i] = parts[a][2 * i + k].astype(jnp.float32) + recv1[a, i].astype(jnp.float32)
    ring = []
    for step in range(nx - 1):
        for a in range(narr):
            src_idx = lax.rem(x + 4 * nx - d * (step + 1), nx)
            if step == 0:
                sendbuf[a, step] = vsum[a, src_idx].astype(sendbuf.dtype)
            else:
                prevcp = ring[(step - 1) * narr + a]
                prevcp.wait_recv()
                sendbuf[a, step] = (recv2[a, step - 1].astype(jnp.float32) + vsum[a, src_idx]).astype(sendbuf.dtype)
            cp = pltpu.make_async_remote_copy(
                src_ref=sendbuf.at[a, step], dst_ref=recv2.at[a, step],
                send_sem=s2.at[a, step], recv_sem=r2.at[a, step],
                device_id=nextdev, device_id_type=MESH)
            cp.start()
            ring.append(cp)
    for a in range(narr):
        last = ring[(nx - 2) * narr + a]
        last.wait_recv()
        outs[a][...] = recv2[a, nx - 2].astype(jnp.float32) + vsum[a, x]
    for cp in ring:
        cp.wait_send()


def col_reduce_scatter(arrays, cid):
    n = lax.axis_size("col")
    nx = n // 2
    narr = len(arrays)
    rows = arrays[0].shape[0] // n
    cols = arrays[0].shape[1]
    parts = [a.reshape(n, rows, cols) for a in arrays]
    return pl.pallas_call(
        functools.partial(_rs_kernel, nx, narr),
        out_shape=[jax.ShapeDtypeStruct((rows, cols), jnp.float32)] * narr,
        in_specs=[pl.BlockSpec(memory_space=pltpu.VMEM)] * narr,
        out_specs=[pl.BlockSpec(memory_space=pltpu.VMEM)] * narr,
        scratch_shapes=[
            pltpu.VMEM((narr, nx, rows, cols), jnp.bfloat16),
            pltpu.VMEM((narr, nx, rows, cols), jnp.float32),
            pltpu.VMEM((narr, nx - 1, rows, cols), jnp.bfloat16),
            pltpu.VMEM((narr, nx - 1, rows, cols), jnp.bfloat16),
            pltpu.SemaphoreType.DMA((narr, nx)),
            pltpu.SemaphoreType.DMA((narr, nx)),
            pltpu.SemaphoreType.DMA((narr, nx - 1)),
            pltpu.SemaphoreType.DMA((narr, nx - 1)),
        ],
        compiler_params=pltpu.CompilerParams(collective_id=cid, has_side_effects=True,
                                             vmem_limit_bytes=64 * 1024 * 1024),
    )(*parts)


def _ag_kernel(nx, narr, *refs):
    chunks = refs[:narr]
    weights = refs[narr:2 * narr]
    outs = refs[2 * narr:3 * narr]
    prods = refs[3 * narr:4 * narr]
    sr, rr, sc, rc = refs[4 * narr:]
    row = lax.axis_index("row")
    x, k, d, nxt, prv = _col_ids(nx)
    _greet(row, k, x, nxt, prv)
    me = 2 * x + k
    partner = (row, 2 * x + 1 - k)
    nextdev = (row, 2 * nxt + k)

    def product(a, slot):
        prods[a][slot] = jnp.dot(outs[a][slot], weights[a][...],
                                 preferred_element_type=jnp.float32).astype(prods[a].dtype)

    for a in range(narr):
        outs[a][me] = chunks[a][...]
    ring, core = [], []
    for step in range(nx):
        for a in range(narr):
            src_x = lax.rem(x + 4 * nx - d * step, nx)
            slot = 2 * src_x + k
            if step > 0:
                ring[(step - 1) * narr + a].wait_recv()
            src = chunks[a] if step == 0 else outs[a].at[slot]
            if step < nx - 1:
                cp = pltpu.make_async_remote_copy(
                    src_ref=src, dst_ref=outs[a].at[slot],
                    send_sem=sr.at[a, step], recv_sem=rr.at[a, step],
                    device_id=nextdev, device_id_type=MESH)
                cp.start()
                ring.append(cp)
            cc = pltpu.make_async_remote_copy(
                src_ref=src, dst_ref=outs[a].at[slot],
                send_sem=sc.at[a, step], recv_sem=rc.at[a, step],
                device_id=partner, device_id_type=MESH)
            cc.start()
            core.append(cc)
        for a in range(narr):
            product(a, 2 * lax.rem(x + 4 * nx - d * step, nx) + k)
    for cp in ring:
        cp.wait_send()
    for step in range(nx):
        for a in range(narr):
            core[step * narr + a].wait()
        for a in range(narr):
            product(a, 2 * lax.rem(x + 4 * nx + d * step, nx) + 1 - k)


def col_all_gather(arrays, weights, cid):
    n = lax.axis_size("col")
    nx = n // 2
    narr = len(arrays)
    rows, cols = arrays[0].shape
    width = weights[0].shape[1]
    res = pl.pallas_call(
        functools.partial(_ag_kernel, nx, narr),
        out_shape=[jax.ShapeDtypeStruct((n, rows, cols), arrays[0].dtype)] * narr
        + [jax.ShapeDtypeStruct((n, rows, width), jnp.bfloat16)] * narr,
        in_specs=[pl.BlockSpec(memory_space=pltpu.VMEM)] * (2 * narr),
        out_specs=[pl.BlockSpec(memory_space=pltpu.VMEM)] * (2 * narr),
        scratch_shapes=[
            pltpu.SemaphoreType.DMA((narr, nx)),
            pltpu.SemaphoreType.DMA((narr, nx)),
            pltpu.SemaphoreType.DMA((narr, nx)),
            pltpu.SemaphoreType.DMA((narr, nx)),
        ],
        compiler_params=pltpu.CompilerParams(collective_id=cid, has_side_effects=True,
                                             vmem_limit_bytes=64 * 1024 * 1024),
    )(*arrays, *weights)
    gathered = [o.reshape(n * rows, cols) for o in res[:narr]]
    products = [o.reshape(n * rows, width) for o in res[narr:]]
    return gathered, products


def _row_ids():
    me = lax.axis_index("row")
    y = me // 4
    z = me % 4
    k = lax.axis_index("col") % 2
    d = 1 - 2 * k
    return y, z, d


def _row_ag_kernel(ny, *refs):
    ins = refs[:2]
    outs = refs[2:4]
    sa, sb, rsem = refs[4:]
    col = lax.axis_index("col")
    y, z, d = _row_ids()
    me = y * 4 + z
    barrier = pltpu.get_barrier_semaphore()
    peers = (y * 4 + lax.rem(z + 4 + d, 4), y * 4 + lax.rem(z + 4 - d, 4),
             lax.rem(y + ny + d, ny) * 4 + z, lax.rem(y + ny - d, ny) * 4 + z)
    for p in peers:
        pl.semaphore_signal(barrier, inc=1, device_id=(p, col), device_id_type=MESH)
    pl.semaphore_wait(barrier, 4)
    geo = []
    for a in range(2):
        if a == 0:
            na, nb = 4, ny
            pos_a, pos_b = z, y
            slot_of = lambda pa, pb: pb * 4 + pa
        else:
            na, nb = ny, 4
            pos_a, pos_b = y, z
            slot_of = lambda pa, pb: pa * 4 + pb
        geo.append((na, nb, pos_a, pos_b, slot_of))
        outs[a][me] = ins[a][...]

    def dev(a, pa, pb):
        return (geo[a][4](pa, pb), col)

    def send(a, src, slot, target, sem):
        cp = pltpu.make_async_remote_copy(
            src_ref=src, dst_ref=outs[a].at[slot], send_sem=sem, recv_sem=rsem.at[a, slot],
            device_id=target, device_id_type=MESH)
        cp.start()
        return cp

    def wait_in(a, slot):
        pltpu.make_async_remote_copy(
            src_ref=ins[a], dst_ref=outs[a].at[slot], send_sem=sa.at[a, 0], recv_sem=rsem.at[a, slot],
            device_id=(peers[0], col), device_id_type=MESH).wait_recv()

    sends = []
    for a in range(2):
        na, nb, pa, pb, slot_of = geo[a]
        next_a = dev(a, lax.rem(pa + na + d, na), pb)
        next_b = dev(a, pa, lax.rem(pb + nb + d, nb))
        sends.append(send(a, ins[a], me, next_a, sa.at[a, 0]))
        sends.append(send(a, ins[a], me, next_b, sb.at[a, 0, 0]))
    for s in range(1, 4):
        for a in range(2):
            na, nb, pa, pb, slot_of = geo[a]
            next_a = dev(a, lax.rem(pa + na + d, na), pb)
            next_b = dev(a, pa, lax.rem(pb + nb + d, nb))
            slot = slot_of(lax.rem(pa + 4 * na - d * s, na), pb)
            wait_in(a, slot)
            if s < na - 1:
                sends.append(send(a, outs[a].at[slot], slot, next_a, sa.at[a, s]))
            sends.append(send(a, outs[a].at[slot], slot, next_b, sb.at[a, 0, s]))
    for t in range(1, 4):
        for j in range(4):
            for a in range(2):
                na, nb, pa, pb, slot_of = geo[a]
                next_b = dev(a, pa, lax.rem(pb + nb + d, nb))
                slot = slot_of(lax.rem(pa + 4 * na - d * j, na), lax.rem(pb + 4 * nb - d * t, nb))
                wait_in(a, slot)
                if t < nb - 1:
                    sends.append(send(a, outs[a].at[slot], slot, next_b, sb.at[a, t, j]))
    for cp in sends:
        cp.wait_send()


def row_all_gather(first, second, cid):
    n = lax.axis_size("row")
    ny = n // 4
    rows, cols = first.shape
    outs = pl.pallas_call(
        functools.partial(_row_ag_kernel, ny),
        out_shape=[jax.ShapeDtypeStruct((n, rows, cols), first.dtype)] * 2,
        in_specs=[pl.BlockSpec(memory_space=pltpu.VMEM)] * 2,
        out_specs=[pl.BlockSpec(memory_space=pltpu.VMEM)] * 2,
        scratch_shapes=[
            pltpu.SemaphoreType.DMA((2, 4)),
            pltpu.SemaphoreType.DMA((2, 4, 4)),
            pltpu.SemaphoreType.DMA((2, n)),
        ],
        compiler_params=pltpu.CompilerParams(collective_id=cid, has_side_effects=True,
                                             vmem_limit_bytes=64 * 1024 * 1024),
    )(first, second)
    return [o.reshape(n * rows, cols) for o in outs]


def gelu_grad(value):
    cdf = 0.5 * (1.0 + jax.scipy.special.erf(value * 0.7071067811865476))
    pdf = jnp.exp(-0.5 * value * value) * 0.3989422804014327
    return cdf + value * pdf


def token_panel(local_rows):
    return lax.all_gather(local_rows, "row", axis=0, tiled=True)


def token_panel_a2a(local_rows):
    n = lax.axis_size("row")
    copies = jnp.broadcast_to(local_rows[None], (n,) + local_rows.shape)
    copies = copies.reshape(n * local_rows.shape[0], local_rows.shape[1])
    return lax.all_to_all(copies, "row", split_axis=0, concat_axis=0, tiled=True)


def hidden_panel(local_rows):
    return lax.all_gather(local_rows, "col", axis=0, tiled=True)


def contract_last(left, right):
    return lax.dot_general(
        left, right, (((1,), (1,)), ((), ())), preferred_element_type=jnp.float32
    )


def width_split(left_all, right, transposed):
    if transposed:
        term = contract_last(left_all, right)
    else:
        term = jnp.dot(left_all, right, preferred_element_type=jnp.float32)
    return lax.psum_scatter(
        term.astype(jnp.bfloat16), "col", scatter_dimension=0, tiled=True
    ).astype(jnp.float32)


def unit_sum(left_all, right, transposed):
    n = lax.axis_size("row")
    if transposed:
        term = contract_last(left_all, right)
    else:
        term = jnp.dot(left_all, right, preferred_element_type=jnp.float32)
    pieces = term.astype(jnp.bfloat16).reshape(n, term.shape[0] // n, term.shape[1])
    pieces = lax.all_to_all(pieces, "row", split_axis=0, concat_axis=0, tiled=True)
    return jnp.sum(pieces.astype(jnp.float32), axis=0)


def row_sum(term):
    n = lax.axis_size("row")
    pieces = term.reshape(n, term.shape[0] // n, term.shape[1])
    pieces = lax.all_to_all(pieces, "row", split_axis=0, concat_axis=0, tiled=True)
    return jnp.sum(pieces.astype(jnp.float32), axis=0)


def local(tokens, w_in, w_out, cotangent):
    tokens_all, upstream_all = row_all_gather(tokens, cotangent, 3)
    pre_term = jnp.dot(tokens_all, w_in, preferred_element_type=jnp.float32).astype(jnp.bfloat16)
    dact_term = contract_last(upstream_all, w_out).astype(jnp.bfloat16)
    pre_part, dact_part = col_reduce_scatter([pre_term, dact_term], 1)
    act = jax.nn.gelu(pre_part, approximate=False).astype(jnp.bfloat16)
    dpre = (dact_part * gelu_grad(pre_part)).astype(jnp.bfloat16)
    (act_all, dpre_all), (mixed_term, back_term) = col_all_gather([act, dpre], [w_out, w_in.T], 2)
    mixed = row_sum(mixed_term)
    block_rows = (tokens.astype(jnp.float32) + mixed).astype(jnp.bfloat16)
    block_out = lax.all_to_all(block_rows, "col", split_axis=0, concat_axis=1, tiled=True)
    grad_out = lax.dot_general(
        act_all, upstream_all, (((0,), (0,)), ((), ())), preferred_element_type=jnp.float32
    )
    grad_in = lax.dot_general(
        tokens_all, dpre_all, (((0,), (0,)), ((), ())), preferred_element_type=jnp.float32
    )
    back = row_sum(back_term)
    grad_tokens = (cotangent.astype(jnp.float32) + back).astype(jnp.bfloat16)
    return (block_out, grad_tokens, grad_in, grad_out)


def solution(mesh):
    in_specs = (P("row", "col"), P("col", "row"), P("row", "col"), P("row", "col"))
    out_specs = (P(("row", "col"), None), P("row", "col"), P("col", "row"), P("row", "col"))
    return jax.shard_map(local, mesh=mesh, in_specs=in_specs, out_specs=out_specs, check_vma=False)
```

```python
import jax
import jax.numpy as jnp
from jax import lax
from jax.sharding import PartitionSpec as P
import functools
from jax.experimental import pallas as pl
from jax.experimental.pallas import tpu as pltpu

MESH = pl.DeviceIdType.MESH


def _col_ids(nx):
    me = lax.axis_index("col")
    x = me // 2
    k = me % 2
    d = 1 - 2 * k
    nxt = lax.rem(x + nx + d, nx)
    prv = lax.rem(x + nx - d, nx)
    return x, k, d, nxt, prv


def _greet(row, k, x, nxt, prv):
    barrier = pltpu.get_barrier_semaphore()
    for peer in (2 * x + 1 - k, 2 * nxt + k, 2 * prv + k):
        pl.semaphore_signal(barrier, inc=1, device_id=(row, peer), device_id_type=MESH)
    pl.semaphore_wait(barrier, 3)


def _rs_kernel(nx, narr, *refs):
    parts = refs[:narr]
    outs = refs[narr:2 * narr]
    recv1, vsum, sendbuf, recv2, s1, r1, s2, r2 = refs[2 * narr:]
    row = lax.axis_index("row")
    x, k, d, nxt, prv = _col_ids(nx)
    _greet(row, k, x, nxt, prv)
    partner = (row, 2 * x + 1 - k)
    nextdev = (row, 2 * nxt + k)
    first = []
    for a in range(narr):
        for i in range(nx):
            cp = pltpu.make_async_remote_copy(
                src_ref=parts[a].at[2 * i + 1 - k], dst_ref=recv1.at[a, i],
                send_sem=s1.at[a, i], recv_sem=r1.at[a, i],
                device_id=partner, device_id_type=MESH)
            cp.start()
            first.append(cp)
    for cp in first:
        cp.wait()
    for a in range(narr):
        for i in range(nx):
            vsum[a, i] = parts[a][2 * i + k].astype(jnp.float32) + recv1[a, i].astype(jnp.float32)
    ring = []
    for step in range(nx - 1):
        for a in range(narr):
            src_idx = lax.rem(x + 4 * nx - d * (step + 1), nx)
            if step == 0:
                sendbuf[a, step] = vsum[a, src_idx].astype(sendbuf.dtype)
            else:
                prevcp = ring[(step - 1) * narr + a]
                prevcp.wait_recv()
                sendbuf[a, step] = (recv2[a, step - 1].astype(jnp.float32) + vsum[a, src_idx]).astype(sendbuf.dtype)
            cp = pltpu.make_async_remote_copy(
                src_ref=sendbuf.at[a, step], dst_ref=recv2.at[a, step],
                send_sem=s2.at[a, step], recv_sem=r2.at[a, step],
                device_id=nextdev, device_id_type=MESH)
            cp.start()
            ring.append(cp)
    for a in range(narr):
        last = ring[(nx - 2) * narr + a]
        last.wait_recv()
        outs[a][...] = recv2[a, nx - 2].astype(jnp.float32) + vsum[a, x]
    for cp in ring:
        cp.wait_send()


def col_reduce_scatter(arrays, cid):
    n = lax.axis_size("col")
    nx = n // 2
    narr = len(arrays)
    rows = arrays[0].shape[0] // n
    cols = arrays[0].shape[1]
    parts = [a.reshape(n, rows, cols) for a in arrays]
    return pl.pallas_call(
        functools.partial(_rs_kernel, nx, narr),
        out_shape=[jax.ShapeDtypeStruct((rows, cols), jnp.float32)] * narr,
        in_specs=[pl.BlockSpec(memory_space=pltpu.VMEM)] * narr,
        out_specs=[pl.BlockSpec(memory_space=pltpu.VMEM)] * narr,
        scratch_shapes=[
            pltpu.VMEM((narr, nx, rows, cols), jnp.bfloat16),
            pltpu.VMEM((narr, nx, rows, cols), jnp.float32),
            pltpu.VMEM((narr, nx - 1, rows, cols), jnp.bfloat16),
            pltpu.VMEM((narr, nx - 1, rows, cols), jnp.bfloat16),
            pltpu.SemaphoreType.DMA((narr, nx)),
            pltpu.SemaphoreType.DMA((narr, nx)),
            pltpu.SemaphoreType.DMA((narr, nx - 1)),
            pltpu.SemaphoreType.DMA((narr, nx - 1)),
        ],
        compiler_params=pltpu.CompilerParams(collective_id=cid, has_side_effects=True,
                                             vmem_limit_bytes=64 * 1024 * 1024),
    )(*parts)


def _ag_kernel(nx, narr, *refs):
    chunks = refs[:narr]
    weights = refs[narr:2 * narr]
    outs = refs[2 * narr:3 * narr]
    prods = refs[3 * narr:4 * narr]
    sr, rr, sc, rc = refs[4 * narr:]
    row = lax.axis_index("row")
    x, k, d, nxt, prv = _col_ids(nx)
    _greet(row, k, x, nxt, prv)
    me = 2 * x + k
    partner = (row, 2 * x + 1 - k)
    nextdev = (row, 2 * nxt + k)

    def product(a, slot):
        prods[a][slot] = jnp.dot(outs[a][slot], weights[a][...],
                                 preferred_element_type=jnp.float32).astype(prods[a].dtype)

    for a in range(narr):
        outs[a][me] = chunks[a][...]
    ring, core = [], []
    for step in range(nx):
        for a in range(narr):
            src_x = lax.rem(x + 4 * nx - d * step, nx)
            slot = 2 * src_x + k
            if step > 0:
                ring[(step - 1) * narr + a].wait_recv()
            src = chunks[a] if step == 0 else outs[a].at[slot]
            if step < nx - 1:
                cp = pltpu.make_async_remote_copy(
                    src_ref=src, dst_ref=outs[a].at[slot],
                    send_sem=sr.at[a, step], recv_sem=rr.at[a, step],
                    device_id=nextdev, device_id_type=MESH)
                cp.start()
                ring.append(cp)
            cc = pltpu.make_async_remote_copy(
                src_ref=src, dst_ref=outs[a].at[slot],
                send_sem=sc.at[a, step], recv_sem=rc.at[a, step],
                device_id=partner, device_id_type=MESH)
            cc.start()
            core.append(cc)
        for a in range(narr):
            product(a, 2 * lax.rem(x + 4 * nx - d * step, nx) + k)
    for cp in ring:
        cp.wait_send()
    for step in range(nx):
        for a in range(narr):
            core[step * narr + a].wait()
        for a in range(narr):
            product(a, 2 * lax.rem(x + 4 * nx + d * step, nx) + 1 - k)


def col_all_gather(arrays, weights, cid):
    n = lax.axis_size("col")
    nx = n // 2
    narr = len(arrays)
    rows, cols = arrays[0].shape
    width = weights[0].shape[1]
    res = pl.pallas_call(
        functools.partial(_ag_kernel, nx, narr),
        out_shape=[jax.ShapeDtypeStruct((n, rows, cols), arrays[0].dtype)] * narr
        + [jax.ShapeDtypeStruct((n, rows, width), jnp.bfloat16)] * narr,
        in_specs=[pl.BlockSpec(memory_space=pltpu.VMEM)] * (2 * narr),
        out_specs=[pl.BlockSpec(memory_space=pltpu.VMEM)] * (2 * narr),
        scratch_shapes=[
            pltpu.SemaphoreType.DMA((narr, nx)),
            pltpu.SemaphoreType.DMA((narr, nx)),
            pltpu.SemaphoreType.DMA((narr, nx)),
            pltpu.SemaphoreType.DMA((narr, nx)),
        ],
        compiler_params=pltpu.CompilerParams(collective_id=cid, has_side_effects=True,
                                             vmem_limit_bytes=64 * 1024 * 1024),
    )(*arrays, *weights)
    gathered = [o.reshape(n * rows, cols) for o in res[:narr]]
    products = [o.reshape(n * rows, width) for o in res[narr:]]
    return gathered, products


def _row_ids():
    me = lax.axis_index("row")
    y = me // 4
    z = me % 4
    k = lax.axis_index("col") % 2
    d = 1 - 2 * k
    return y, z, d


def _row_ag_kernel(ny, *refs):
    ins = refs[:2]
    outs = refs[2:4]
    sa, sb, rsem = refs[4:]
    col = lax.axis_index("col")
    y, z, d = _row_ids()
    me = y * 4 + z
    barrier = pltpu.get_barrier_semaphore()
    peers = (y * 4 + lax.rem(z + 4 + d, 4), y * 4 + lax.rem(z + 4 - d, 4),
             lax.rem(y + ny + d, ny) * 4 + z, lax.rem(y + ny - d, ny) * 4 + z)
    for p in peers:
        pl.semaphore_signal(barrier, inc=1, device_id=(p, col), device_id_type=MESH)
    pl.semaphore_wait(barrier, 4)
    geo = []
    for a in range(2):
        if a == 0:
            na, nb = 4, ny
            pos_a, pos_b = z, y
            slot_of = lambda pa, pb: pb * 4 + pa
        else:
            na, nb = ny, 4
            pos_a, pos_b = y, z
            slot_of = lambda pa, pb: pa * 4 + pb
        geo.append((na, nb, pos_a, pos_b, slot_of))
        outs[a][me] = ins[a][...]

    def dev(a, pa, pb):
        return (geo[a][4](pa, pb), col)

    def send(a, src, slot, target, sem):
        cp = pltpu.make_async_remote_copy(
            src_ref=src, dst_ref=outs[a].at[slot], send_sem=sem, recv_sem=rsem.at[a, slot],
            device_id=target, device_id_type=MESH)
        cp.start()
        return cp

    def wait_in(a, slot):
        pltpu.make_async_remote_copy(
            src_ref=ins[a], dst_ref=outs[a].at[slot], send_sem=sa.at[a, 0], recv_sem=rsem.at[a, slot],
            device_id=(peers[0], col), device_id_type=MESH).wait_recv()

    sends = []
    for a in range(2):
        na, nb, pa, pb, slot_of = geo[a]
        next_a = dev(a, lax.rem(pa + na + d, na), pb)
        next_b = dev(a, pa, lax.rem(pb + nb + d, nb))
        sends.append(send(a, ins[a], me, next_a, sa.at[a, 0]))
        sends.append(send(a, ins[a], me, next_b, sb.at[a, 0, 0]))
    for s in range(1, 4):
        for a in range(2):
            na, nb, pa, pb, slot_of = geo[a]
            next_a = dev(a, lax.rem(pa + na + d, na), pb)
            next_b = dev(a, pa, lax.rem(pb + nb + d, nb))
            slot = slot_of(lax.rem(pa + 4 * na - d * s, na), pb)
            wait_in(a, slot)
            if s < na - 1:
                sends.append(send(a, outs[a].at[slot], slot, next_a, sa.at[a, s]))
            sends.append(send(a, outs[a].at[slot], slot, next_b, sb.at[a, 0, s]))
    for t in range(1, 4):
        for j in range(4):
            for a in range(2):
                na, nb, pa, pb, slot_of = geo[a]
                next_b = dev(a, pa, lax.rem(pb + nb + d, nb))
                slot = slot_of(lax.rem(pa + 4 * na - d * j, na), lax.rem(pb + 4 * nb - d * t, nb))
                wait_in(a, slot)
                if t < nb - 1:
                    sends.append(send(a, outs[a].at[slot], slot, next_b, sb.at[a, t, j]))
    for cp in sends:
        cp.wait_send()


def row_all_gather(first, second, cid):
    n = lax.axis_size("row")
    ny = n // 4
    rows, cols = first.shape
    outs = pl.pallas_call(
        functools.partial(_row_ag_kernel, ny),
        out_shape=[jax.ShapeDtypeStruct((n, rows, cols), first.dtype)] * 2,
        in_specs=[pl.BlockSpec(memory_space=pltpu.VMEM)] * 2,
        out_specs=[pl.BlockSpec(memory_space=pltpu.VMEM)] * 2,
        scratch_shapes=[
            pltpu.SemaphoreType.DMA((2, 4)),
            pltpu.SemaphoreType.DMA((2, 4, 4)),
            pltpu.SemaphoreType.DMA((2, n)),
        ],
        compiler_params=pltpu.CompilerParams(collective_id=cid, has_side_effects=True,
                                             vmem_limit_bytes=64 * 1024 * 1024),
    )(first, second)
    return [o.reshape(n * rows, cols) for o in outs]


def _row_rs_kernel(ny, *refs):
    ins = refs[:2]
    outs = refs[2:4]
    sb1, rb1, ssum, sb2, rb2, s1, r1, s2, r2 = refs[4:]
    col = lax.axis_index("col")
    y, z, d = _row_ids()
    barrier = pltpu.get_barrier_semaphore()
    peers = (y * 4 + lax.rem(z + 4 + d, 4), y * 4 + lax.rem(z + 4 - d, 4),
             lax.rem(y + ny + d, ny) * 4 + z, lax.rem(y + ny - d, ny) * 4 + z)
    for p in peers:
        pl.semaphore_signal(barrier, inc=1, device_id=(p, col), device_id_type=MESH)
    pl.semaphore_wait(barrier, 4)
    geo = [(4, ny, z, y, lambda pa, pb: pb * 4 + pa), (ny, 4, y, z, lambda pa, pb: pa * 4 + pb)]

    def dev(a, pa, pb):
        return (geo[a][4](pa, pb), col)

    def send(src, dst, ssem, rsem, target):
        cp = pltpu.make_async_remote_copy(src_ref=src, dst_ref=dst, send_sem=ssem, recv_sem=rsem,
                                          device_id=target, device_id_type=MESH)
        cp.start()
        return cp

    sends = []
    first = [[] for _ in range(2)]
    for s in range(4 - 1):
        for a in range(2):
            na, nb, pa, pb, slot_of = geo[a]
            pos = lax.rem(pa + 4 * na - d * (s + 1), na)
            for bq in range(nb):
                own = ins[a][slot_of(pos, bq)]
                if s == 0:
                    sb1[a, s, bq] = own
                else:
                    sb1[a, s, bq] = (rb1[a, s - 1, bq].astype(jnp.float32) + own.astype(jnp.float32)).astype(sb1.dtype)
            cp = send(sb1.at[a, s], rb1.at[a, s], s1.at[a, s], r1.at[a, s],
                      dev(a, lax.rem(pa + na + d, na), pb))
            sends.append(cp)
            first[a].append(cp)
        for a in range(2):
            first[a][s].wait_recv()
    for a in range(2):
        na, nb, pa, pb, slot_of = geo[a]
        for bq in range(nb):
            ssum[a, bq] = rb1[a, 2, bq].astype(jnp.float32) + ins[a][slot_of(pa, bq)].astype(jnp.float32)
    second = [[] for _ in range(2)]
    for t in range(4 - 1):
        for a in range(2):
            na, nb, pa, pb, slot_of = geo[a]
            pos = lax.rem(pb + 4 * nb - d * (t + 1), nb)
            if t == 0:
                sb2[a, t] = ssum[a, pos].astype(sb2.dtype)
            else:
                sb2[a, t] = (rb2[a, t - 1].astype(jnp.float32) + ssum[a, pos]).astype(sb2.dtype)
            cp = send(sb2.at[a, t], rb2.at[a, t], s2.at[a, t], r2.at[a, t],
                      dev(a, pa, lax.rem(pb + nb + d, nb)))
            sends.append(cp)
            second[a].append(cp)
        for a in range(2):
            second[a][t].wait_recv()
    for a in range(2):
        na, nb, pa, pb, slot_of = geo[a]
        outs[a][...] = rb2[a, 2].astype(jnp.float32) + ssum[a, pb]
    for cp in sends:
        cp.wait_send()


def row_reduce_scatter(first, second, cid):
    n = lax.axis_size("row")
    ny = n // 4
    rows, cols = first.shape[0] // n, first.shape[1]
    ins = [v.reshape(n, rows, cols) for v in (first, second)]
    return pl.pallas_call(
        functools.partial(_row_rs_kernel, ny),
        out_shape=[jax.ShapeDtypeStruct((rows, cols), jnp.float32)] * 2,
        in_specs=[pl.BlockSpec(memory_space=pltpu.VMEM)] * 2,
        out_specs=[pl.BlockSpec(memory_space=pltpu.VMEM)] * 2,
        scratch_shapes=[
            pltpu.VMEM((2, 3, 4, rows, cols), jnp.bfloat16),
            pltpu.VMEM((2, 3, 4, rows, cols), jnp.bfloat16),
            pltpu.VMEM((2, 4, rows, cols), jnp.float32),
            pltpu.VMEM((2, 3, rows, cols), jnp.bfloat16),
            pltpu.VMEM((2, 3, rows, cols), jnp.bfloat16),
            pltpu.SemaphoreType.DMA((2, 3)),
            pltpu.SemaphoreType.DMA((2, 3)),
            pltpu.SemaphoreType.DMA((2, 3)),
            pltpu.SemaphoreType.DMA((2, 3)),
        ],
        compiler_params=pltpu.CompilerParams(collective_id=cid, has_side_effects=True,
                                             vmem_limit_bytes=64 * 1024 * 1024),
    )(*ins)


def gelu_grad(value):
    cdf = 0.5 * (1.0 + jax.scipy.special.erf(value * 0.7071067811865476))
    pdf = jnp.exp(-0.5 * value * value) * 0.3989422804014327
    return cdf + value * pdf


def token_panel(local_rows):
    return lax.all_gather(local_rows, "row", axis=0, tiled=True)


def token_panel_a2a(local_rows):
    n = lax.axis_size("row")
    copies = jnp.broadcast_to(local_rows[None], (n,) + local_rows.shape)
    copies = copies.reshape(n * local_rows.shape[0], local_rows.shape[1])
    return lax.all_to_all(copies, "row", split_axis=0, concat_axis=0, tiled=True)


def hidden_panel(local_rows):
    return lax.all_gather(local_rows, "col", axis=0, tiled=True)


def contract_last(left, right):
    return lax.dot_general(
        left, right, (((1,), (1,)), ((), ())), preferred_element_type=jnp.float32
    )


def width_split(left_all, right, transposed):
    if transposed:
        term = contract_last(left_all, right)
    else:
        term = jnp.dot(left_all, right, preferred_element_type=jnp.float32)
    return lax.psum_scatter(
        term.astype(jnp.bfloat16), "col", scatter_dimension=0, tiled=True
    ).astype(jnp.float32)


def unit_sum(left_all, right, transposed):
    n = lax.axis_size("row")
    if transposed:
        term = contract_last(left_all, right)
    else:
        term = jnp.dot(left_all, right, preferred_element_type=jnp.float32)
    pieces = term.astype(jnp.bfloat16).reshape(n, term.shape[0] // n, term.shape[1])
    pieces = lax.all_to_all(pieces, "row", split_axis=0, concat_axis=0, tiled=True)
    return jnp.sum(pieces.astype(jnp.float32), axis=0)


def row_sum(term):
    n = lax.axis_size("row")
    pieces = term.reshape(n, term.shape[0] // n, term.shape[1])
    pieces = lax.all_to_all(pieces, "row", split_axis=0, concat_axis=0, tiled=True)
    return jnp.sum(pieces.astype(jnp.float32), axis=0)


def local(tokens, w_in, w_out, cotangent):
    tokens_all, upstream_all = row_all_gather(tokens, cotangent, 3)
    pre_term = jnp.dot(tokens_all, w_in, preferred_element_type=jnp.float32).astype(jnp.bfloat16)
    dact_term = contract_last(upstream_all, w_out).astype(jnp.bfloat16)
    pre_part, dact_part = col_reduce_scatter([pre_term, dact_term], 1)
    act = jax.nn.gelu(pre_part, approximate=False).astype(jnp.bfloat16)
    dpre = (dact_part * gelu_grad(pre_part)).astype(jnp.bfloat16)
    (act_all, dpre_all), (mixed_term, back_term) = col_all_gather([act, dpre], [w_out, w_in.T], 2)
    mixed, back = row_reduce_scatter(mixed_term, back_term, 4)
    block_rows = (tokens.astype(jnp.float32) + mixed).astype(jnp.bfloat16)
    block_out = lax.all_to_all(block_rows, "col", split_axis=0, concat_axis=1, tiled=True)
    grad_out = lax.dot_general(
        act_all, upstream_all, (((0,), (0,)), ((), ())), preferred_element_type=jnp.float32
    )
    grad_in = lax.dot_general(
        tokens_all, dpre_all, (((0,), (0,)), ((), ())), preferred_element_type=jnp.float32
    )
    grad_tokens = (cotangent.astype(jnp.float32) + back).astype(jnp.bfloat16)
    return (block_out, grad_tokens, grad_in, grad_out)


def solution(mesh):
    in_specs = (P("row", "col"), P("col", "row"), P("row", "col"), P("row", "col"))
    out_specs = (P(("row", "col"), None), P("row", "col"), P("col", "row"), P("row", "col"))
    return jax.shard_map(local, mesh=mesh, in_specs=in_specs, out_specs=out_specs, check_vma=False)
```

```python
import jax
import jax.numpy as jnp
from jax import lax
from jax.sharding import PartitionSpec as P
import functools
from jax.experimental import pallas as pl
from jax.experimental.pallas import tpu as pltpu

MESH = pl.DeviceIdType.MESH


def _col_ids(nx):
    me = lax.axis_index("col")
    x = me // 2
    k = me % 2
    d = 1 - 2 * k
    nxt = lax.rem(x + nx + d, nx)
    prv = lax.rem(x + nx - d, nx)
    return x, k, d, nxt, prv


def _greet(row, k, x, nxt, prv):
    barrier = pltpu.get_barrier_semaphore()
    for peer in (2 * x + 1 - k, 2 * nxt + k, 2 * prv + k):
        pl.semaphore_signal(barrier, inc=1, device_id=(row, peer), device_id_type=MESH)
    pl.semaphore_wait(barrier, 3)


def _rs_kernel(nx, narr, *refs):
    parts = refs[:narr]
    outs = refs[narr:2 * narr]
    recv1, vsum, sendbuf, recv2, s1, r1, s2, r2 = refs[2 * narr:]
    row = lax.axis_index("row")
    x, k, d, nxt, prv = _col_ids(nx)
    _greet(row, k, x, nxt, prv)
    partner = (row, 2 * x + 1 - k)
    nextdev = (row, 2 * nxt + k)
    first = []
    for a in range(narr):
        for i in range(nx):
            cp = pltpu.make_async_remote_copy(
                src_ref=parts[a].at[2 * i + 1 - k], dst_ref=recv1.at[a, i],
                send_sem=s1.at[a, i], recv_sem=r1.at[a, i],
                device_id=partner, device_id_type=MESH)
            cp.start()
            first.append(cp)
    for cp in first:
        cp.wait()
    for a in range(narr):
        for i in range(nx):
            vsum[a, i] = parts[a][2 * i + k].astype(jnp.float32) + recv1[a, i].astype(jnp.float32)
    ring = []
    for step in range(nx - 1):
        for a in range(narr):
            src_idx = lax.rem(x + 4 * nx - d * (step + 1), nx)
            if step == 0:
                sendbuf[a, step] = vsum[a, src_idx].astype(sendbuf.dtype)
            else:
                prevcp = ring[(step - 1) * narr + a]
                prevcp.wait_recv()
                sendbuf[a, step] = (recv2[a, step - 1].astype(jnp.float32) + vsum[a, src_idx]).astype(sendbuf.dtype)
            cp = pltpu.make_async_remote_copy(
                src_ref=sendbuf.at[a, step], dst_ref=recv2.at[a, step],
                send_sem=s2.at[a, step], recv_sem=r2.at[a, step],
                device_id=nextdev, device_id_type=MESH)
            cp.start()
            ring.append(cp)
    for a in range(narr):
        last = ring[(nx - 2) * narr + a]
        last.wait_recv()
        outs[a][...] = recv2[a, nx - 2].astype(jnp.float32) + vsum[a, x]
    for cp in ring:
        cp.wait_send()


def col_reduce_scatter(arrays, cid):
    n = lax.axis_size("col")
    nx = n // 2
    narr = len(arrays)
    rows = arrays[0].shape[0] // n
    cols = arrays[0].shape[1]
    parts = [a.reshape(n, rows, cols) for a in arrays]
    return pl.pallas_call(
        functools.partial(_rs_kernel, nx, narr),
        out_shape=[jax.ShapeDtypeStruct((rows, cols), jnp.float32)] * narr,
        in_specs=[pl.BlockSpec(memory_space=pltpu.VMEM)] * narr,
        out_specs=[pl.BlockSpec(memory_space=pltpu.VMEM)] * narr,
        scratch_shapes=[
            pltpu.VMEM((narr, nx, rows, cols), jnp.bfloat16),
            pltpu.VMEM((narr, nx, rows, cols), jnp.float32),
            pltpu.VMEM((narr, nx - 1, rows, cols), jnp.bfloat16),
            pltpu.VMEM((narr, nx - 1, rows, cols), jnp.bfloat16),
            pltpu.SemaphoreType.DMA((narr, nx)),
            pltpu.SemaphoreType.DMA((narr, nx)),
            pltpu.SemaphoreType.DMA((narr, nx - 1)),
            pltpu.SemaphoreType.DMA((narr, nx - 1)),
        ],
        compiler_params=pltpu.CompilerParams(collective_id=cid, has_side_effects=True,
                                             vmem_limit_bytes=64 * 1024 * 1024),
    )(*parts)


def _ag_kernel(nx, narr, *refs):
    chunks = refs[:narr]
    weights = refs[narr:2 * narr]
    outs = refs[2 * narr:3 * narr]
    prods = refs[3 * narr:4 * narr]
    sr, rr, sc, rc = refs[4 * narr:]
    row = lax.axis_index("row")
    x, k, d, nxt, prv = _col_ids(nx)
    _greet(row, k, x, nxt, prv)
    me = 2 * x + k
    partner = (row, 2 * x + 1 - k)
    nextdev = (row, 2 * nxt + k)

    def product(a, slot):
        prods[a][slot] = jnp.dot(outs[a][slot], weights[a][...],
                                 preferred_element_type=jnp.float32).astype(prods[a].dtype)

    for a in range(narr):
        outs[a][me] = chunks[a][...]
    ring, core = [], []
    for step in range(nx):
        for a in range(narr):
            src_x = lax.rem(x + 4 * nx - d * step, nx)
            slot = 2 * src_x + k
            if step > 0:
                ring[(step - 1) * narr + a].wait_recv()
            src = chunks[a] if step == 0 else outs[a].at[slot]
            if step < nx - 1:
                cp = pltpu.make_async_remote_copy(
                    src_ref=src, dst_ref=outs[a].at[slot],
                    send_sem=sr.at[a, step], recv_sem=rr.at[a, step],
                    device_id=nextdev, device_id_type=MESH)
                cp.start()
                ring.append(cp)
            cc = pltpu.make_async_remote_copy(
                src_ref=src, dst_ref=outs[a].at[slot],
                send_sem=sc.at[a, step], recv_sem=rc.at[a, step],
                device_id=partner, device_id_type=MESH)
            cc.start()
            core.append(cc)
        for a in range(narr):
            product(a, 2 * lax.rem(x + 4 * nx - d * step, nx) + k)
    for cp in ring:
        cp.wait_send()
    for step in range(nx):
        for a in range(narr):
            core[step * narr + a].wait()
        for a in range(narr):
            product(a, 2 * lax.rem(x + 4 * nx + d * step, nx) + 1 - k)


def col_all_gather(arrays, weights, cid):
    n = lax.axis_size("col")
    nx = n // 2
    narr = len(arrays)
    rows, cols = arrays[0].shape
    width = weights[0].shape[1]
    res = pl.pallas_call(
        functools.partial(_ag_kernel, nx, narr),
        out_shape=[jax.ShapeDtypeStruct((n, rows, cols), arrays[0].dtype)] * narr
        + [jax.ShapeDtypeStruct((n, rows, width), jnp.bfloat16)] * narr,
        in_specs=[pl.BlockSpec(memory_space=pltpu.VMEM)] * (2 * narr),
        out_specs=[pl.BlockSpec(memory_space=pltpu.VMEM)] * (2 * narr),
        scratch_shapes=[
            pltpu.SemaphoreType.DMA((narr, nx)),
            pltpu.SemaphoreType.DMA((narr, nx)),
            pltpu.SemaphoreType.DMA((narr, nx)),
            pltpu.SemaphoreType.DMA((narr, nx)),
        ],
        compiler_params=pltpu.CompilerParams(collective_id=cid, has_side_effects=True,
                                             vmem_limit_bytes=64 * 1024 * 1024),
    )(*arrays, *weights)
    gathered = [o.reshape(n * rows, cols) for o in res[:narr]]
    products = [o.reshape(n * rows, width) for o in res[narr:]]
    return gathered, products


def _row_ids():
    me = lax.axis_index("row")
    y = me // 4
    z = me % 4
    k = lax.axis_index("col") % 2
    d = 1 - 2 * k
    return y, z, d


def _row_ag_kernel(ny, *refs):
    ins = refs[:2]
    weights = refs[2:4]
    outs = refs[4:6]
    terms = refs[6:8]
    sa, sb, rsem = refs[8:]

    def product(a, slot):
        if a == 0:
            value = jnp.dot(outs[a][slot], weights[a][...], preferred_element_type=jnp.float32)
        else:
            value = lax.dot_general(outs[a][slot], weights[a][...], (((1,), (1,)), ((), ())),
                                    preferred_element_type=jnp.float32)
        terms[a][slot] = value.astype(terms[a].dtype)

    col = lax.axis_index("col")
    y, z, d = _row_ids()
    me = y * 4 + z
    barrier = pltpu.get_barrier_semaphore()
    peers = (y * 4 + lax.rem(z + 4 + d, 4), y * 4 + lax.rem(z + 4 - d, 4),
             lax.rem(y + ny + d, ny) * 4 + z, lax.rem(y + ny - d, ny) * 4 + z)
    for p in peers:
        pl.semaphore_signal(barrier, inc=1, device_id=(p, col), device_id_type=MESH)
    pl.semaphore_wait(barrier, 4)
    geo = []
    for a in range(2):
        if a == 0:
            na, nb = 4, ny
            pos_a, pos_b = z, y
            slot_of = lambda pa, pb: pb * 4 + pa
        else:
            na, nb = ny, 4
            pos_a, pos_b = y, z
            slot_of = lambda pa, pb: pa * 4 + pb
        geo.append((na, nb, pos_a, pos_b, slot_of))
        outs[a][me] = ins[a][...]

    def dev(a, pa, pb):
        return (geo[a][4](pa, pb), col)

    def send(a, src, slot, target, sem):
        cp = pltpu.make_async_remote_copy(
            src_ref=src, dst_ref=outs[a].at[slot], send_sem=sem, recv_sem=rsem.at[a, slot],
            device_id=target, device_id_type=MESH)
        cp.start()
        return cp

    def wait_in(a, slot):
        pltpu.make_async_remote_copy(
            src_ref=ins[a], dst_ref=outs[a].at[slot], send_sem=sa.at[a, 0], recv_sem=rsem.at[a, slot],
            device_id=(peers[0], col), device_id_type=MESH).wait_recv()

    sends = []
    for a in range(2):
        na, nb, pa, pb, slot_of = geo[a]
        next_a = dev(a, lax.rem(pa + na + d, na), pb)
        next_b = dev(a, pa, lax.rem(pb + nb + d, nb))
        sends.append(send(a, ins[a], me, next_a, sa.at[a, 0]))
        sends.append(send(a, ins[a], me, next_b, sb.at[a, 0, 0]))
    for a in range(2):
        product(a, me)
    for s in range(1, 4):
        for a in range(2):
            na, nb, pa, pb, slot_of = geo[a]
            next_a = dev(a, lax.rem(pa + na + d, na), pb)
            next_b = dev(a, pa, lax.rem(pb + nb + d, nb))
            slot = slot_of(lax.rem(pa + 4 * na - d * s, na), pb)
            wait_in(a, slot)
            if s < na - 1:
                sends.append(send(a, outs[a].at[slot], slot, next_a, sa.at[a, s]))
            sends.append(send(a, outs[a].at[slot], slot, next_b, sb.at[a, 0, s]))
            product(a, slot)
    for t in range(1, 4):
        for j in range(4):
            for a in range(2):
                na, nb, pa, pb, slot_of = geo[a]
                next_b = dev(a, pa, lax.rem(pb + nb + d, nb))
                slot = slot_of(lax.rem(pa + 4 * na - d * j, na), lax.rem(pb + 4 * nb - d * t, nb))
                wait_in(a, slot)
                if t < nb - 1:
                    sends.append(send(a, outs[a].at[slot], slot, next_b, sb.at[a, t, j]))
                product(a, slot)
    for cp in sends:
        cp.wait_send()


def row_all_gather(first, second, w_first, w_second, cid):
    n = lax.axis_size("row")
    ny = n // 4
    rows, cols = first.shape
    width = w_first.shape[1]
    outs = pl.pallas_call(
        functools.partial(_row_ag_kernel, ny),
        out_shape=[jax.ShapeDtypeStruct((n, rows, cols), first.dtype)] * 2
        + [jax.ShapeDtypeStruct((n, rows, width), jnp.bfloat16)] * 2,
        in_specs=[pl.BlockSpec(memory_space=pltpu.VMEM)] * 4,
        out_specs=[pl.BlockSpec(memory_space=pltpu.VMEM)] * 4,
        scratch_shapes=[
            pltpu.SemaphoreType.DMA((2, 4)),
            pltpu.SemaphoreType.DMA((2, 4, 4)),
            pltpu.SemaphoreType.DMA((2, n)),
        ],
        compiler_params=pltpu.CompilerParams(collective_id=cid, has_side_effects=True,
                                             vmem_limit_bytes=64 * 1024 * 1024),
    )(first, second, w_first, w_second)
    return [o.reshape(n * rows, o.shape[2]) for o in outs]


def _row_rs_kernel(ny, *refs):
    ins = refs[:2]
    outs = refs[2:4]
    sb1, rb1, ssum, sb2, rb2, s1, r1, s2, r2 = refs[4:]
    col = lax.axis_index("col")
    y, z, d = _row_ids()
    barrier = pltpu.get_barrier_semaphore()
    peers = (y * 4 + lax.rem(z + 4 + d, 4), y * 4 + lax.rem(z + 4 - d, 4),
             lax.rem(y + ny + d, ny) * 4 + z, lax.rem(y + ny - d, ny) * 4 + z)
    for p in peers:
        pl.semaphore_signal(barrier, inc=1, device_id=(p, col), device_id_type=MESH)
    pl.semaphore_wait(barrier, 4)
    geo = [(4, ny, z, y, lambda pa, pb: pb * 4 + pa), (ny, 4, y, z, lambda pa, pb: pa * 4 + pb)]

    def dev(a, pa, pb):
        return (geo[a][4](pa, pb), col)

    def send(src, dst, ssem, rsem, target):
        cp = pltpu.make_async_remote_copy(src_ref=src, dst_ref=dst, send_sem=ssem, recv_sem=rsem,
                                          device_id=target, device_id_type=MESH)
        cp.start()
        return cp

    sends = []
    first = [[] for _ in range(2)]
    for s in range(4 - 1):
        for a in range(2):
            na, nb, pa, pb, slot_of = geo[a]
            pos = lax.rem(pa + 4 * na - d * (s + 1), na)
            for bq in range(nb):
                own = ins[a][slot_of(pos, bq)]
                if s == 0:
                    sb1[a, s, bq] = own
                else:
                    sb1[a, s, bq] = (rb1[a, s - 1, bq].astype(jnp.float32) + own.astype(jnp.float32)).astype(sb1.dtype)
            cp = send(sb1.at[a, s], rb1.at[a, s], s1.at[a, s], r1.at[a, s],
                      dev(a, lax.rem(pa + na + d, na), pb))
            sends.append(cp)
            first[a].append(cp)
        for a in range(2):
            first[a][s].wait_recv()
    for a in range(2):
        na, nb, pa, pb, slot_of = geo[a]
        for bq in range(nb):
            ssum[a, bq] = rb1[a, 2, bq].astype(jnp.float32) + ins[a][slot_of(pa, bq)].astype(jnp.float32)
    second = [[] for _ in range(2)]
    for t in range(4 - 1):
        for a in range(2):
            na, nb, pa, pb, slot_of = geo[a]
            pos = lax.rem(pb + 4 * nb - d * (t + 1), nb)
            if t == 0:
                sb2[a, t] = ssum[a, pos].astype(sb2.dtype)
            else:
                sb2[a, t] = (rb2[a, t - 1].astype(jnp.float32) + ssum[a, pos]).astype(sb2.dtype)
            cp = send(sb2.at[a, t], rb2.at[a, t], s2.at[a, t], r2.at[a, t],
                      dev(a, pa, lax.rem(pb + nb + d, nb)))
            sends.append(cp)
            second[a].append(cp)
        for a in range(2):
            second[a][t].wait_recv()
    for a in range(2):
        na, nb, pa, pb, slot_of = geo[a]
        outs[a][...] = rb2[a, 2].astype(jnp.float32) + ssum[a, pb]
    for cp in sends:
        cp.wait_send()


def row_reduce_scatter(first, second, cid):
    n = lax.axis_size("row")
    ny = n // 4
    rows, cols = first.shape[0] // n, first.shape[1]
    ins = [v.reshape(n, rows, cols) for v in (first, second)]
    return pl.pallas_call(
        functools.partial(_row_rs_kernel, ny),
        out_shape=[jax.ShapeDtypeStruct((rows, cols), jnp.float32)] * 2,
        in_specs=[pl.BlockSpec(memory_space=pltpu.VMEM)] * 2,
        out_specs=[pl.BlockSpec(memory_space=pltpu.VMEM)] * 2,
        scratch_shapes=[
            pltpu.VMEM((2, 3, 4, rows, cols), jnp.bfloat16),
            pltpu.VMEM((2, 3, 4, rows, cols), jnp.bfloat16),
            pltpu.VMEM((2, 4, rows, cols), jnp.float32),
            pltpu.VMEM((2, 3, rows, cols), jnp.bfloat16),
            pltpu.VMEM((2, 3, rows, cols), jnp.bfloat16),
            pltpu.SemaphoreType.DMA((2, 3)),
            pltpu.SemaphoreType.DMA((2, 3)),
            pltpu.SemaphoreType.DMA((2, 3)),
            pltpu.SemaphoreType.DMA((2, 3)),
        ],
        compiler_params=pltpu.CompilerParams(collective_id=cid, has_side_effects=True,
                                             vmem_limit_bytes=64 * 1024 * 1024),
    )(*ins)


def gelu_grad(value):
    cdf = 0.5 * (1.0 + jax.scipy.special.erf(value * 0.7071067811865476))
    pdf = jnp.exp(-0.5 * value * value) * 0.3989422804014327
    return cdf + value * pdf


def token_panel(local_rows):
    return lax.all_gather(local_rows, "row", axis=0, tiled=True)


def token_panel_a2a(local_rows):
    n = lax.axis_size("row")
    copies = jnp.broadcast_to(local_rows[None], (n,) + local_rows.shape)
    copies = copies.reshape(n * local_rows.shape[0], local_rows.shape[1])
    return lax.all_to_all(copies, "row", split_axis=0, concat_axis=0, tiled=True)


def hidden_panel(local_rows):
    return lax.all_gather(local_rows, "col", axis=0, tiled=True)


def contract_last(left, right):
    return lax.dot_general(
        left, right, (((1,), (1,)), ((), ())), preferred_element_type=jnp.float32
    )


def width_split(left_all, right, transposed):
    if transposed:
        term = contract_last(left_all, right)
    else:
        term = jnp.dot(left_all, right, preferred_element_type=jnp.float32)
    return lax.psum_scatter(
        term.astype(jnp.bfloat16), "col", scatter_dimension=0, tiled=True
    ).astype(jnp.float32)


def unit_sum(left_all, right, transposed):
    n = lax.axis_size("row")
    if transposed:
        term = contract_last(left_all, right)
    else:
        term = jnp.dot(left_all, right, preferred_element_type=jnp.float32)
    pieces = term.astype(jnp.bfloat16).reshape(n, term.shape[0] // n, term.shape[1])
    pieces = lax.all_to_all(pieces, "row", split_axis=0, concat_axis=0, tiled=True)
    return jnp.sum(pieces.astype(jnp.float32), axis=0)


def row_sum(term):
    n = lax.axis_size("row")
    pieces = term.reshape(n, term.shape[0] // n, term.shape[1])
    pieces = lax.all_to_all(pieces, "row", split_axis=0, concat_axis=0, tiled=True)
    return jnp.sum(pieces.astype(jnp.float32), axis=0)


def local(tokens, w_in, w_out, cotangent):
    tokens_all, upstream_all, pre_term, dact_term = row_all_gather(tokens, cotangent, w_in, w_out, 3)
    pre_part, dact_part = col_reduce_scatter([pre_term, dact_term], 1)
    act = jax.nn.gelu(pre_part, approximate=False).astype(jnp.bfloat16)
    dpre = (dact_part * gelu_grad(pre_part)).astype(jnp.bfloat16)
    (act_all, dpre_all), (mixed_term, back_term) = col_all_gather([act, dpre], [w_out, w_in.T], 2)
    mixed, back = row_reduce_scatter(mixed_term, back_term, 4)
    block_rows = (tokens.astype(jnp.float32) + mixed).astype(jnp.bfloat16)
    block_out = lax.all_to_all(block_rows, "col", split_axis=0, concat_axis=1, tiled=True)
    grad_out = lax.dot_general(
        act_all, upstream_all, (((0,), (0,)), ((), ())), preferred_element_type=jnp.float32
    )
    grad_in = lax.dot_general(
        tokens_all, dpre_all, (((0,), (0,)), ((), ())), preferred_element_type=jnp.float32
    )
    grad_tokens = (cotangent.astype(jnp.float32) + back).astype(jnp.bfloat16)
    return (block_out, grad_tokens, grad_in, grad_out)


def solution(mesh):
    in_specs = (P("row", "col"), P("col", "row"), P("row", "col"), P("row", "col"))
    out_specs = (P(("row", "col"), None), P("row", "col"), P("col", "row"), P("row", "col"))
    return jax.shard_map(local, mesh=mesh, in_specs=in_specs, out_specs=out_specs, check_vma=False)
```

```python
import jax
import jax.numpy as jnp
from jax import lax
from jax.sharding import PartitionSpec as P
import functools
from jax.experimental import pallas as pl
from jax.experimental.pallas import tpu as pltpu

MESH = pl.DeviceIdType.MESH


def _col_ids(nx):
    me = lax.axis_index("col")
    x = me // 2
    k = me % 2
    d = 1 - 2 * k
    nxt = lax.rem(x + nx + d, nx)
    prv = lax.rem(x + nx - d, nx)
    return x, k, d, nxt, prv


def _greet(row, k, x, nxt, prv):
    barrier = pltpu.get_barrier_semaphore()
    for peer in (2 * x + 1 - k, 2 * nxt + k, 2 * prv + k):
        pl.semaphore_signal(barrier, inc=1, device_id=(row, peer), device_id_type=MESH)
    pl.semaphore_wait(barrier, 3)


def _rs_kernel(nx, narr, *refs):
    parts = refs[:narr]
    outs = refs[narr:2 * narr]
    recv1, vsum, sendbuf, recv2, s1, r1, s2, r2 = refs[2 * narr:]
    row = lax.axis_index("row")
    x, k, d, nxt, prv = _col_ids(nx)
    _greet(row, k, x, nxt, prv)
    partner = (row, 2 * x + 1 - k)
    nextdev = (row, 2 * nxt + k)
    first = []
    for a in range(narr):
        for i in range(nx):
            cp = pltpu.make_async_remote_copy(
                src_ref=parts[a].at[2 * i + 1 - k], dst_ref=recv1.at[a, i],
                send_sem=s1.at[a, i], recv_sem=r1.at[a, i],
                device_id=partner, device_id_type=MESH)
            cp.start()
            first.append(cp)
    for cp in first:
        cp.wait()
    for a in range(narr):
        for i in range(nx):
            vsum[a, i] = parts[a][2 * i + k].astype(jnp.float32) + recv1[a, i].astype(jnp.float32)
    ring = []
    for step in range(nx - 1):
        for a in range(narr):
            src_idx = lax.rem(x + 4 * nx - d * (step + 1), nx)
            if step == 0:
                sendbuf[a, step] = vsum[a, src_idx].astype(sendbuf.dtype)
            else:
                prevcp = ring[(step - 1) * narr + a]
                prevcp.wait_recv()
                sendbuf[a, step] = (recv2[a, step - 1].astype(jnp.float32) + vsum[a, src_idx]).astype(sendbuf.dtype)
            cp = pltpu.make_async_remote_copy(
                src_ref=sendbuf.at[a, step], dst_ref=recv2.at[a, step],
                send_sem=s2.at[a, step], recv_sem=r2.at[a, step],
                device_id=nextdev, device_id_type=MESH)
            cp.start()
            ring.append(cp)
    for a in range(narr):
        last = ring[(nx - 2) * narr + a]
        last.wait_recv()
        outs[a][...] = recv2[a, nx - 2].astype(jnp.float32) + vsum[a, x]
    for cp in ring:
        cp.wait_send()


def col_reduce_scatter(arrays, cid):
    n = lax.axis_size("col")
    nx = n // 2
    narr = len(arrays)
    rows = arrays[0].shape[0] // n
    cols = arrays[0].shape[1]
    parts = [a.reshape(n, rows, cols) for a in arrays]
    return pl.pallas_call(
        functools.partial(_rs_kernel, nx, narr),
        out_shape=[jax.ShapeDtypeStruct((rows, cols), jnp.float32)] * narr,
        in_specs=[pl.BlockSpec(memory_space=pltpu.VMEM)] * narr,
        out_specs=[pl.BlockSpec(memory_space=pltpu.VMEM)] * narr,
        scratch_shapes=[
            pltpu.VMEM((narr, nx, rows, cols), jnp.bfloat16),
            pltpu.VMEM((narr, nx, rows, cols), jnp.float32),
            pltpu.VMEM((narr, nx - 1, rows, cols), jnp.bfloat16),
            pltpu.VMEM((narr, nx - 1, rows, cols), jnp.bfloat16),
            pltpu.SemaphoreType.DMA((narr, nx)),
            pltpu.SemaphoreType.DMA((narr, nx)),
            pltpu.SemaphoreType.DMA((narr, nx - 1)),
            pltpu.SemaphoreType.DMA((narr, nx - 1)),
        ],
        compiler_params=pltpu.CompilerParams(collective_id=cid, has_side_effects=True,
                                             vmem_limit_bytes=64 * 1024 * 1024),
    )(*parts)


def _ag_kernel(nx, narr, *refs):
    chunks = refs[:narr]
    weights = refs[narr:2 * narr]
    outs = refs[2 * narr:3 * narr]
    prods = refs[3 * narr:4 * narr]
    sr, rr, sc, rc = refs[4 * narr:]
    row = lax.axis_index("row")
    x, k, d, nxt, prv = _col_ids(nx)
    _greet(row, k, x, nxt, prv)
    me = 2 * x + k
    partner = (row, 2 * x + 1 - k)
    nextdev = (row, 2 * nxt + k)

    def product(a, slot):
        prods[a][slot] = jnp.dot(outs[a][slot], weights[a][...],
                                 preferred_element_type=jnp.float32).astype(prods[a].dtype)

    for a in range(narr):
        outs[a][me] = chunks[a][...]
    ring, core = [], []
    for step in range(nx):
        for a in range(narr):
            src_x = lax.rem(x + 4 * nx - d * step, nx)
            slot = 2 * src_x + k
            if step > 0:
                ring[(step - 1) * narr + a].wait_recv()
            src = chunks[a] if step == 0 else outs[a].at[slot]
            if step < nx - 1:
                cp = pltpu.make_async_remote_copy(
                    src_ref=src, dst_ref=outs[a].at[slot],
                    send_sem=sr.at[a, step], recv_sem=rr.at[a, step],
                    device_id=nextdev, device_id_type=MESH)
                cp.start()
                ring.append(cp)
            cc = pltpu.make_async_remote_copy(
                src_ref=src, dst_ref=outs[a].at[slot],
                send_sem=sc.at[a, step], recv_sem=rc.at[a, step],
                device_id=partner, device_id_type=MESH)
            cc.start()
            core.append(cc)
        for a in range(narr):
            product(a, 2 * lax.rem(x + 4 * nx - d * step, nx) + k)
    for cp in ring:
        cp.wait_send()
    for step in range(nx):
        for a in range(narr):
            core[step * narr + a].wait()
        for a in range(narr):
            product(a, 2 * lax.rem(x + 4 * nx + d * step, nx) + 1 - k)


def col_all_gather(arrays, weights, cid):
    n = lax.axis_size("col")
    nx = n // 2
    narr = len(arrays)
    rows, cols = arrays[0].shape
    width = weights[0].shape[1]
    res = pl.pallas_call(
        functools.partial(_ag_kernel, nx, narr),
        out_shape=[jax.ShapeDtypeStruct((n, rows, cols), arrays[0].dtype)] * narr
        + [jax.ShapeDtypeStruct((n, rows, width), jnp.bfloat16)] * narr,
        in_specs=[pl.BlockSpec(memory_space=pltpu.VMEM)] * (2 * narr),
        out_specs=[pl.BlockSpec(memory_space=pltpu.VMEM)] * (2 * narr),
        scratch_shapes=[
            pltpu.SemaphoreType.DMA((narr, nx)),
            pltpu.SemaphoreType.DMA((narr, nx)),
            pltpu.SemaphoreType.DMA((narr, nx)),
            pltpu.SemaphoreType.DMA((narr, nx)),
        ],
        compiler_params=pltpu.CompilerParams(collective_id=cid, has_side_effects=True,
                                             vmem_limit_bytes=64 * 1024 * 1024),
    )(*arrays, *weights)
    gathered = [o.reshape(n * rows, cols) for o in res[:narr]]
    products = [o.reshape(n * rows, width) for o in res[narr:]]
    return gathered, products


def _row_ids():
    me = lax.axis_index("row")
    y = me // 4
    z = me % 4
    k = lax.axis_index("col") % 2
    d = 1 - 2 * k
    return y, z, d


def _row_ag_kernel(ny, *refs):
    ins = refs[:2]
    weights = refs[2:4]
    outs = refs[4:6]
    terms = refs[6:8]
    sa, sb, rsem = refs[8:]

    def product(a, slot):
        if a == 0:
            value = jnp.dot(outs[a][slot], weights[a][...], preferred_element_type=jnp.float32)
        else:
            value = lax.dot_general(outs[a][slot], weights[a][...], (((1,), (1,)), ((), ())),
                                    preferred_element_type=jnp.float32)
        terms[a][slot] = value.astype(terms[a].dtype)

    col = lax.axis_index("col")
    y, z, d = _row_ids()
    me = y * 4 + z
    barrier = pltpu.get_barrier_semaphore()
    peers = (y * 4 + lax.rem(z + 4 + d, 4), y * 4 + lax.rem(z + 4 - d, 4),
             lax.rem(y + ny + d, ny) * 4 + z, lax.rem(y + ny - d, ny) * 4 + z)
    for p in peers:
        pl.semaphore_signal(barrier, inc=1, device_id=(p, col), device_id_type=MESH)
    pl.semaphore_wait(barrier, 4)
    geo = []
    for a in range(2):
        if a == 0:
            na, nb = 4, ny
            pos_a, pos_b = z, y
            slot_of = lambda pa, pb: pb * 4 + pa
        else:
            na, nb = ny, 4
            pos_a, pos_b = y, z
            slot_of = lambda pa, pb: pa * 4 + pb
        geo.append((na, nb, pos_a, pos_b, slot_of))
        outs[a][me] = ins[a][...]

    def dev(a, pa, pb):
        return (geo[a][4](pa, pb), col)

    def send(a, src, slot, target, sem):
        cp = pltpu.make_async_remote_copy(
            src_ref=src, dst_ref=outs[a].at[slot], send_sem=sem, recv_sem=rsem.at[a, slot],
            device_id=target, device_id_type=MESH)
        cp.start()
        return cp

    def wait_in(a, slot):
        pltpu.make_async_remote_copy(
            src_ref=ins[a], dst_ref=outs[a].at[slot], send_sem=sa.at[a, 0], recv_sem=rsem.at[a, slot],
            device_id=(peers[0], col), device_id_type=MESH).wait_recv()

    sends = []
    for a in range(2):
        na, nb, pa, pb, slot_of = geo[a]
        next_a = dev(a, lax.rem(pa + na + d, na), pb)
        next_b = dev(a, pa, lax.rem(pb + nb + d, nb))
        sends.append(send(a, ins[a], me, next_a, sa.at[a, 0]))
        sends.append(send(a, ins[a], me, next_b, sb.at[a, 0, 0]))
    for a in range(2):
        product(a, me)
    for s in range(1, 4):
        for a in range(2):
            na, nb, pa, pb, slot_of = geo[a]
            next_a = dev(a, lax.rem(pa + na + d, na), pb)
            next_b = dev(a, pa, lax.rem(pb + nb + d, nb))
            slot = slot_of(lax.rem(pa + 4 * na - d * s, na), pb)
            wait_in(a, slot)
            if s < na - 1:
                sends.append(send(a, outs[a].at[slot], slot, next_a, sa.at[a, s]))
            sends.append(send(a, outs[a].at[slot], slot, next_b, sb.at[a, 0, s]))
            product(a, slot)
    for t in range(1, 4):
        for j in range(4):
            for a in range(2):
                na, nb, pa, pb, slot_of = geo[a]
                next_b = dev(a, pa, lax.rem(pb + nb + d, nb))
                slot = slot_of(lax.rem(pa + 4 * na - d * j, na), lax.rem(pb + 4 * nb - d * t, nb))
                wait_in(a, slot)
                if t < nb - 1:
                    sends.append(send(a, outs[a].at[slot], slot, next_b, sb.at[a, t, j]))
                product(a, slot)
    for cp in sends:
        cp.wait_send()


def row_all_gather(first, second, w_first, w_second, cid):
    n = lax.axis_size("row")
    ny = n // 4
    rows, cols = first.shape
    width = w_first.shape[1]
    outs = pl.pallas_call(
        functools.partial(_row_ag_kernel, ny),
        out_shape=[jax.ShapeDtypeStruct((n, rows, cols), first.dtype)] * 2
        + [jax.ShapeDtypeStruct((n, rows, width), jnp.bfloat16)] * 2,
        in_specs=[pl.BlockSpec(memory_space=pltpu.VMEM)] * 4,
        out_specs=[pl.BlockSpec(memory_space=pltpu.VMEM)] * 4,
        scratch_shapes=[
            pltpu.SemaphoreType.DMA((2, 4)),
            pltpu.SemaphoreType.DMA((2, 4, 4)),
            pltpu.SemaphoreType.DMA((2, n)),
        ],
        compiler_params=pltpu.CompilerParams(collective_id=cid, has_side_effects=True,
                                             vmem_limit_bytes=64 * 1024 * 1024),
    )(first, second, w_first, w_second)
    return [o.reshape(n * rows, o.shape[2]) for o in outs]


def _row_rs_kernel(ny, *refs):
    ins = refs[:2]
    lefts = refs[2:4]
    rights = refs[4:6]
    outs = refs[6:8]
    grads = refs[8:10]
    sb1, rb1, ssum, sb2, rb2, s1, r1, s2, r2 = refs[10:]
    span = 256
    pending = [(g, c) for c in range(lefts[0].shape[0] // span) for g in range(2)]

    def grad_work(count):
        for _ in range(count):
            if not pending:
                return
            g, c = pending.pop(0)
            rows = pl.ds(c * span, span)
            value = lax.dot_general(lefts[g][rows, :], rights[g][rows, :], (((0,), (0,)), ((), ())),
                                    preferred_element_type=jnp.float32)
            if c == 0:
                grads[g][...] = value
            else:
                grads[g][...] += value

    col = lax.axis_index("col")
    y, z, d = _row_ids()
    barrier = pltpu.get_barrier_semaphore()
    peers = (y * 4 + lax.rem(z + 4 + d, 4), y * 4 + lax.rem(z + 4 - d, 4),
             lax.rem(y + ny + d, ny) * 4 + z, lax.rem(y + ny - d, ny) * 4 + z)
    for p in peers:
        pl.semaphore_signal(barrier, inc=1, device_id=(p, col), device_id_type=MESH)
    pl.semaphore_wait(barrier, 4)
    geo = [(4, ny, z, y, lambda pa, pb: pb * 4 + pa), (ny, 4, y, z, lambda pa, pb: pa * 4 + pb)]

    def dev(a, pa, pb):
        return (geo[a][4](pa, pb), col)

    def send(src, dst, ssem, rsem, target):
        cp = pltpu.make_async_remote_copy(src_ref=src, dst_ref=dst, send_sem=ssem, recv_sem=rsem,
                                          device_id=target, device_id_type=MESH)
        cp.start()
        return cp

    sends = []
    first = [[] for _ in range(2)]
    for s in range(4 - 1):
        for a in range(2):
            na, nb, pa, pb, slot_of = geo[a]
            pos = lax.rem(pa + 4 * na - d * (s + 1), na)
            for bq in range(nb):
                own = ins[a][slot_of(pos, bq)]
                if s == 0:
                    sb1[a, s, bq] = own
                else:
                    sb1[a, s, bq] = (rb1[a, s - 1, bq].astype(jnp.float32) + own.astype(jnp.float32)).astype(sb1.dtype)
            cp = send(sb1.at[a, s], rb1.at[a, s], s1.at[a, s], r1.at[a, s],
                      dev(a, lax.rem(pa + na + d, na), pb))
            sends.append(cp)
            first[a].append(cp)
        grad_work(3)
        for a in range(2):
            first[a][s].wait_recv()
    for a in range(2):
        na, nb, pa, pb, slot_of = geo[a]
        for bq in range(nb):
            ssum[a, bq] = rb1[a, 2, bq].astype(jnp.float32) + ins[a][slot_of(pa, bq)].astype(jnp.float32)
    second = [[] for _ in range(2)]
    for t in range(4 - 1):
        for a in range(2):
            na, nb, pa, pb, slot_of = geo[a]
            pos = lax.rem(pb + 4 * nb - d * (t + 1), nb)
            if t == 0:
                sb2[a, t] = ssum[a, pos].astype(sb2.dtype)
            else:
                sb2[a, t] = (rb2[a, t - 1].astype(jnp.float32) + ssum[a, pos]).astype(sb2.dtype)
            cp = send(sb2.at[a, t], rb2.at[a, t], s2.at[a, t], r2.at[a, t],
                      dev(a, pa, lax.rem(pb + nb + d, nb)))
            sends.append(cp)
            second[a].append(cp)
        grad_work(3)
        for a in range(2):
            second[a][t].wait_recv()
    for a in range(2):
        na, nb, pa, pb, slot_of = geo[a]
        outs[a][...] = rb2[a, 2].astype(jnp.float32) + ssum[a, pb]
    grad_work(len(pending))
    for cp in sends:
        cp.wait_send()


def row_reduce_scatter(first, second, lefts, rights, cid):
    n = lax.axis_size("row")
    ny = n // 4
    rows, cols = first.shape[0] // n, first.shape[1]
    ins = [v.reshape(n, rows, cols) for v in (first, second)]
    grad_shapes = [jax.ShapeDtypeStruct((l.shape[1], r.shape[1]), jnp.float32) for l, r in zip(lefts, rights)]
    return pl.pallas_call(
        functools.partial(_row_rs_kernel, ny),
        out_shape=[jax.ShapeDtypeStruct((rows, cols), jnp.float32)] * 2 + grad_shapes,
        in_specs=[pl.BlockSpec(memory_space=pltpu.VMEM)] * 6,
        out_specs=[pl.BlockSpec(memory_space=pltpu.VMEM)] * 4,
        scratch_shapes=[
            pltpu.VMEM((2, 3, 4, rows, cols), jnp.bfloat16),
            pltpu.VMEM((2, 3, 4, rows, cols), jnp.bfloat16),
            pltpu.VMEM((2, 4, rows, cols), jnp.float32),
            pltpu.VMEM((2, 3, rows, cols), jnp.bfloat16),
            pltpu.VMEM((2, 3, rows, cols), jnp.bfloat16),
            pltpu.SemaphoreType.DMA((2, 3)),
            pltpu.SemaphoreType.DMA((2, 3)),
            pltpu.SemaphoreType.DMA((2, 3)),
            pltpu.SemaphoreType.DMA((2, 3)),
        ],
        compiler_params=pltpu.CompilerParams(collective_id=cid, has_side_effects=True,
                                             vmem_limit_bytes=64 * 1024 * 1024),
    )(*ins, *lefts, *rights)


def gelu_grad(value):
    cdf = 0.5 * (1.0 + jax.scipy.special.erf(value * 0.7071067811865476))
    pdf = jnp.exp(-0.5 * value * value) * 0.3989422804014327
    return cdf + value * pdf


def token_panel(local_rows):
    return lax.all_gather(local_rows, "row", axis=0, tiled=True)


def token_panel_a2a(local_rows):
    n = lax.axis_size("row")
    copies = jnp.broadcast_to(local_rows[None], (n,) + local_rows.shape)
    copies = copies.reshape(n * local_rows.shape[0], local_rows.shape[1])
    return lax.all_to_all(copies, "row", split_axis=0, concat_axis=0, tiled=True)


def hidden_panel(local_rows):
    return lax.all_gather(local_rows, "col", axis=0, tiled=True)


def contract_last(left, right):
    return lax.dot_general(
        left, right, (((1,), (1,)), ((), ())), preferred_element_type=jnp.float32
    )


def width_split(left_all, right, transposed):
    if transposed:
        term = contract_last(left_all, right)
    else:
        term = jnp.dot(left_all, right, preferred_element_type=jnp.float32)
    return lax.psum_scatter(
        term.astype(jnp.bfloat16), "col", scatter_dimension=0, tiled=True
    ).astype(jnp.float32)


def unit_sum(left_all, right, transposed):
    n = lax.axis_size("row")
    if transposed:
        term = contract_last(left_all, right)
    else:
        term = jnp.dot(left_all, right, preferred_element_type=jnp.float32)
    pieces = term.astype(jnp.bfloat16).reshape(n, term.shape[0] // n, term.shape[1])
    pieces = lax.all_to_all(pieces, "row", split_axis=0, concat_axis=0, tiled=True)
    return jnp.sum(pieces.astype(jnp.float32), axis=0)


def row_sum(term):
    n = lax.axis_size("row")
    pieces = term.reshape(n, term.shape[0] // n, term.shape[1])
    pieces = lax.all_to_all(pieces, "row", split_axis=0, concat_axis=0, tiled=True)
    return jnp.sum(pieces.astype(jnp.float32), axis=0)


def local(tokens, w_in, w_out, cotangent):
    tokens_all, upstream_all, pre_term, dact_term = row_all_gather(tokens, cotangent, w_in, w_out, 3)
    pre_part, dact_part = col_reduce_scatter([pre_term, dact_term], 1)
    act = jax.nn.gelu(pre_part, approximate=False).astype(jnp.bfloat16)
    dpre = (dact_part * gelu_grad(pre_part)).astype(jnp.bfloat16)
    (act_all, dpre_all), (mixed_term, back_term) = col_all_gather([act, dpre], [w_out, w_in.T], 2)
    mixed, back, grad_out, grad_in = row_reduce_scatter(
        mixed_term, back_term, [act_all, tokens_all], [upstream_all, dpre_all], 4)
    block_rows = (tokens.astype(jnp.float32) + mixed).astype(jnp.bfloat16)
    block_out = lax.all_to_all(block_rows, "col", split_axis=0, concat_axis=1, tiled=True)
    grad_tokens = (cotangent.astype(jnp.float32) + back).astype(jnp.bfloat16)
    return (block_out, grad_tokens, grad_in, grad_out)


def solution(mesh):
    in_specs = (P("row", "col"), P("col", "row"), P("row", "col"), P("row", "col"))
    out_specs = (P(("row", "col"), None), P("row", "col"), P("col", "row"), P("row", "col"))
    return jax.shard_map(local, mesh=mesh, in_specs=in_specs, out_specs=out_specs, check_vma=False)
```

```python
import jax
import jax.numpy as jnp
from jax import lax
from jax.sharding import PartitionSpec as P
import functools
from jax.experimental import pallas as pl
from jax.experimental.pallas import tpu as pltpu

MESH = pl.DeviceIdType.MESH


def _col_ids(nx):
    me = lax.axis_index("col")
    x = me // 2
    k = me % 2
    d = 1 - 2 * k
    nxt = lax.rem(x + nx + d, nx)
    prv = lax.rem(x + nx - d, nx)
    return x, k, d, nxt, prv


def _greet(row, k, x, nxt, prv):
    barrier = pltpu.get_barrier_semaphore()
    for peer in (2 * x + 1 - k, 2 * nxt + k, 2 * prv + k):
        pl.semaphore_signal(barrier, inc=1, device_id=(row, peer), device_id_type=MESH)
    pl.semaphore_wait(barrier, 3)


def _rs_kernel(nx, narr, *refs):
    parts = refs[:narr]
    outs = refs[narr:2 * narr]
    recv1, sendbuf, recv2, s1, r1, s2, r2 = refs[2 * narr:]
    row = lax.axis_index("row")
    x, k, d, nxt, prv = _col_ids(nx)
    _greet(row, k, x, nxt, prv)
    partner = (row, 2 * x + 1 - k)
    nextdev = (row, 2 * nxt + k)

    def order(j, sign):
        if j == nx - 1:
            return x
        return lax.rem(x + 4 * nx + sign * d * (j + 1), nx)

    first = []
    for j in range(nx):
        for a in range(narr):
            cp = pltpu.make_async_remote_copy(
                src_ref=parts[a].at[2 * order(j, 1) + 1 - k], dst_ref=recv1.at[a, j],
                send_sem=s1.at[a, j], recv_sem=r1.at[a, j],
                device_id=partner, device_id_type=MESH)
            cp.start()
            first.append(cp)

    def chip_sum(a, j):
        first[j * narr + a].wait_recv()
        own = parts[a][2 * order(j, -1) + k].astype(jnp.float32)
        return own + recv1[a, j].astype(jnp.float32)

    ring = []
    for step in range(nx - 1):
        for a in range(narr):
            value = chip_sum(a, step)
            if step == 0:
                sendbuf[a, step] = value.astype(sendbuf.dtype)
            else:
                ring[(step - 1) * narr + a].wait_recv()
                sendbuf[a, step] = (recv2[a, step - 1].astype(jnp.float32) + value).astype(sendbuf.dtype)
            cp = pltpu.make_async_remote_copy(
                src_ref=sendbuf.at[a, step], dst_ref=recv2.at[a, step],
                send_sem=s2.at[a, step], recv_sem=r2.at[a, step],
                device_id=nextdev, device_id_type=MESH)
            cp.start()
            ring.append(cp)
    for a in range(narr):
        value = chip_sum(a, nx - 1)
        ring[(nx - 2) * narr + a].wait_recv()
        outs[a][...] = recv2[a, nx - 2].astype(jnp.float32) + value
    for cp in first:
        cp.wait_send()
    for cp in ring:
        cp.wait_send()


def col_reduce_scatter(arrays, cid):
    n = lax.axis_size("col")
    nx = n // 2
    narr = len(arrays)
    rows = arrays[0].shape[0] // n
    cols = arrays[0].shape[1]
    parts = [a.reshape(n, rows, cols) for a in arrays]
    return pl.pallas_call(
        functools.partial(_rs_kernel, nx, narr),
        out_shape=[jax.ShapeDtypeStruct((rows, cols), jnp.float32)] * narr,
        in_specs=[pl.BlockSpec(memory_space=pltpu.VMEM)] * narr,
        out_specs=[pl.BlockSpec(memory_space=pltpu.VMEM)] * narr,
        scratch_shapes=[
            pltpu.VMEM((narr, nx, rows, cols), jnp.bfloat16),
            pltpu.VMEM((narr, nx - 1, rows, cols), jnp.bfloat16),
            pltpu.VMEM((narr, nx - 1, rows, cols), jnp.bfloat16),
            pltpu.SemaphoreType.DMA((narr, nx)),
            pltpu.SemaphoreType.DMA((narr, nx)),
            pltpu.SemaphoreType.DMA((narr, nx - 1)),
            pltpu.SemaphoreType.DMA((narr, nx - 1)),
        ],
        compiler_params=pltpu.CompilerParams(collective_id=cid, has_side_effects=True,
                                             vmem_limit_bytes=64 * 1024 * 1024),
    )(*parts)


def _ag_kernel(nx, narr, *refs):
    chunks = refs[:narr]
    weights = refs[narr:2 * narr]
    outs = refs[2 * narr:3 * narr]
    prods = refs[3 * narr:4 * narr]
    sr, rr, sc, rc = refs[4 * narr:]
    row = lax.axis_index("row")
    x, k, d, nxt, prv = _col_ids(nx)
    _greet(row, k, x, nxt, prv)
    me = 2 * x + k
    partner = (row, 2 * x + 1 - k)
    nextdev = (row, 2 * nxt + k)

    def product(a, slot):
        prods[a][slot] = jnp.dot(outs[a][slot], weights[a][...],
                                 preferred_element_type=jnp.float32).astype(prods[a].dtype)

    for a in range(narr):
        outs[a][me] = chunks[a][...]
    ring, core = [], []
    for step in range(nx):
        for a in range(narr):
            src_x = lax.rem(x + 4 * nx - d * step, nx)
            slot = 2 * src_x + k
            if step > 0:
                ring[(step - 1) * narr + a].wait_recv()
            src = chunks[a] if step == 0 else outs[a].at[slot]
            if step < nx - 1:
                cp = pltpu.make_async_remote_copy(
                    src_ref=src, dst_ref=outs[a].at[slot],
                    send_sem=sr.at[a, step], recv_sem=rr.at[a, step],
                    device_id=nextdev, device_id_type=MESH)
                cp.start()
                ring.append(cp)
            cc = pltpu.make_async_remote_copy(
                src_ref=src, dst_ref=outs[a].at[slot],
                send_sem=sc.at[a, step], recv_sem=rc.at[a, step],
                device_id=partner, device_id_type=MESH)
            cc.start()
            core.append(cc)
        for a in range(narr):
            product(a, 2 * lax.rem(x + 4 * nx - d * step, nx) + k)
    for cp in ring:
        cp.wait_send()
    for step in range(nx):
        for a in range(narr):
            core[step * narr + a].wait()
        for a in range(narr):
            product(a, 2 * lax.rem(x + 4 * nx + d * step, nx) + 1 - k)


def col_all_gather(arrays, weights, cid):
    n = lax.axis_size("col")
    nx = n // 2
    narr = len(arrays)
    rows, cols = arrays[0].shape
    width = weights[0].shape[1]
    res = pl.pallas_call(
        functools.partial(_ag_kernel, nx, narr),
        out_shape=[jax.ShapeDtypeStruct((n, rows, cols), arrays[0].dtype)] * narr
        + [jax.ShapeDtypeStruct((n, rows, width), jnp.bfloat16)] * narr,
        in_specs=[pl.BlockSpec(memory_space=pltpu.VMEM)] * (2 * narr),
        out_specs=[pl.BlockSpec(memory_space=pltpu.VMEM)] * (2 * narr),
        scratch_shapes=[
            pltpu.SemaphoreType.DMA((narr, nx)),
            pltpu.SemaphoreType.DMA((narr, nx)),
            pltpu.SemaphoreType.DMA((narr, nx)),
            pltpu.SemaphoreType.DMA((narr, nx)),
        ],
        compiler_params=pltpu.CompilerParams(collective_id=cid, has_side_effects=True,
                                             vmem_limit_bytes=64 * 1024 * 1024),
    )(*arrays, *weights)
    gathered = [o.reshape(n * rows, cols) for o in res[:narr]]
    products = [o.reshape(n * rows, width) for o in res[narr:]]
    return gathered, products


def _row_ids():
    me = lax.axis_index("row")
    y = me // 4
    z = me % 4
    k = lax.axis_index("col") % 2
    d = 1 - 2 * k
    return y, z, d


def _row_ag_kernel(ny, *refs):
    ins = refs[:2]
    weights = refs[2:4]
    outs = refs[4:6]
    terms = refs[6:8]
    sa, sb, rsem = refs[8:]

    def product(a, slot):
        if a == 0:
            value = jnp.dot(outs[a][slot], weights[a][...], preferred_element_type=jnp.float32)
        else:
            value = lax.dot_general(outs[a][slot], weights[a][...], (((1,), (1,)), ((), ())),
                                    preferred_element_type=jnp.float32)
        terms[a][slot] = value.astype(terms[a].dtype)

    col = lax.axis_index("col")
    y, z, d = _row_ids()
    me = y * 4 + z
    barrier = pltpu.get_barrier_semaphore()
    peers = (y * 4 + lax.rem(z + 4 + d, 4), y * 4 + lax.rem(z + 4 - d, 4),
             lax.rem(y + ny + d, ny) * 4 + z, lax.rem(y + ny - d, ny) * 4 + z)
    for p in peers:
        pl.semaphore_signal(barrier, inc=1, device_id=(p, col), device_id_type=MESH)
    pl.semaphore_wait(barrier, 4)
    geo = []
    for a in range(2):
        if a == 0:
            na, nb = 4, ny
            pos_a, pos_b = z, y
            slot_of = lambda pa, pb: pb * 4 + pa
        else:
            na, nb = ny, 4
            pos_a, pos_b = y, z
            slot_of = lambda pa, pb: pa * 4 + pb
        geo.append((na, nb, pos_a, pos_b, slot_of))
        outs[a][me] = ins[a][...]

    def dev(a, pa, pb):
        return (geo[a][4](pa, pb), col)

    def send(a, src, slot, target, sem):
        cp = pltpu.make_async_remote_copy(
            src_ref=src, dst_ref=outs[a].at[slot], send_sem=sem, recv_sem=rsem.at[a, slot],
            device_id=target, device_id_type=MESH)
        cp.start()
        return cp

    def wait_in(a, slot):
        pltpu.make_async_remote_copy(
            src_ref=ins[a], dst_ref=outs[a].at[slot], send_sem=sa.at[a, 0], recv_sem=rsem.at[a, slot],
            device_id=(peers[0], col), device_id_type=MESH).wait_recv()

    sends = []
    for a in range(2):
        na, nb, pa, pb, slot_of = geo[a]
        next_a = dev(a, lax.rem(pa + na + d, na), pb)
        next_b = dev(a, pa, lax.rem(pb + nb + d, nb))
        sends.append(send(a, ins[a], me, next_a, sa.at[a, 0]))
        sends.append(send(a, ins[a], me, next_b, sb.at[a, 0, 0]))
    for a in range(2):
        product(a, me)
    for s in range(1, 4):
        for a in range(2):
            na, nb, pa, pb, slot_of = geo[a]
            next_a = dev(a, lax.rem(pa + na + d, na), pb)
            next_b = dev(a, pa, lax.rem(pb + nb + d, nb))
            slot = slot_of(lax.rem(pa + 4 * na - d * s, na), pb)
            wait_in(a, slot)
            if s < na - 1:
                sends.append(send(a, outs[a].at[slot], slot, next_a, sa.at[a, s]))
            sends.append(send(a, outs[a].at[slot], slot, next_b, sb.at[a, 0, s]))
            product(a, slot)
    for t in range(1, 4):
        for j in range(4):
            for a in range(2):
                na, nb, pa, pb, slot_of = geo[a]
                next_b = dev(a, pa, lax.rem(pb + nb + d, nb))
                slot = slot_of(lax.rem(pa + 4 * na - d * j, na), lax.rem(pb + 4 * nb - d * t, nb))
                wait_in(a, slot)
                if t < nb - 1:
                    sends.append(send(a, outs[a].at[slot], slot, next_b, sb.at[a, t, j]))
                product(a, slot)
    for cp in sends:
        cp.wait_send()


def row_all_gather(first, second, w_first, w_second, cid):
    n = lax.axis_size("row")
    ny = n // 4
    rows, cols = first.shape
    width = w_first.shape[1]
    outs = pl.pallas_call(
        functools.partial(_row_ag_kernel, ny),
        out_shape=[jax.ShapeDtypeStruct((n, rows, cols), first.dtype)] * 2
        + [jax.ShapeDtypeStruct((n, rows, width), jnp.bfloat16)] * 2,
        in_specs=[pl.BlockSpec(memory_space=pltpu.VMEM)] * 4,
        out_specs=[pl.BlockSpec(memory_space=pltpu.VMEM)] * 4,
        scratch_shapes=[
            pltpu.SemaphoreType.DMA((2, 4)),
            pltpu.SemaphoreType.DMA((2, 4, 4)),
            pltpu.SemaphoreType.DMA((2, n)),
        ],
        compiler_params=pltpu.CompilerParams(collective_id=cid, has_side_effects=True,
                                             vmem_limit_bytes=64 * 1024 * 1024),
    )(first, second, w_first, w_second)
    return [o.reshape(n * rows, o.shape[2]) for o in outs]


def _row_rs_kernel(ny, *refs):
    ins = refs[:2]
    outs = refs[2:4]
    sb1, rb1, ssum, sb2, rb2, s1, r1, s2, r2 = refs[4:]
    col = lax.axis_index("col")
    y, z, d = _row_ids()
    barrier = pltpu.get_barrier_semaphore()
    peers = (y * 4 + lax.rem(z + 4 + d, 4), y * 4 + lax.rem(z + 4 - d, 4),
             lax.rem(y + ny + d, ny) * 4 + z, lax.rem(y + ny - d, ny) * 4 + z)
    for p in peers:
        pl.semaphore_signal(barrier, inc=1, device_id=(p, col), device_id_type=MESH)
    pl.semaphore_wait(barrier, 4)
    geo = [(4, ny, z, y, lambda pa, pb: pb * 4 + pa), (ny, 4, y, z, lambda pa, pb: pa * 4 + pb)]

    def dev(a, pa, pb):
        return (geo[a][4](pa, pb), col)

    def send(src, dst, ssem, rsem, target):
        cp = pltpu.make_async_remote_copy(src_ref=src, dst_ref=dst, send_sem=ssem, recv_sem=rsem,
                                          device_id=target, device_id_type=MESH)
        cp.start()
        return cp

    sends = []
    first = [[] for _ in range(2)]
    for s in range(4 - 1):
        for a in range(2):
            na, nb, pa, pb, slot_of = geo[a]
            pos = lax.rem(pa + 4 * na - d * (s + 1), na)
            for bq in range(nb):
                own = ins[a][slot_of(pos, bq)]
                if s == 0:
                    sb1[a, s, bq] = own
                else:
                    sb1[a, s, bq] = (rb1[a, s - 1, bq].astype(jnp.float32) + own.astype(jnp.float32)).astype(sb1.dtype)
            cp = send(sb1.at[a, s], rb1.at[a, s], s1.at[a, s], r1.at[a, s],
                      dev(a, lax.rem(pa + na + d, na), pb))
            sends.append(cp)
            first[a].append(cp)
        for a in range(2):
            first[a][s].wait_recv()
    for a in range(2):
        na, nb, pa, pb, slot_of = geo[a]
        for bq in range(nb):
            ssum[a, bq] = rb1[a, 2, bq].astype(jnp.float32) + ins[a][slot_of(pa, bq)].astype(jnp.float32)
    second = [[] for _ in range(2)]
    for t in range(4 - 1):
        for a in range(2):
            na, nb, pa, pb, slot_of = geo[a]
            pos = lax.rem(pb + 4 * nb - d * (t + 1), nb)
            if t == 0:
                sb2[a, t] = ssum[a, pos].astype(sb2.dtype)
            else:
                sb2[a, t] = (rb2[a, t - 1].astype(jnp.float32) + ssum[a, pos]).astype(sb2.dtype)
            cp = send(sb2.at[a, t], rb2.at[a, t], s2.at[a, t], r2.at[a, t],
                      dev(a, pa, lax.rem(pb + nb + d, nb)))
            sends.append(cp)
            second[a].append(cp)
        for a in range(2):
            second[a][t].wait_recv()
    for a in range(2):
        na, nb, pa, pb, slot_of = geo[a]
        outs[a][...] = rb2[a, 2].astype(jnp.float32) + ssum[a, pb]
    for cp in sends:
        cp.wait_send()


def row_reduce_scatter(first, second, cid):
    n = lax.axis_size("row")
    ny = n // 4
    rows, cols = first.shape[0] // n, first.shape[1]
    ins = [v.reshape(n, rows, cols) for v in (first, second)]
    return pl.pallas_call(
        functools.partial(_row_rs_kernel, ny),
        out_shape=[jax.ShapeDtypeStruct((rows, cols), jnp.float32)] * 2,
        in_specs=[pl.BlockSpec(memory_space=pltpu.VMEM)] * 2,
        out_specs=[pl.BlockSpec(memory_space=pltpu.VMEM)] * 2,
        scratch_shapes=[
            pltpu.VMEM((2, 3, 4, rows, cols), jnp.bfloat16),
            pltpu.VMEM((2, 3, 4, rows, cols), jnp.bfloat16),
            pltpu.VMEM((2, 4, rows, cols), jnp.float32),
            pltpu.VMEM((2, 3, rows, cols), jnp.bfloat16),
            pltpu.VMEM((2, 3, rows, cols), jnp.bfloat16),
            pltpu.SemaphoreType.DMA((2, 3)),
            pltpu.SemaphoreType.DMA((2, 3)),
            pltpu.SemaphoreType.DMA((2, 3)),
            pltpu.SemaphoreType.DMA((2, 3)),
        ],
        compiler_params=pltpu.CompilerParams(collective_id=cid, has_side_effects=True,
                                             vmem_limit_bytes=64 * 1024 * 1024),
    )(*ins)


def gelu_grad(value):
    cdf = 0.5 * (1.0 + jax.scipy.special.erf(value * 0.7071067811865476))
    pdf = jnp.exp(-0.5 * value * value) * 0.3989422804014327
    return cdf + value * pdf


def token_panel(local_rows):
    return lax.all_gather(local_rows, "row", axis=0, tiled=True)


def token_panel_a2a(local_rows):
    n = lax.axis_size("row")
    copies = jnp.broadcast_to(local_rows[None], (n,) + local_rows.shape)
    copies = copies.reshape(n * local_rows.shape[0], local_rows.shape[1])
    return lax.all_to_all(copies, "row", split_axis=0, concat_axis=0, tiled=True)


def hidden_panel(local_rows):
    return lax.all_gather(local_rows, "col", axis=0, tiled=True)


def contract_last(left, right):
    return lax.dot_general(
        left, right, (((1,), (1,)), ((), ())), preferred_element_type=jnp.float32
    )


def width_split(left_all, right, transposed):
    if transposed:
        term = contract_last(left_all, right)
    else:
        term = jnp.dot(left_all, right, preferred_element_type=jnp.float32)
    return lax.psum_scatter(
        term.astype(jnp.bfloat16), "col", scatter_dimension=0, tiled=True
    ).astype(jnp.float32)


def unit_sum(left_all, right, transposed):
    n = lax.axis_size("row")
    if transposed:
        term = contract_last(left_all, right)
    else:
        term = jnp.dot(left_all, right, preferred_element_type=jnp.float32)
    pieces = term.astype(jnp.bfloat16).reshape(n, term.shape[0] // n, term.shape[1])
    pieces = lax.all_to_all(pieces, "row", split_axis=0, concat_axis=0, tiled=True)
    return jnp.sum(pieces.astype(jnp.float32), axis=0)


def row_sum(term):
    n = lax.axis_size("row")
    pieces = term.reshape(n, term.shape[0] // n, term.shape[1])
    pieces = lax.all_to_all(pieces, "row", split_axis=0, concat_axis=0, tiled=True)
    return jnp.sum(pieces.astype(jnp.float32), axis=0)


def local(tokens, w_in, w_out, cotangent):
    tokens_all, upstream_all, pre_term, dact_term = row_all_gather(tokens, cotangent, w_in, w_out, 3)
    pre_part, dact_part = col_reduce_scatter([pre_term, dact_term], 1)
    act = jax.nn.gelu(pre_part, approximate=False).astype(jnp.bfloat16)
    dpre = (dact_part * gelu_grad(pre_part)).astype(jnp.bfloat16)
    (act_all, dpre_all), (mixed_term, back_term) = col_all_gather([act, dpre], [w_out, w_in.T], 2)
    mixed, back = row_reduce_scatter(mixed_term, back_term, 4)
    block_rows = (tokens.astype(jnp.float32) + mixed).astype(jnp.bfloat16)
    block_out = lax.all_to_all(block_rows, "col", split_axis=0, concat_axis=1, tiled=True)
    grad_out = lax.dot_general(
        act_all, upstream_all, (((0,), (0,)), ((), ())), preferred_element_type=jnp.float32
    )
    grad_in = lax.dot_general(
        tokens_all, dpre_all, (((0,), (0,)), ((), ())), preferred_element_type=jnp.float32
    )
    grad_tokens = (cotangent.astype(jnp.float32) + back).astype(jnp.bfloat16)
    return (block_out, grad_tokens, grad_in, grad_out)


def solution(mesh):
    in_specs = (P("row", "col"), P("col", "row"), P("row", "col"), P("row", "col"))
    out_specs = (P(("row", "col"), None), P("row", "col"), P("col", "row"), P("row", "col"))
    return jax.shard_map(local, mesh=mesh, in_specs=in_specs, out_specs=out_specs, check_vma=False)
```

```python
import jax
import jax.numpy as jnp
from jax import lax
from jax.sharding import PartitionSpec as P
import functools
from jax.experimental import pallas as pl
from jax.experimental.pallas import tpu as pltpu

MESH = pl.DeviceIdType.MESH


def _col_ids(nx):
    me = lax.axis_index("col")
    x = me // 2
    k = me % 2
    d = 1 - 2 * k
    nxt = lax.rem(x + nx + d, nx)
    prv = lax.rem(x + nx - d, nx)
    return x, k, d, nxt, prv


def _greet(row, k, x, nxt, prv):
    barrier = pltpu.get_barrier_semaphore()
    for peer in (2 * x + 1 - k, 2 * nxt + k, 2 * prv + k):
        pl.semaphore_signal(barrier, inc=1, device_id=(row, peer), device_id_type=MESH)
    pl.semaphore_wait(barrier, 3)


def _rs_kernel(nx, narr, *refs):
    parts = refs[:narr]
    outs = refs[narr:2 * narr]
    recv1, sendbuf, recv2, s1, r1, s2, r2 = refs[2 * narr:]
    row = lax.axis_index("row")
    x, k, d, nxt, prv = _col_ids(nx)
    _greet(row, k, x, nxt, prv)
    partner = (row, 2 * x + 1 - k)
    nextdev = (row, 2 * nxt + k)

    def order(j, sign):
        if j == nx - 1:
            return x
        return lax.rem(x + 4 * nx + sign * d * (j + 1), nx)

    first = []
    for j in range(nx):
        for a in range(narr):
            cp = pltpu.make_async_remote_copy(
                src_ref=parts[a].at[2 * order(j, 1) + 1 - k], dst_ref=recv1.at[a, j],
                send_sem=s1.at[a, j], recv_sem=r1.at[a, j],
                device_id=partner, device_id_type=MESH)
            cp.start()
            first.append(cp)

    def chip_sum(a, j):
        first[j * narr + a].wait_recv()
        own = parts[a][2 * order(j, -1) + k].astype(jnp.float32)
        return own + recv1[a, j].astype(jnp.float32)

    ring = []
    for step in range(nx - 1):
        for a in range(narr):
            value = chip_sum(a, step)
            if step == 0:
                sendbuf[a, step] = value.astype(sendbuf.dtype)
            else:
                ring[(step - 1) * narr + a].wait_recv()
                sendbuf[a, step] = (recv2[a, step - 1].astype(jnp.float32) + value).astype(sendbuf.dtype)
            cp = pltpu.make_async_remote_copy(
                src_ref=sendbuf.at[a, step], dst_ref=recv2.at[a, step],
                send_sem=s2.at[a, step], recv_sem=r2.at[a, step],
                device_id=nextdev, device_id_type=MESH)
            cp.start()
            ring.append(cp)
    for a in range(narr):
        value = chip_sum(a, nx - 1)
        ring[(nx - 2) * narr + a].wait_recv()
        outs[a][...] = recv2[a, nx - 2].astype(jnp.float32) + value
    for cp in first:
        cp.wait_send()
    for cp in ring:
        cp.wait_send()


def col_reduce_scatter(arrays, cid):
    n = lax.axis_size("col")
    nx = n // 2
    narr = len(arrays)
    rows = arrays[0].shape[0] // n
    cols = arrays[0].shape[1]
    parts = [a.reshape(n, rows, cols) for a in arrays]
    return pl.pallas_call(
        functools.partial(_rs_kernel, nx, narr),
        out_shape=[jax.ShapeDtypeStruct((rows, cols), jnp.float32)] * narr,
        in_specs=[pl.BlockSpec(memory_space=pltpu.VMEM)] * narr,
        out_specs=[pl.BlockSpec(memory_space=pltpu.VMEM)] * narr,
        scratch_shapes=[
            pltpu.VMEM((narr, nx, rows, cols), jnp.bfloat16),
            pltpu.VMEM((narr, nx - 1, rows, cols), jnp.bfloat16),
            pltpu.VMEM((narr, nx - 1, rows, cols), jnp.bfloat16),
            pltpu.SemaphoreType.DMA((narr, nx)),
            pltpu.SemaphoreType.DMA((narr, nx)),
            pltpu.SemaphoreType.DMA((narr, nx - 1)),
            pltpu.SemaphoreType.DMA((narr, nx - 1)),
        ],
        compiler_params=pltpu.CompilerParams(collective_id=cid, has_side_effects=True,
                                             vmem_limit_bytes=64 * 1024 * 1024),
    )(*parts)


def _ag_kernel(nx, narr, *refs):
    chunks = refs[:narr]
    weights = refs[narr:2 * narr]
    outs = refs[2 * narr:3 * narr]
    prods = refs[3 * narr:4 * narr]
    sr, rr, sc, rc = refs[4 * narr:]
    row = lax.axis_index("row")
    x, k, d, nxt, prv = _col_ids(nx)
    _greet(row, k, x, nxt, prv)
    me = 2 * x + k
    partner = (row, 2 * x + 1 - k)
    nextdev = (row, 2 * nxt + k)

    def product(a, slot):
        prods[a][slot] = jnp.dot(outs[a][slot], weights[a][...],
                                 preferred_element_type=jnp.float32).astype(prods[a].dtype)

    for a in range(narr):
        outs[a][me] = chunks[a][...]
    ring, core = [], []
    for step in range(nx):
        for a in range(narr):
            src_x = lax.rem(x + 4 * nx - d * step, nx)
            slot = 2 * src_x + k
            if step > 0:
                ring[(step - 1) * narr + a].wait_recv()
            src = chunks[a] if step == 0 else outs[a].at[slot]
            if step < nx - 1:
                cp = pltpu.make_async_remote_copy(
                    src_ref=src, dst_ref=outs[a].at[slot],
                    send_sem=sr.at[a, step], recv_sem=rr.at[a, step],
                    device_id=nextdev, device_id_type=MESH)
                cp.start()
                ring.append(cp)
            cc = pltpu.make_async_remote_copy(
                src_ref=src, dst_ref=outs[a].at[slot],
                send_sem=sc.at[a, step], recv_sem=rc.at[a, step],
                device_id=partner, device_id_type=MESH)
            cc.start()
            core.append(cc)
        for a in range(narr):
            product(a, 2 * lax.rem(x + 4 * nx - d * step, nx) + k)
        if step > 0:
            for a in range(narr):
                core[(step - 1) * narr + a].wait()
            for a in range(narr):
                product(a, 2 * lax.rem(x + 4 * nx + d * (step - 1), nx) + 1 - k)
    for cp in ring:
        cp.wait_send()
    for a in range(narr):
        core[(nx - 1) * narr + a].wait()
    for a in range(narr):
        product(a, 2 * lax.rem(x + 4 * nx + d * (nx - 1), nx) + 1 - k)


def col_all_gather(arrays, weights, cid):
    n = lax.axis_size("col")
    nx = n // 2
    narr = len(arrays)
    rows, cols = arrays[0].shape
    width = weights[0].shape[1]
    res = pl.pallas_call(
        functools.partial(_ag_kernel, nx, narr),
        out_shape=[jax.ShapeDtypeStruct((n, rows, cols), arrays[0].dtype)] * narr
        + [jax.ShapeDtypeStruct((n, rows, width), jnp.bfloat16)] * narr,
        in_specs=[pl.BlockSpec(memory_space=pltpu.VMEM)] * (2 * narr),
        out_specs=[pl.BlockSpec(memory_space=pltpu.VMEM)] * (2 * narr),
        scratch_shapes=[
            pltpu.SemaphoreType.DMA((narr, nx)),
            pltpu.SemaphoreType.DMA((narr, nx)),
            pltpu.SemaphoreType.DMA((narr, nx)),
            pltpu.SemaphoreType.DMA((narr, nx)),
        ],
        compiler_params=pltpu.CompilerParams(collective_id=cid, has_side_effects=True,
                                             vmem_limit_bytes=64 * 1024 * 1024),
    )(*arrays, *weights)
    gathered = [o.reshape(n * rows, cols) for o in res[:narr]]
    products = [o.reshape(n * rows, width) for o in res[narr:]]
    return gathered, products


def _row_ids():
    me = lax.axis_index("row")
    y = me // 4
    z = me % 4
    k = lax.axis_index("col") % 2
    d = 1 - 2 * k
    return y, z, d


def _row_ag_kernel(ny, *refs):
    ins = refs[:2]
    weights = refs[2:4]
    outs = refs[4:6]
    terms = refs[6:8]
    sa, sb, rsem = refs[8:]

    def product(a, slot):
        if a == 0:
            value = jnp.dot(outs[a][slot], weights[a][...], preferred_element_type=jnp.float32)
        else:
            value = lax.dot_general(outs[a][slot], weights[a][...], (((1,), (1,)), ((), ())),
                                    preferred_element_type=jnp.float32)
        terms[a][slot] = value.astype(terms[a].dtype)

    col = lax.axis_index("col")
    y, z, d = _row_ids()
    me = y * 4 + z
    barrier = pltpu.get_barrier_semaphore()
    peers = (y * 4 + lax.rem(z + 4 + d, 4), y * 4 + lax.rem(z + 4 - d, 4),
             lax.rem(y + ny + d, ny) * 4 + z, lax.rem(y + ny - d, ny) * 4 + z)
    for p in peers:
        pl.semaphore_signal(barrier, inc=1, device_id=(p, col), device_id_type=MESH)
    pl.semaphore_wait(barrier, 4)
    geo = []
    for a in range(2):
        if a == 0:
            na, nb = 4, ny
            pos_a, pos_b = z, y
            slot_of = lambda pa, pb: pb * 4 + pa
        else:
            na, nb = ny, 4
            pos_a, pos_b = y, z
            slot_of = lambda pa, pb: pa * 4 + pb
        geo.append((na, nb, pos_a, pos_b, slot_of))
        outs[a][me] = ins[a][...]

    def dev(a, pa, pb):
        return (geo[a][4](pa, pb), col)

    def send(a, src, slot, target, sem):
        cp = pltpu.make_async_remote_copy(
            src_ref=src, dst_ref=outs[a].at[slot], send_sem=sem, recv_sem=rsem.at[a, slot],
            device_id=target, device_id_type=MESH)
        cp.start()
        return cp

    def wait_in(a, slot):
        pltpu.make_async_remote_copy(
            src_ref=ins[a], dst_ref=outs[a].at[slot], send_sem=sa.at[a, 0], recv_sem=rsem.at[a, slot],
            device_id=(peers[0], col), device_id_type=MESH).wait_recv()

    sends = []
    for a in range(2):
        na, nb, pa, pb, slot_of = geo[a]
        next_a = dev(a, lax.rem(pa + na + d, na), pb)
        next_b = dev(a, pa, lax.rem(pb + nb + d, nb))
        sends.append(send(a, ins[a], me, next_a, sa.at[a, 0]))
        sends.append(send(a, ins[a], me, next_b, sb.at[a, 0, 0]))
    for a in range(2):
        product(a, me)
    for s in range(1, 4):
        for a in range(2):
            na, nb, pa, pb, slot_of = geo[a]
            next_a = dev(a, lax.rem(pa + na + d, na), pb)
            next_b = dev(a, pa, lax.rem(pb + nb + d, nb))
            slot = slot_of(lax.rem(pa + 4 * na - d * s, na), pb)
            wait_in(a, slot)
            if s < na - 1:
                sends.append(send(a, outs[a].at[slot], slot, next_a, sa.at[a, s]))
            sends.append(send(a, outs[a].at[slot], slot, next_b, sb.at[a, 0, s]))
            product(a, slot)
    for t in range(1, 4):
        for j in range(4):
            for a in range(2):
                na, nb, pa, pb, slot_of = geo[a]
                next_b = dev(a, pa, lax.rem(pb + nb + d, nb))
                slot = slot_of(lax.rem(pa + 4 * na - d * j, na), lax.rem(pb + 4 * nb - d * t, nb))
                wait_in(a, slot)
                if t < nb - 1:
                    sends.append(send(a, outs[a].at[slot], slot, next_b, sb.at[a, t, j]))
                product(a, slot)
    for cp in sends:
        cp.wait_send()


def row_all_gather(first, second, w_first, w_second, cid):
    n = lax.axis_size("row")
    ny = n // 4
    rows, cols = first.shape
    width = w_first.shape[1]
    outs = pl.pallas_call(
        functools.partial(_row_ag_kernel, ny),
        out_shape=[jax.ShapeDtypeStruct((n, rows, cols), first.dtype)] * 2
        + [jax.ShapeDtypeStruct((n, rows, width), jnp.bfloat16)] * 2,
        in_specs=[pl.BlockSpec(memory_space=pltpu.VMEM)] * 4,
        out_specs=[pl.BlockSpec(memory_space=pltpu.VMEM)] * 4,
        scratch_shapes=[
            pltpu.SemaphoreType.DMA((2, 4)),
            pltpu.SemaphoreType.DMA((2, 4, 4)),
            pltpu.SemaphoreType.DMA((2, n)),
        ],
        compiler_params=pltpu.CompilerParams(collective_id=cid, has_side_effects=True,
                                             vmem_limit_bytes=64 * 1024 * 1024),
    )(first, second, w_first, w_second)
    return [o.reshape(n * rows, o.shape[2]) for o in outs]


def _row_rs_kernel(ny, *refs):
    ins = refs[:2]
    outs = refs[2:4]
    sb1, rb1, ssum, sb2, rb2, s1, r1, s2, r2 = refs[4:]
    col = lax.axis_index("col")
    y, z, d = _row_ids()
    barrier = pltpu.get_barrier_semaphore()
    peers = (y * 4 + lax.rem(z + 4 + d, 4), y * 4 + lax.rem(z + 4 - d, 4),
             lax.rem(y + ny + d, ny) * 4 + z, lax.rem(y + ny - d, ny) * 4 + z)
    for p in peers:
        pl.semaphore_signal(barrier, inc=1, device_id=(p, col), device_id_type=MESH)
    pl.semaphore_wait(barrier, 4)
    geo = [(4, ny, z, y, lambda pa, pb: pb * 4 + pa), (ny, 4, y, z, lambda pa, pb: pa * 4 + pb)]

    def dev(a, pa, pb):
        return (geo[a][4](pa, pb), col)

    def send(src, dst, ssem, rsem, target):
        cp = pltpu.make_async_remote_copy(src_ref=src, dst_ref=dst, send_sem=ssem, recv_sem=rsem,
                                          device_id=target, device_id_type=MESH)
        cp.start()
        return cp

    sends = []
    first = [[] for _ in range(2)]
    for s in range(4 - 1):
        for a in range(2):
            na, nb, pa, pb, slot_of = geo[a]
            pos = lax.rem(pa + 4 * na - d * (s + 1), na)
            for bq in range(nb):
                own = ins[a][slot_of(pos, bq)]
                if s == 0:
                    sb1[a, s, bq] = own
                else:
                    sb1[a, s, bq] = (rb1[a, s - 1, bq].astype(jnp.float32) + own.astype(jnp.float32)).astype(sb1.dtype)
            cp = send(sb1.at[a, s], rb1.at[a, s], s1.at[a, s], r1.at[a, s],
                      dev(a, lax.rem(pa + na + d, na), pb))
            sends.append(cp)
            first[a].append(cp)
        for a in range(2):
            first[a][s].wait_recv()
    for a in range(2):
        na, nb, pa, pb, slot_of = geo[a]
        for bq in range(nb):
            ssum[a, bq] = rb1[a, 2, bq].astype(jnp.float32) + ins[a][slot_of(pa, bq)].astype(jnp.float32)
    second = [[] for _ in range(2)]
    for t in range(4 - 1):
        for a in range(2):
            na, nb, pa, pb, slot_of = geo[a]
            pos = lax.rem(pb + 4 * nb - d * (t + 1), nb)
            if t == 0:
                sb2[a, t] = ssum[a, pos].astype(sb2.dtype)
            else:
                sb2[a, t] = (rb2[a, t - 1].astype(jnp.float32) + ssum[a, pos]).astype(sb2.dtype)
            cp = send(sb2.at[a, t], rb2.at[a, t], s2.at[a, t], r2.at[a, t],
                      dev(a, pa, lax.rem(pb + nb + d, nb)))
            sends.append(cp)
            second[a].append(cp)
        for a in range(2):
            second[a][t].wait_recv()
    for a in range(2):
        na, nb, pa, pb, slot_of = geo[a]
        outs[a][...] = rb2[a, 2].astype(jnp.float32) + ssum[a, pb]
    for cp in sends:
        cp.wait_send()


def row_reduce_scatter(first, second, cid):
    n = lax.axis_size("row")
    ny = n // 4
    rows, cols = first.shape[0] // n, first.shape[1]
    ins = [v.reshape(n, rows, cols) for v in (first, second)]
    return pl.pallas_call(
        functools.partial(_row_rs_kernel, ny),
        out_shape=[jax.ShapeDtypeStruct((rows, cols), jnp.float32)] * 2,
        in_specs=[pl.BlockSpec(memory_space=pltpu.VMEM)] * 2,
        out_specs=[pl.BlockSpec(memory_space=pltpu.VMEM)] * 2,
        scratch_shapes=[
            pltpu.VMEM((2, 3, 4, rows, cols), jnp.bfloat16),
            pltpu.VMEM((2, 3, 4, rows, cols), jnp.bfloat16),
            pltpu.VMEM((2, 4, rows, cols), jnp.float32),
            pltpu.VMEM((2, 3, rows, cols), jnp.bfloat16),
            pltpu.VMEM((2, 3, rows, cols), jnp.bfloat16),
            pltpu.SemaphoreType.DMA((2, 3)),
            pltpu.SemaphoreType.DMA((2, 3)),
            pltpu.SemaphoreType.DMA((2, 3)),
            pltpu.SemaphoreType.DMA((2, 3)),
        ],
        compiler_params=pltpu.CompilerParams(collective_id=cid, has_side_effects=True,
                                             vmem_limit_bytes=64 * 1024 * 1024),
    )(*ins)


def gelu_grad(value):
    cdf = 0.5 * (1.0 + jax.scipy.special.erf(value * 0.7071067811865476))
    pdf = jnp.exp(-0.5 * value * value) * 0.3989422804014327
    return cdf + value * pdf


def token_panel(local_rows):
    return lax.all_gather(local_rows, "row", axis=0, tiled=True)


def token_panel_a2a(local_rows):
    n = lax.axis_size("row")
    copies = jnp.broadcast_to(local_rows[None], (n,) + local_rows.shape)
    copies = copies.reshape(n * local_rows.shape[0], local_rows.shape[1])
    return lax.all_to_all(copies, "row", split_axis=0, concat_axis=0, tiled=True)


def hidden_panel(local_rows):
    return lax.all_gather(local_rows, "col", axis=0, tiled=True)


def contract_last(left, right):
    return lax.dot_general(
        left, right, (((1,), (1,)), ((), ())), preferred_element_type=jnp.float32
    )


def width_split(left_all, right, transposed):
    if transposed:
        term = contract_last(left_all, right)
    else:
        term = jnp.dot(left_all, right, preferred_element_type=jnp.float32)
    return lax.psum_scatter(
        term.astype(jnp.bfloat16), "col", scatter_dimension=0, tiled=True
    ).astype(jnp.float32)


def unit_sum(left_all, right, transposed):
    n = lax.axis_size("row")
    if transposed:
        term = contract_last(left_all, right)
    else:
        term = jnp.dot(left_all, right, preferred_element_type=jnp.float32)
    pieces = term.astype(jnp.bfloat16).reshape(n, term.shape[0] // n, term.shape[1])
    pieces = lax.all_to_all(pieces, "row", split_axis=0, concat_axis=0, tiled=True)
    return jnp.sum(pieces.astype(jnp.float32), axis=0)


def row_sum(term):
    n = lax.axis_size("row")
    pieces = term.reshape(n, term.shape[0] // n, term.shape[1])
    pieces = lax.all_to_all(pieces, "row", split_axis=0, concat_axis=0, tiled=True)
    return jnp.sum(pieces.astype(jnp.float32), axis=0)


def local(tokens, w_in, w_out, cotangent):
    tokens_all, upstream_all, pre_term, dact_term = row_all_gather(tokens, cotangent, w_in, w_out, 3)
    pre_part, dact_part = col_reduce_scatter([pre_term, dact_term], 1)
    act = jax.nn.gelu(pre_part, approximate=False).astype(jnp.bfloat16)
    dpre = (dact_part * gelu_grad(pre_part)).astype(jnp.bfloat16)
    (act_all, dpre_all), (mixed_term, back_term) = col_all_gather([act, dpre], [w_out, w_in.T], 2)
    mixed, back = row_reduce_scatter(mixed_term, back_term, 4)
    block_rows = (tokens.astype(jnp.float32) + mixed).astype(jnp.bfloat16)
    block_out = lax.all_to_all(block_rows, "col", split_axis=0, concat_axis=1, tiled=True)
    grad_out = lax.dot_general(
        act_all, upstream_all, (((0,), (0,)), ((), ())), preferred_element_type=jnp.float32
    )
    grad_in = lax.dot_general(
        tokens_all, dpre_all, (((0,), (0,)), ((), ())), preferred_element_type=jnp.float32
    )
    grad_tokens = (cotangent.astype(jnp.float32) + back).astype(jnp.bfloat16)
    return (block_out, grad_tokens, grad_in, grad_out)


def solution(mesh):
    in_specs = (P("row", "col"), P("col", "row"), P("row", "col"), P("row", "col"))
    out_specs = (P(("row", "col"), None), P("row", "col"), P("col", "row"), P("row", "col"))
    return jax.shard_map(local, mesh=mesh, in_specs=in_specs, out_specs=out_specs, check_vma=False)
```

```python
import jax
import jax.numpy as jnp
from jax import lax
from jax.sharding import PartitionSpec as P
import functools
from jax.experimental import pallas as pl
from jax.experimental.pallas import tpu as pltpu

MESH = pl.DeviceIdType.MESH


def _col_ids(nx):
    me = lax.axis_index("col")
    x = me // 2
    k = me % 2
    d = 1 - 2 * k
    nxt = lax.rem(x + nx + d, nx)
    prv = lax.rem(x + nx - d, nx)
    return x, k, d, nxt, prv


def _greet(row, k, x, nxt, prv):
    barrier = pltpu.get_barrier_semaphore()
    for peer in (2 * x + 1 - k, 2 * nxt + k, 2 * prv + k):
        pl.semaphore_signal(barrier, inc=1, device_id=(row, peer), device_id_type=MESH)
    pl.semaphore_wait(barrier, 3)


def _rs_kernel(nx, narr, *refs):
    parts = refs[:narr]
    outs = refs[narr:2 * narr]
    recv1, sendbuf, recv2, s1, r1, s2, r2 = refs[2 * narr:]
    row = lax.axis_index("row")
    x, k, d, nxt, prv = _col_ids(nx)
    _greet(row, k, x, nxt, prv)
    partner = (row, 2 * x + 1 - k)
    nextdev = (row, 2 * nxt + k)

    def order(j, sign):
        if j == nx - 1:
            return x
        return lax.rem(x + 4 * nx + sign * d * (j + 1), nx)

    first = []
    for j in range(nx):
        for a in range(narr):
            cp = pltpu.make_async_remote_copy(
                src_ref=parts[a].at[2 * order(j, 1) + 1 - k], dst_ref=recv1.at[a, j],
                send_sem=s1.at[a, j], recv_sem=r1.at[a, j],
                device_id=partner, device_id_type=MESH)
            cp.start()
            first.append(cp)

    def chip_sum(a, j):
        first[j * narr + a].wait_recv()
        own = parts[a][2 * order(j, -1) + k].astype(jnp.float32)
        return own + recv1[a, j].astype(jnp.float32)

    ring = []
    for step in range(nx - 1):
        for a in range(narr):
            value = chip_sum(a, step)
            if step == 0:
                sendbuf[a, step] = value.astype(sendbuf.dtype)
            else:
                ring[(step - 1) * narr + a].wait_recv()
                sendbuf[a, step] = (recv2[a, step - 1].astype(jnp.float32) + value).astype(sendbuf.dtype)
            cp = pltpu.make_async_remote_copy(
                src_ref=sendbuf.at[a, step], dst_ref=recv2.at[a, step],
                send_sem=s2.at[a, step], recv_sem=r2.at[a, step],
                device_id=nextdev, device_id_type=MESH)
            cp.start()
            ring.append(cp)
    for a in range(narr):
        value = chip_sum(a, nx - 1)
        ring[(nx - 2) * narr + a].wait_recv()
        outs[a][...] = recv2[a, nx - 2].astype(jnp.float32) + value
    for cp in first:
        cp.wait_send()
    for cp in ring:
        cp.wait_send()


def col_reduce_scatter(arrays, cid):
    n = lax.axis_size("col")
    nx = n // 2
    narr = len(arrays)
    rows = arrays[0].shape[0] // n
    cols = arrays[0].shape[1]
    parts = [a.reshape(n, rows, cols) for a in arrays]
    return pl.pallas_call(
        functools.partial(_rs_kernel, nx, narr),
        out_shape=[jax.ShapeDtypeStruct((rows, cols), jnp.float32)] * narr,
        in_specs=[pl.BlockSpec(memory_space=pltpu.VMEM)] * narr,
        out_specs=[pl.BlockSpec(memory_space=pltpu.VMEM)] * narr,
        scratch_shapes=[
            pltpu.VMEM((narr, nx, rows, cols), jnp.bfloat16),
            pltpu.VMEM((narr, nx - 1, rows, cols), jnp.bfloat16),
            pltpu.VMEM((narr, nx - 1, rows, cols), jnp.bfloat16),
            pltpu.SemaphoreType.DMA((narr, nx)),
            pltpu.SemaphoreType.DMA((narr, nx)),
            pltpu.SemaphoreType.DMA((narr, nx - 1)),
            pltpu.SemaphoreType.DMA((narr, nx - 1)),
        ],
        compiler_params=pltpu.CompilerParams(collective_id=cid, has_side_effects=True,
                                             vmem_limit_bytes=64 * 1024 * 1024),
    )(*parts)


def _ag_kernel(nx, narr, *refs):
    chunks = refs[:narr]
    weights = refs[narr:2 * narr]
    outs = refs[2 * narr:3 * narr]
    prods = refs[3 * narr:4 * narr]
    sr, rr, sc, rc = refs[4 * narr:]
    row = lax.axis_index("row")
    x, k, d, nxt, prv = _col_ids(nx)
    _greet(row, k, x, nxt, prv)
    me = 2 * x + k
    partner = (row, 2 * x + 1 - k)
    nextdev = (row, 2 * nxt + k)

    def product(a, slot):
        prods[a][slot] = jnp.dot(outs[a][slot], weights[a][...],
                                 preferred_element_type=jnp.float32).astype(prods[a].dtype)

    for a in range(narr):
        outs[a][me] = chunks[a][...]
    ring, core = [], []
    for step in range(nx):
        for a in range(narr):
            src_x = lax.rem(x + 4 * nx - d * step, nx)
            slot = 2 * src_x + k
            if step > 0:
                ring[(step - 1) * narr + a].wait_recv()
            src = chunks[a] if step == 0 else outs[a].at[slot]
            if step < nx - 1:
                cp = pltpu.make_async_remote_copy(
                    src_ref=src, dst_ref=outs[a].at[slot],
                    send_sem=sr.at[a, step], recv_sem=rr.at[a, step],
                    device_id=nextdev, device_id_type=MESH)
                cp.start()
                ring.append(cp)
            cc = pltpu.make_async_remote_copy(
                src_ref=src, dst_ref=outs[a].at[slot],
                send_sem=sc.at[a, step], recv_sem=rc.at[a, step],
                device_id=partner, device_id_type=MESH)
            cc.start()
            core.append(cc)
        for a in range(narr):
            product(a, 2 * lax.rem(x + 4 * nx - d * step, nx) + k)
        if step > 0:
            for a in range(narr):
                core[(step - 1) * narr + a].wait()
            for a in range(narr):
                product(a, 2 * lax.rem(x + 4 * nx + d * (step - 1), nx) + 1 - k)
    for cp in ring:
        cp.wait_send()
    for a in range(narr):
        core[(nx - 1) * narr + a].wait()
    for a in range(narr):
        product(a, 2 * lax.rem(x + 4 * nx + d * (nx - 1), nx) + 1 - k)


def col_all_gather(arrays, weights, cid):
    n = lax.axis_size("col")
    nx = n // 2
    narr = len(arrays)
    rows, cols = arrays[0].shape
    width = weights[0].shape[1]
    res = pl.pallas_call(
        functools.partial(_ag_kernel, nx, narr),
        out_shape=[jax.ShapeDtypeStruct((n, rows, cols), arrays[0].dtype)] * narr
        + [jax.ShapeDtypeStruct((n, rows, width), jnp.bfloat16)] * narr,
        in_specs=[pl.BlockSpec(memory_space=pltpu.VMEM)] * (2 * narr),
        out_specs=[pl.BlockSpec(memory_space=pltpu.VMEM)] * (2 * narr),
        scratch_shapes=[
            pltpu.SemaphoreType.DMA((narr, nx)),
            pltpu.SemaphoreType.DMA((narr, nx)),
            pltpu.SemaphoreType.DMA((narr, nx)),
            pltpu.SemaphoreType.DMA((narr, nx)),
        ],
        compiler_params=pltpu.CompilerParams(collective_id=cid, has_side_effects=True,
                                             vmem_limit_bytes=64 * 1024 * 1024),
    )(*arrays, *weights)
    gathered = [o.reshape(n * rows, cols) for o in res[:narr]]
    products = [o.reshape(n * rows, width) for o in res[narr:]]
    return gathered, products


def _row_ids():
    me = lax.axis_index("row")
    y = me // 4
    z = me % 4
    k = lax.axis_index("col") % 2
    d = 1 - 2 * k
    return y, z, d


def _row_ag_kernel(ny, *refs):
    ins = refs[:2]
    weights = refs[2:4]
    outs = refs[4:6]
    terms = refs[6:8]
    sa, sb, rsem = refs[8:]

    def product(a, slot):
        if a == 0:
            value = jnp.dot(outs[a][slot], weights[a][...], preferred_element_type=jnp.float32)
        else:
            value = lax.dot_general(outs[a][slot], weights[a][...], (((1,), (1,)), ((), ())),
                                    preferred_element_type=jnp.float32)
        terms[a][slot] = value.astype(terms[a].dtype)

    col = lax.axis_index("col")
    y, z, d = _row_ids()
    me = y * 4 + z
    barrier = pltpu.get_barrier_semaphore()
    peers = (y * 4 + lax.rem(z + 4 + d, 4), y * 4 + lax.rem(z + 4 - d, 4),
             lax.rem(y + ny + d, ny) * 4 + z, lax.rem(y + ny - d, ny) * 4 + z)
    for p in peers:
        pl.semaphore_signal(barrier, inc=1, device_id=(p, col), device_id_type=MESH)
    pl.semaphore_wait(barrier, 4)
    geo = []
    for a in range(2):
        if a == 0:
            na, nb = 4, ny
            pos_a, pos_b = z, y
            slot_of = lambda pa, pb: pb * 4 + pa
        else:
            na, nb = ny, 4
            pos_a, pos_b = y, z
            slot_of = lambda pa, pb: pa * 4 + pb
        geo.append((na, nb, pos_a, pos_b, slot_of))
        outs[a][me] = ins[a][...]

    def dev(a, pa, pb):
        return (geo[a][4](pa, pb), col)

    def send(a, src, slot, target, sem):
        cp = pltpu.make_async_remote_copy(
            src_ref=src, dst_ref=outs[a].at[slot], send_sem=sem, recv_sem=rsem.at[a, slot],
            device_id=target, device_id_type=MESH)
        cp.start()
        return cp

    def wait_in(a, slot):
        pltpu.make_async_remote_copy(
            src_ref=ins[a], dst_ref=outs[a].at[slot], send_sem=sa.at[a, 0], recv_sem=rsem.at[a, slot],
            device_id=(peers[0], col), device_id_type=MESH).wait_recv()

    sends = []
    for a in range(2):
        na, nb, pa, pb, slot_of = geo[a]
        next_a = dev(a, lax.rem(pa + na + d, na), pb)
        next_b = dev(a, pa, lax.rem(pb + nb + d, nb))
        sends.append(send(a, ins[a], me, next_a, sa.at[a, 0]))
        sends.append(send(a, ins[a], me, next_b, sb.at[a, 0, 0]))
    for a in range(2):
        product(a, me)
    for s in range(1, 4):
        for a in range(2):
            na, nb, pa, pb, slot_of = geo[a]
            next_a = dev(a, lax.rem(pa + na + d, na), pb)
            next_b = dev(a, pa, lax.rem(pb + nb + d, nb))
            slot = slot_of(lax.rem(pa + 4 * na - d * s, na), pb)
            wait_in(a, slot)
            if s < na - 1:
                sends.append(send(a, outs[a].at[slot], slot, next_a, sa.at[a, s]))
            sends.append(send(a, outs[a].at[slot], slot, next_b, sb.at[a, 0, s]))
            product(a, slot)
    for t in range(1, 4):
        for j in range(4):
            for a in range(2):
                na, nb, pa, pb, slot_of = geo[a]
                next_b = dev(a, pa, lax.rem(pb + nb + d, nb))
                slot = slot_of(lax.rem(pa + 4 * na - d * j, na), lax.rem(pb + 4 * nb - d * t, nb))
                wait_in(a, slot)
                if t < nb - 1:
                    sends.append(send(a, outs[a].at[slot], slot, next_b, sb.at[a, t, j]))
                product(a, slot)
    for cp in sends:
        cp.wait_send()


def row_all_gather(first, second, w_first, w_second, cid):
    n = lax.axis_size("row")
    ny = n // 4
    rows, cols = first.shape
    width = w_first.shape[1]
    outs = pl.pallas_call(
        functools.partial(_row_ag_kernel, ny),
        out_shape=[jax.ShapeDtypeStruct((n, rows, cols), first.dtype)] * 2
        + [jax.ShapeDtypeStruct((n, rows, width), jnp.bfloat16)] * 2,
        in_specs=[pl.BlockSpec(memory_space=pltpu.VMEM)] * 4,
        out_specs=[pl.BlockSpec(memory_space=pltpu.VMEM)] * 4,
        scratch_shapes=[
            pltpu.SemaphoreType.DMA((2, 4)),
            pltpu.SemaphoreType.DMA((2, 4, 4)),
            pltpu.SemaphoreType.DMA((2, n)),
        ],
        compiler_params=pltpu.CompilerParams(collective_id=cid, has_side_effects=True,
                                             vmem_limit_bytes=64 * 1024 * 1024),
    )(first, second, w_first, w_second)
    return [o.reshape(n * rows, o.shape[2]) for o in outs]


def _row_rs_kernel(ny, *refs):
    ins = refs[:2]
    outs = refs[2:4]
    sb1, rb1, ssum, sb2, rb2, s1, r1, s2, r2 = refs[4:]
    col = lax.axis_index("col")
    y, z, d = _row_ids()
    barrier = pltpu.get_barrier_semaphore()
    peers = (y * 4 + lax.rem(z + 4 + d, 4), y * 4 + lax.rem(z + 4 - d, 4),
             lax.rem(y + ny + d, ny) * 4 + z, lax.rem(y + ny - d, ny) * 4 + z)
    for p in peers:
        pl.semaphore_signal(barrier, inc=1, device_id=(p, col), device_id_type=MESH)
    pl.semaphore_wait(barrier, 4)
    geo = [(4, ny, z, y, lambda pa, pb: pb * 4 + pa), (ny, 4, y, z, lambda pa, pb: pa * 4 + pb)]

    def dev(a, pa, pb):
        return (geo[a][4](pa, pb), col)

    def send(src, dst, ssem, rsem, target):
        cp = pltpu.make_async_remote_copy(src_ref=src, dst_ref=dst, send_sem=ssem, recv_sem=rsem,
                                          device_id=target, device_id_type=MESH)
        cp.start()
        return cp

    sends = []
    first = {}
    for s in range(4 - 1):
        for bq in range(4):
            for a in range(2):
                na, nb, pa, pb, slot_of = geo[a]
                slot = slot_of(lax.rem(pa + 4 * na - d * (s + 1), na), bq)
                if s == 0:
                    src = ins[a].at[slot]
                else:
                    first[(a, s - 1, bq)].wait_recv()
                    sb1[a, s, bq] = (rb1[a, s - 1, bq].astype(jnp.float32)
                                     + ins[a][slot].astype(jnp.float32)).astype(sb1.dtype)
                    src = sb1.at[a, s, bq]
                cp = send(src, rb1.at[a, s, bq], s1.at[a, s, bq], r1.at[a, s, bq],
                          dev(a, lax.rem(pa + na + d, na), pb))
                sends.append(cp)
                first[(a, s, bq)] = cp
    for bq in range(4):
        for a in range(2):
            na, nb, pa, pb, slot_of = geo[a]
            first[(a, 2, bq)].wait_recv()
            ssum[a, bq] = rb1[a, 2, bq].astype(jnp.float32) + ins[a][slot_of(pa, bq)].astype(jnp.float32)
    second = [[] for _ in range(2)]
    for t in range(4 - 1):
        for a in range(2):
            na, nb, pa, pb, slot_of = geo[a]
            pos = lax.rem(pb + 4 * nb - d * (t + 1), nb)
            if t == 0:
                sb2[a, t] = ssum[a, pos].astype(sb2.dtype)
            else:
                sb2[a, t] = (rb2[a, t - 1].astype(jnp.float32) + ssum[a, pos]).astype(sb2.dtype)
            cp = send(sb2.at[a, t], rb2.at[a, t], s2.at[a, t], r2.at[a, t],
                      dev(a, pa, lax.rem(pb + nb + d, nb)))
            sends.append(cp)
            second[a].append(cp)
        for a in range(2):
            second[a][t].wait_recv()
    for a in range(2):
        na, nb, pa, pb, slot_of = geo[a]
        outs[a][...] = rb2[a, 2].astype(jnp.float32) + ssum[a, pb]
    for cp in sends:
        cp.wait_send()


def row_reduce_scatter(first, second, cid):
    n = lax.axis_size("row")
    ny = n // 4
    rows, cols = first.shape[0] // n, first.shape[1]
    ins = [v.reshape(n, rows, cols) for v in (first, second)]
    return pl.pallas_call(
        functools.partial(_row_rs_kernel, ny),
        out_shape=[jax.ShapeDtypeStruct((rows, cols), jnp.float32)] * 2,
        in_specs=[pl.BlockSpec(memory_space=pltpu.VMEM)] * 2,
        out_specs=[pl.BlockSpec(memory_space=pltpu.VMEM)] * 2,
        scratch_shapes=[
            pltpu.VMEM((2, 3, 4, rows, cols), jnp.bfloat16),
            pltpu.VMEM((2, 3, 4, rows, cols), jnp.bfloat16),
            pltpu.VMEM((2, 4, rows, cols), jnp.float32),
            pltpu.VMEM((2, 3, rows, cols), jnp.bfloat16),
            pltpu.VMEM((2, 3, rows, cols), jnp.bfloat16),
            pltpu.SemaphoreType.DMA((2, 3, 4)),
            pltpu.SemaphoreType.DMA((2, 3, 4)),
            pltpu.SemaphoreType.DMA((2, 3)),
            pltpu.SemaphoreType.DMA((2, 3)),
        ],
        compiler_params=pltpu.CompilerParams(collective_id=cid, has_side_effects=True,
                                             vmem_limit_bytes=64 * 1024 * 1024),
    )(*ins)


def gelu_grad(value):
    cdf = 0.5 * (1.0 + jax.scipy.special.erf(value * 0.7071067811865476))
    pdf = jnp.exp(-0.5 * value * value) * 0.3989422804014327
    return cdf + value * pdf


def token_panel(local_rows):
    return lax.all_gather(local_rows, "row", axis=0, tiled=True)


def token_panel_a2a(local_rows):
    n = lax.axis_size("row")
    copies = jnp.broadcast_to(local_rows[None], (n,) + local_rows.shape)
    copies = copies.reshape(n * local_rows.shape[0], local_rows.shape[1])
    return lax.all_to_all(copies, "row", split_axis=0, concat_axis=0, tiled=True)


def hidden_panel(local_rows):
    return lax.all_gather(local_rows, "col", axis=0, tiled=True)


def contract_last(left, right):
    return lax.dot_general(
        left, right, (((1,), (1,)), ((), ())), preferred_element_type=jnp.float32
    )


def width_split(left_all, right, transposed):
    if transposed:
        term = contract_last(left_all, right)
    else:
        term = jnp.dot(left_all, right, preferred_element_type=jnp.float32)
    return lax.psum_scatter(
        term.astype(jnp.bfloat16), "col", scatter_dimension=0, tiled=True
    ).astype(jnp.float32)


def unit_sum(left_all, right, transposed):
    n = lax.axis_size("row")
    if transposed:
        term = contract_last(left_all, right)
    else:
        term = jnp.dot(left_all, right, preferred_element_type=jnp.float32)
    pieces = term.astype(jnp.bfloat16).reshape(n, term.shape[0] // n, term.shape[1])
    pieces = lax.all_to_all(pieces, "row", split_axis=0, concat_axis=0, tiled=True)
    return jnp.sum(pieces.astype(jnp.float32), axis=0)


def row_sum(term):
    n = lax.axis_size("row")
    pieces = term.reshape(n, term.shape[0] // n, term.shape[1])
    pieces = lax.all_to_all(pieces, "row", split_axis=0, concat_axis=0, tiled=True)
    return jnp.sum(pieces.astype(jnp.float32), axis=0)


def local(tokens, w_in, w_out, cotangent):
    tokens_all, upstream_all, pre_term, dact_term = row_all_gather(tokens, cotangent, w_in, w_out, 3)
    pre_part, dact_part = col_reduce_scatter([pre_term, dact_term], 1)
    act = jax.nn.gelu(pre_part, approximate=False).astype(jnp.bfloat16)
    dpre = (dact_part * gelu_grad(pre_part)).astype(jnp.bfloat16)
    (act_all, dpre_all), (mixed_term, back_term) = col_all_gather([act, dpre], [w_out, w_in.T], 2)
    mixed, back = row_reduce_scatter(mixed_term, back_term, 4)
    block_rows = (tokens.astype(jnp.float32) + mixed).astype(jnp.bfloat16)
    block_out = lax.all_to_all(block_rows, "col", split_axis=0, concat_axis=1, tiled=True)
    grad_out = lax.dot_general(
        act_all, upstream_all, (((0,), (0,)), ((), ())), preferred_element_type=jnp.float32
    )
    grad_in = lax.dot_general(
        tokens_all, dpre_all, (((0,), (0,)), ((), ())), preferred_element_type=jnp.float32
    )
    grad_tokens = (cotangent.astype(jnp.float32) + back).astype(jnp.bfloat16)
    return (block_out, grad_tokens, grad_in, grad_out)


def solution(mesh):
    in_specs = (P("row", "col"), P("col", "row"), P("row", "col"), P("row", "col"))
    out_specs = (P(("row", "col"), None), P("row", "col"), P("col", "row"), P("row", "col"))
    return jax.shard_map(local, mesh=mesh, in_specs=in_specs, out_specs=out_specs, check_vma=False)
```

```python
import jax
import jax.numpy as jnp
from jax import lax
from jax.sharding import PartitionSpec as P
import functools
from jax.experimental import pallas as pl
from jax.experimental.pallas import tpu as pltpu

MESH = pl.DeviceIdType.MESH


def _col_ids(nx):
    me = lax.axis_index("col")
    x = me // 2
    k = me % 2
    d = 1 - 2 * k
    nxt = lax.rem(x + nx + d, nx)
    prv = lax.rem(x + nx - d, nx)
    return x, k, d, nxt, prv


def _greet(row, k, x, nxt, prv):
    barrier = pltpu.get_barrier_semaphore()
    for peer in (2 * x + 1 - k, 2 * nxt + k, 2 * prv + k):
        pl.semaphore_signal(barrier, inc=1, device_id=(row, peer), device_id_type=MESH)
    pl.semaphore_wait(barrier, 3)


def _rs_kernel(nx, narr, *refs):
    parts = refs[:narr]
    outs = refs[narr:2 * narr]
    recv1, sendbuf, recv2, s1, r1, s2, r2 = refs[2 * narr:]
    row = lax.axis_index("row")
    x, k, d, nxt, prv = _col_ids(nx)
    _greet(row, k, x, nxt, prv)
    partner = (row, 2 * x + 1 - k)
    nextdev = (row, 2 * nxt + k)

    def order(j, sign):
        if j == nx - 1:
            return x
        return lax.rem(x + 4 * nx + sign * d * (j + 1), nx)

    first = []
    for j in range(nx):
        for a in range(narr):
            cp = pltpu.make_async_remote_copy(
                src_ref=parts[a].at[2 * order(j, 1) + 1 - k], dst_ref=recv1.at[a, j],
                send_sem=s1.at[a, j], recv_sem=r1.at[a, j],
                device_id=partner, device_id_type=MESH)
            cp.start()
            first.append(cp)

    def chip_sum(a, j):
        first[j * narr + a].wait_recv()
        own = parts[a][2 * order(j, -1) + k].astype(jnp.float32)
        return own + recv1[a, j].astype(jnp.float32)

    pieces = 4
    span = outs[0].shape[0] // pieces
    ring = {}
    for step in range(nx - 1):
        for a in range(narr):
            first[step * narr + a].wait_recv()
        for q in range(pieces):
            rows = pl.ds(q * span, span)
            for a in range(narr):
                value = (parts[a][2 * order(step, -1) + k, rows, :].astype(jnp.float32)
                         + recv1[a, step, rows, :].astype(jnp.float32))
                if step == 0:
                    sendbuf[a, step, rows, :] = value.astype(sendbuf.dtype)
                else:
                    ring[(a, step - 1, q)].wait_recv()
                    sendbuf[a, step, rows, :] = (recv2[a, step - 1, rows, :].astype(jnp.float32)
                                                 + value).astype(sendbuf.dtype)
                cp = pltpu.make_async_remote_copy(
                    src_ref=sendbuf.at[a, step, rows], dst_ref=recv2.at[a, step, rows],
                    send_sem=s2.at[a, step, q], recv_sem=r2.at[a, step, q],
                    device_id=nextdev, device_id_type=MESH)
                cp.start()
                ring[(a, step, q)] = cp
    for a in range(narr):
        first[(nx - 1) * narr + a].wait_recv()
    for q in range(pieces):
        rows = pl.ds(q * span, span)
        for a in range(narr):
            value = (parts[a][2 * x + k, rows, :].astype(jnp.float32)
                     + recv1[a, nx - 1, rows, :].astype(jnp.float32))
            ring[(a, nx - 2, q)].wait_recv()
            outs[a][rows, :] = recv2[a, nx - 2, rows, :].astype(jnp.float32) + value
    for cp in first:
        cp.wait_send()
    for cp in ring.values():
        cp.wait_send()


def col_reduce_scatter(arrays, cid):
    n = lax.axis_size("col")
    nx = n // 2
    narr = len(arrays)
    rows = arrays[0].shape[0] // n
    cols = arrays[0].shape[1]
    parts = [a.reshape(n, rows, cols) for a in arrays]
    return pl.pallas_call(
        functools.partial(_rs_kernel, nx, narr),
        out_shape=[jax.ShapeDtypeStruct((rows, cols), jnp.float32)] * narr,
        in_specs=[pl.BlockSpec(memory_space=pltpu.VMEM)] * narr,
        out_specs=[pl.BlockSpec(memory_space=pltpu.VMEM)] * narr,
        scratch_shapes=[
            pltpu.VMEM((narr, nx, rows, cols), jnp.bfloat16),
            pltpu.VMEM((narr, nx - 1, rows, cols), jnp.bfloat16),
            pltpu.VMEM((narr, nx - 1, rows, cols), jnp.bfloat16),
            pltpu.SemaphoreType.DMA((narr, nx)),
            pltpu.SemaphoreType.DMA((narr, nx)),
            pltpu.SemaphoreType.DMA((narr, nx - 1, 4)),
            pltpu.SemaphoreType.DMA((narr, nx - 1, 4)),
        ],
        compiler_params=pltpu.CompilerParams(collective_id=cid, has_side_effects=True,
                                             vmem_limit_bytes=64 * 1024 * 1024),
    )(*parts)


def _ag_kernel(nx, narr, *refs):
    chunks = refs[:narr]
    weights = refs[narr:2 * narr]
    outs = refs[2 * narr:3 * narr]
    prods = refs[3 * narr:4 * narr]
    sr, rr, sc, rc = refs[4 * narr:]
    row = lax.axis_index("row")
    x, k, d, nxt, prv = _col_ids(nx)
    _greet(row, k, x, nxt, prv)
    me = 2 * x + k
    partner = (row, 2 * x + 1 - k)
    nextdev = (row, 2 * nxt + k)

    def product(a, slot):
        prods[a][slot] = jnp.dot(outs[a][slot], weights[a][...],
                                 preferred_element_type=jnp.float32).astype(prods[a].dtype)

    for a in range(narr):
        outs[a][me] = chunks[a][...]
    ring, core = [], []
    for step in range(nx):
        for a in range(narr):
            src_x = lax.rem(x + 4 * nx - d * step, nx)
            slot = 2 * src_x + k
            if step > 0:
                ring[(step - 1) * narr + a].wait_recv()
            src = chunks[a] if step == 0 else outs[a].at[slot]
            if step < nx - 1:
                cp = pltpu.make_async_remote_copy(
                    src_ref=src, dst_ref=outs[a].at[slot],
                    send_sem=sr.at[a, step], recv_sem=rr.at[a, step],
                    device_id=nextdev, device_id_type=MESH)
                cp.start()
                ring.append(cp)
            cc = pltpu.make_async_remote_copy(
                src_ref=src, dst_ref=outs[a].at[slot],
                send_sem=sc.at[a, step], recv_sem=rc.at[a, step],
                device_id=partner, device_id_type=MESH)
            cc.start()
            core.append(cc)
        for a in range(narr):
            product(a, 2 * lax.rem(x + 4 * nx - d * step, nx) + k)
        if step > 0:
            for a in range(narr):
                core[(step - 1) * narr + a].wait()
            for a in range(narr):
                product(a, 2 * lax.rem(x + 4 * nx + d * (step - 1), nx) + 1 - k)
    for cp in ring:
        cp.wait_send()
    for a in range(narr):
        core[(nx - 1) * narr + a].wait()
    for a in range(narr):
        product(a, 2 * lax.rem(x + 4 * nx + d * (nx - 1), nx) + 1 - k)


def col_all_gather(arrays, weights, cid):
    n = lax.axis_size("col")
    nx = n // 2
    narr = len(arrays)
    rows, cols = arrays[0].shape
    width = weights[0].shape[1]
    res = pl.pallas_call(
        functools.partial(_ag_kernel, nx, narr),
        out_shape=[jax.ShapeDtypeStruct((n, rows, cols), arrays[0].dtype)] * narr
        + [jax.ShapeDtypeStruct((n, rows, width), jnp.bfloat16)] * narr,
        in_specs=[pl.BlockSpec(memory_space=pltpu.VMEM)] * (2 * narr),
        out_specs=[pl.BlockSpec(memory_space=pltpu.VMEM)] * (2 * narr),
        scratch_shapes=[
            pltpu.SemaphoreType.DMA((narr, nx)),
            pltpu.SemaphoreType.DMA((narr, nx)),
            pltpu.SemaphoreType.DMA((narr, nx)),
            pltpu.SemaphoreType.DMA((narr, nx)),
        ],
        compiler_params=pltpu.CompilerParams(collective_id=cid, has_side_effects=True,
                                             vmem_limit_bytes=64 * 1024 * 1024),
    )(*arrays, *weights)
    gathered = [o.reshape(n * rows, cols) for o in res[:narr]]
    products = [o.reshape(n * rows, width) for o in res[narr:]]
    return gathered, products


def _row_ids():
    me = lax.axis_index("row")
    y = me // 4
    z = me % 4
    k = lax.axis_index("col") % 2
    d = 1 - 2 * k
    return y, z, d


def _row_ag_kernel(ny, *refs):
    ins = refs[:2]
    weights = refs[2:4]
    outs = refs[4:6]
    terms = refs[6:8]
    sa, sb, rsem = refs[8:]

    def product(a, slot):
        if a == 0:
            value = jnp.dot(outs[a][slot], weights[a][...], preferred_element_type=jnp.float32)
        else:
            value = lax.dot_general(outs[a][slot], weights[a][...], (((1,), (1,)), ((), ())),
                                    preferred_element_type=jnp.float32)
        terms[a][slot] = value.astype(terms[a].dtype)

    col = lax.axis_index("col")
    y, z, d = _row_ids()
    me = y * 4 + z
    barrier = pltpu.get_barrier_semaphore()
    peers = (y * 4 + lax.rem(z + 4 + d, 4), y * 4 + lax.rem(z + 4 - d, 4),
             lax.rem(y + ny + d, ny) * 4 + z, lax.rem(y + ny - d, ny) * 4 + z)
    for p in peers:
        pl.semaphore_signal(barrier, inc=1, device_id=(p, col), device_id_type=MESH)
    pl.semaphore_wait(barrier, 4)
    geo = []
    for a in range(2):
        if a == 0:
            na, nb = 4, ny
            pos_a, pos_b = z, y
            slot_of = lambda pa, pb: pb * 4 + pa
        else:
            na, nb = ny, 4
            pos_a, pos_b = y, z
            slot_of = lambda pa, pb: pa * 4 + pb
        geo.append((na, nb, pos_a, pos_b, slot_of))
        outs[a][me] = ins[a][...]

    def dev(a, pa, pb):
        return (geo[a][4](pa, pb), col)

    def send(a, src, slot, target, sem):
        cp = pltpu.make_async_remote_copy(
            src_ref=src, dst_ref=outs[a].at[slot], send_sem=sem, recv_sem=rsem.at[a, slot],
            device_id=target, device_id_type=MESH)
        cp.start()
        return cp

    def wait_in(a, slot):
        pltpu.make_async_remote_copy(
            src_ref=ins[a], dst_ref=outs[a].at[slot], send_sem=sa.at[a, 0], recv_sem=rsem.at[a, slot],
            device_id=(peers[0], col), device_id_type=MESH).wait_recv()

    sends = []
    for a in range(2):
        na, nb, pa, pb, slot_of = geo[a]
        next_a = dev(a, lax.rem(pa + na + d, na), pb)
        next_b = dev(a, pa, lax.rem(pb + nb + d, nb))
        sends.append(send(a, ins[a], me, next_a, sa.at[a, 0]))
        sends.append(send(a, ins[a], me, next_b, sb.at[a, 0, 0]))
    for a in range(2):
        product(a, me)
    for s in range(1, 4):
        for a in range(2):
            na, nb, pa, pb, slot_of = geo[a]
            next_a = dev(a, lax.rem(pa + na + d, na), pb)
            next_b = dev(a, pa, lax.rem(pb + nb + d, nb))
            slot = slot_of(lax.rem(pa + 4 * na - d * s, na), pb)
            wait_in(a, slot)
            if s < na - 1:
                sends.append(send(a, outs[a].at[slot], slot, next_a, sa.at[a, s]))
            sends.append(send(a, outs[a].at[slot], slot, next_b, sb.at[a, 0, s]))
            product(a, slot)
    for t in range(1, 4):
        for j in range(4):
            for a in range(2):
                na, nb, pa, pb, slot_of = geo[a]
                next_b = dev(a, pa, lax.rem(pb + nb + d, nb))
                slot = slot_of(lax.rem(pa + 4 * na - d * j, na), lax.rem(pb + 4 * nb - d * t, nb))
                wait_in(a, slot)
                if t < nb - 1:
                    sends.append(send(a, outs[a].at[slot], slot, next_b, sb.at[a, t, j]))
                product(a, slot)
    for cp in sends:
        cp.wait_send()


def row_all_gather(first, second, w_first, w_second, cid):
    n = lax.axis_size("row")
    ny = n // 4
    rows, cols = first.shape
    width = w_first.shape[1]
    outs = pl.pallas_call(
        functools.partial(_row_ag_kernel, ny),
        out_shape=[jax.ShapeDtypeStruct((n, rows, cols), first.dtype)] * 2
        + [jax.ShapeDtypeStruct((n, rows, width), jnp.bfloat16)] * 2,
        in_specs=[pl.BlockSpec(memory_space=pltpu.VMEM)] * 4,
        out_specs=[pl.BlockSpec(memory_space=pltpu.VMEM)] * 4,
        scratch_shapes=[
            pltpu.SemaphoreType.DMA((2, 4)),
            pltpu.SemaphoreType.DMA((2, 4, 4)),
            pltpu.SemaphoreType.DMA((2, n)),
        ],
        compiler_params=pltpu.CompilerParams(collective_id=cid, has_side_effects=True,
                                             vmem_limit_bytes=64 * 1024 * 1024),
    )(first, second, w_first, w_second)
    return [o.reshape(n * rows, o.shape[2]) for o in outs]


def _row_rs_kernel(ny, *refs):
    ins = refs[:2]
    outs = refs[2:4]
    sb1, rb1, ssum, sb2, rb2, s1, r1, s2, r2 = refs[4:]
    col = lax.axis_index("col")
    y, z, d = _row_ids()
    barrier = pltpu.get_barrier_semaphore()
    peers = (y * 4 + lax.rem(z + 4 + d, 4), y * 4 + lax.rem(z + 4 - d, 4),
             lax.rem(y + ny + d, ny) * 4 + z, lax.rem(y + ny - d, ny) * 4 + z)
    for p in peers:
        pl.semaphore_signal(barrier, inc=1, device_id=(p, col), device_id_type=MESH)
    pl.semaphore_wait(barrier, 4)
    geo = [(4, ny, z, y, lambda pa, pb: pb * 4 + pa), (ny, 4, y, z, lambda pa, pb: pa * 4 + pb)]

    def dev(a, pa, pb):
        return (geo[a][4](pa, pb), col)

    def send(src, dst, ssem, rsem, target):
        cp = pltpu.make_async_remote_copy(src_ref=src, dst_ref=dst, send_sem=ssem, recv_sem=rsem,
                                          device_id=target, device_id_type=MESH)
        cp.start()
        return cp

    sends = []
    first = {}
    for s in range(4 - 1):
        for bq in range(4):
            for a in range(2):
                na, nb, pa, pb, slot_of = geo[a]
                slot = slot_of(lax.rem(pa + 4 * na - d * (s + 1), na), bq)
                if s == 0:
                    src = ins[a].at[slot]
                else:
                    first[(a, s - 1, bq)].wait_recv()
                    sb1[a, s, bq] = (rb1[a, s - 1, bq].astype(jnp.float32)
                                     + ins[a][slot].astype(jnp.float32)).astype(sb1.dtype)
                    src = sb1.at[a, s, bq]
                cp = send(src, rb1.at[a, s, bq], s1.at[a, s, bq], r1.at[a, s, bq],
                          dev(a, lax.rem(pa + na + d, na), pb))
                sends.append(cp)
                first[(a, s, bq)] = cp
    for bq in range(4):
        for a in range(2):
            na, nb, pa, pb, slot_of = geo[a]
            first[(a, 2, bq)].wait_recv()
            ssum[a, bq] = rb1[a, 2, bq].astype(jnp.float32) + ins[a][slot_of(pa, bq)].astype(jnp.float32)
    second = [[] for _ in range(2)]
    for t in range(4 - 1):
        for a in range(2):
            na, nb, pa, pb, slot_of = geo[a]
            pos = lax.rem(pb + 4 * nb - d * (t + 1), nb)
            if t == 0:
                sb2[a, t] = ssum[a, pos].astype(sb2.dtype)
            else:
                sb2[a, t] = (rb2[a, t - 1].astype(jnp.float32) + ssum[a, pos]).astype(sb2.dtype)
            cp = send(sb2.at[a, t], rb2.at[a, t], s2.at[a, t], r2.at[a, t],
                      dev(a, pa, lax.rem(pb + nb + d, nb)))
            sends.append(cp)
            second[a].append(cp)
        for a in range(2):
            second[a][t].wait_recv()
    for a in range(2):
        na, nb, pa, pb, slot_of = geo[a]
        outs[a][...] = rb2[a, 2].astype(jnp.float32) + ssum[a, pb]
    for cp in sends:
        cp.wait_send()


def row_reduce_scatter(first, second, cid):
    n = lax.axis_size("row")
    ny = n // 4
    rows, cols = first.shape[0] // n, first.shape[1]
    ins = [v.reshape(n, rows, cols) for v in (first, second)]
    return pl.pallas_call(
        functools.partial(_row_rs_kernel, ny),
        out_shape=[jax.ShapeDtypeStruct((rows, cols), jnp.float32)] * 2,
        in_specs=[pl.BlockSpec(memory_space=pltpu.VMEM)] * 2,
        out_specs=[pl.BlockSpec(memory_space=pltpu.VMEM)] * 2,
        scratch_shapes=[
            pltpu.VMEM((2, 3, 4, rows, cols), jnp.bfloat16),
            pltpu.VMEM((2, 3, 4, rows, cols), jnp.bfloat16),
            pltpu.VMEM((2, 4, rows, cols), jnp.float32),
            pltpu.VMEM((2, 3, rows, cols), jnp.bfloat16),
            pltpu.VMEM((2, 3, rows, cols), jnp.bfloat16),
            pltpu.SemaphoreType.DMA((2, 3, 4)),
            pltpu.SemaphoreType.DMA((2, 3, 4)),
            pltpu.SemaphoreType.DMA((2, 3)),
            pltpu.SemaphoreType.DMA((2, 3)),
        ],
        compiler_params=pltpu.CompilerParams(collective_id=cid, has_side_effects=True,
                                             vmem_limit_bytes=64 * 1024 * 1024),
    )(*ins)


def gelu_grad(value):
    cdf = 0.5 * (1.0 + jax.scipy.special.erf(value * 0.7071067811865476))
    pdf = jnp.exp(-0.5 * value * value) * 0.3989422804014327
    return cdf + value * pdf


def token_panel(local_rows):
    return lax.all_gather(local_rows, "row", axis=0, tiled=True)


def token_panel_a2a(local_rows):
    n = lax.axis_size("row")
    copies = jnp.broadcast_to(local_rows[None], (n,) + local_rows.shape)
    copies = copies.reshape(n * local_rows.shape[0], local_rows.shape[1])
    return lax.all_to_all(copies, "row", split_axis=0, concat_axis=0, tiled=True)


def hidden_panel(local_rows):
    return lax.all_gather(local_rows, "col", axis=0, tiled=True)


def contract_last(left, right):
    return lax.dot_general(
        left, right, (((1,), (1,)), ((), ())), preferred_element_type=jnp.float32
    )


def width_split(left_all, right, transposed):
    if transposed:
        term = contract_last(left_all, right)
    else:
        term = jnp.dot(left_all, right, preferred_element_type=jnp.float32)
    return lax.psum_scatter(
        term.astype(jnp.bfloat16), "col", scatter_dimension=0, tiled=True
    ).astype(jnp.float32)


def unit_sum(left_all, right, transposed):
    n = lax.axis_size("row")
    if transposed:
        term = contract_last(left_all, right)
    else:
        term = jnp.dot(left_all, right, preferred_element_type=jnp.float32)
    pieces = term.astype(jnp.bfloat16).reshape(n, term.shape[0] // n, term.shape[1])
    pieces = lax.all_to_all(pieces, "row", split_axis=0, concat_axis=0, tiled=True)
    return jnp.sum(pieces.astype(jnp.float32), axis=0)


def row_sum(term):
    n = lax.axis_size("row")
    pieces = term.reshape(n, term.shape[0] // n, term.shape[1])
    pieces = lax.all_to_all(pieces, "row", split_axis=0, concat_axis=0, tiled=True)
    return jnp.sum(pieces.astype(jnp.float32), axis=0)


def local(tokens, w_in, w_out, cotangent):
    tokens_all, upstream_all, pre_term, dact_term = row_all_gather(tokens, cotangent, w_in, w_out, 3)
    pre_part, dact_part = col_reduce_scatter([pre_term, dact_term], 1)
    act = jax.nn.gelu(pre_part, approximate=False).astype(jnp.bfloat16)
    dpre = (dact_part * gelu_grad(pre_part)).astype(jnp.bfloat16)
    (act_all, dpre_all), (mixed_term, back_term) = col_all_gather([act, dpre], [w_out, w_in.T], 2)
    mixed, back = row_reduce_scatter(mixed_term, back_term, 4)
    block_rows = (tokens.astype(jnp.float32) + mixed).astype(jnp.bfloat16)
    block_out = lax.all_to_all(block_rows, "col", split_axis=0, concat_axis=1, tiled=True)
    grad_out = lax.dot_general(
        act_all, upstream_all, (((0,), (0,)), ((), ())), preferred_element_type=jnp.float32
    )
    grad_in = lax.dot_general(
        tokens_all, dpre_all, (((0,), (0,)), ((), ())), preferred_element_type=jnp.float32
    )
    grad_tokens = (cotangent.astype(jnp.float32) + back).astype(jnp.bfloat16)
    return (block_out, grad_tokens, grad_in, grad_out)


def solution(mesh):
    in_specs = (P("row", "col"), P("col", "row"), P("row", "col"), P("row", "col"))
    out_specs = (P(("row", "col"), None), P("row", "col"), P("col", "row"), P("row", "col"))
    return jax.shard_map(local, mesh=mesh, in_specs=in_specs, out_specs=out_specs, check_vma=False)
```

```python
import jax
import jax.numpy as jnp
from jax import lax
from jax.sharding import PartitionSpec as P
import functools
from jax.experimental import pallas as pl
from jax.experimental.pallas import tpu as pltpu

MESH = pl.DeviceIdType.MESH


def _col_ids(nx):
    me = lax.axis_index("col")
    x = me // 2
    k = me % 2
    d = 1 - 2 * k
    nxt = lax.rem(x + nx + d, nx)
    prv = lax.rem(x + nx - d, nx)
    return x, k, d, nxt, prv


def _greet(row, k, x, nxt, prv):
    barrier = pltpu.get_barrier_semaphore()
    for peer in (2 * x + 1 - k, 2 * nxt + k, 2 * prv + k):
        pl.semaphore_signal(barrier, inc=1, device_id=(row, peer), device_id_type=MESH)
    pl.semaphore_wait(barrier, 3)


def _rs_kernel(nx, narr, *refs):
    parts = refs[:narr]
    outs = refs[narr:2 * narr]
    recv1, sendbuf, recv2, s1, r1, s2, r2 = refs[2 * narr:]
    row = lax.axis_index("row")
    x, k, d, nxt, prv = _col_ids(nx)
    _greet(row, k, x, nxt, prv)
    partner = (row, 2 * x + 1 - k)
    nextdev = (row, 2 * nxt + k)

    def order(j, sign):
        if j == nx - 1:
            return x
        return lax.rem(x + 4 * nx + sign * d * (j + 1), nx)

    first = []
    for j in range(nx):
        for a in range(narr):
            cp = pltpu.make_async_remote_copy(
                src_ref=parts[a].at[2 * order(j, 1) + 1 - k], dst_ref=recv1.at[a, j],
                send_sem=s1.at[a, j], recv_sem=r1.at[a, j],
                device_id=partner, device_id_type=MESH)
            cp.start()
            first.append(cp)

    def chip_sum(a, j):
        first[j * narr + a].wait_recv()
        own = parts[a][2 * order(j, -1) + k].astype(jnp.float32)
        return own + recv1[a, j].astype(jnp.float32)

    pieces = 4
    span = outs[0].shape[0] // pieces
    ring = {}
    for step in range(nx - 1):
        for a in range(narr):
            first[step * narr + a].wait_recv()
        for q in range(pieces):
            rows = pl.ds(q * span, span)
            for a in range(narr):
                value = (parts[a][2 * order(step, -1) + k, rows, :].astype(jnp.float32)
                         + recv1[a, step, rows, :].astype(jnp.float32))
                if step == 0:
                    sendbuf[a, step, rows, :] = value.astype(sendbuf.dtype)
                else:
                    ring[(a, step - 1, q)].wait_recv()
                    sendbuf[a, step, rows, :] = (recv2[a, step - 1, rows, :].astype(jnp.float32)
                                                 + value).astype(sendbuf.dtype)
                cp = pltpu.make_async_remote_copy(
                    src_ref=sendbuf.at[a, step, rows], dst_ref=recv2.at[a, step, rows],
                    send_sem=s2.at[a, step, q], recv_sem=r2.at[a, step, q],
                    device_id=nextdev, device_id_type=MESH)
                cp.start()
                ring[(a, step, q)] = cp
    for a in range(narr):
        first[(nx - 1) * narr + a].wait_recv()
    for q in range(pieces):
        rows = pl.ds(q * span, span)
        sums = []
        for a in range(narr):
            value = (parts[a][2 * x + k, rows, :].astype(jnp.float32)
                     + recv1[a, nx - 1, rows, :].astype(jnp.float32))
            ring[(a, nx - 2, q)].wait_recv()
            sums.append(recv2[a, nx - 2, rows, :].astype(jnp.float32) + value)
        pre, dact = sums
        cdf = 0.5 * (1.0 + jax.scipy.special.erf(pre * 0.7071067811865476))
        outs[0][rows, :] = (pre * cdf).astype(outs[0].dtype)
        outs[1][rows, :] = (dact * gelu_grad(pre)).astype(outs[1].dtype)
    for cp in first:
        cp.wait_send()
    for cp in ring.values():
        cp.wait_send()


def col_reduce_scatter(arrays, cid):
    n = lax.axis_size("col")
    nx = n // 2
    narr = len(arrays)
    rows = arrays[0].shape[0] // n
    cols = arrays[0].shape[1]
    parts = [a.reshape(n, rows, cols) for a in arrays]
    return pl.pallas_call(
        functools.partial(_rs_kernel, nx, narr),
        out_shape=[jax.ShapeDtypeStruct((rows, cols), jnp.bfloat16)] * narr,
        in_specs=[pl.BlockSpec(memory_space=pltpu.VMEM)] * narr,
        out_specs=[pl.BlockSpec(memory_space=pltpu.VMEM)] * narr,
        scratch_shapes=[
            pltpu.VMEM((narr, nx, rows, cols), jnp.bfloat16),
            pltpu.VMEM((narr, nx - 1, rows, cols), jnp.bfloat16),
            pltpu.VMEM((narr, nx - 1, rows, cols), jnp.bfloat16),
            pltpu.SemaphoreType.DMA((narr, nx)),
            pltpu.SemaphoreType.DMA((narr, nx)),
            pltpu.SemaphoreType.DMA((narr, nx - 1, 4)),
            pltpu.SemaphoreType.DMA((narr, nx - 1, 4)),
        ],
        compiler_params=pltpu.CompilerParams(collective_id=cid, has_side_effects=True,
                                             vmem_limit_bytes=64 * 1024 * 1024),
    )(*parts)


def _ag_kernel(nx, narr, *refs):
    chunks = refs[:narr]
    weights = refs[narr:2 * narr]
    outs = refs[2 * narr:3 * narr]
    prods = refs[3 * narr:4 * narr]
    sr, rr, sc, rc = refs[4 * narr:]
    row = lax.axis_index("row")
    x, k, d, nxt, prv = _col_ids(nx)
    _greet(row, k, x, nxt, prv)
    me = 2 * x + k
    partner = (row, 2 * x + 1 - k)
    nextdev = (row, 2 * nxt + k)

    def product(a, slot):
        prods[a][slot] = jnp.dot(outs[a][slot], weights[a][...],
                                 preferred_element_type=jnp.float32).astype(prods[a].dtype)

    for a in range(narr):
        outs[a][me] = chunks[a][...]
    ring, core = [], []
    for step in range(nx):
        for a in range(narr):
            src_x = lax.rem(x + 4 * nx - d * step, nx)
            slot = 2 * src_x + k
            if step > 0:
                ring[(step - 1) * narr + a].wait_recv()
            src = chunks[a] if step == 0 else outs[a].at[slot]
            if step < nx - 1:
                cp = pltpu.make_async_remote_copy(
                    src_ref=src, dst_ref=outs[a].at[slot],
                    send_sem=sr.at[a, step], recv_sem=rr.at[a, step],
                    device_id=nextdev, device_id_type=MESH)
                cp.start()
                ring.append(cp)
            cc = pltpu.make_async_remote_copy(
                src_ref=src, dst_ref=outs[a].at[slot],
                send_sem=sc.at[a, step], recv_sem=rc.at[a, step],
                device_id=partner, device_id_type=MESH)
            cc.start()
            core.append(cc)
        for a in range(narr):
            product(a, 2 * lax.rem(x + 4 * nx - d * step, nx) + k)
        if step > 0:
            for a in range(narr):
                core[(step - 1) * narr + a].wait()
            for a in range(narr):
                product(a, 2 * lax.rem(x + 4 * nx + d * (step - 1), nx) + 1 - k)
    for cp in ring:
        cp.wait_send()
    for a in range(narr):
        core[(nx - 1) * narr + a].wait()
    for a in range(narr):
        product(a, 2 * lax.rem(x + 4 * nx + d * (nx - 1), nx) + 1 - k)


def col_all_gather(arrays, weights, cid):
    n = lax.axis_size("col")
    nx = n // 2
    narr = len(arrays)
    rows, cols = arrays[0].shape
    width = weights[0].shape[1]
    res = pl.pallas_call(
        functools.partial(_ag_kernel, nx, narr),
        out_shape=[jax.ShapeDtypeStruct((n, rows, cols), arrays[0].dtype)] * narr
        + [jax.ShapeDtypeStruct((n, rows, width), jnp.bfloat16)] * narr,
        in_specs=[pl.BlockSpec(memory_space=pltpu.VMEM)] * (2 * narr),
        out_specs=[pl.BlockSpec(memory_space=pltpu.VMEM)] * (2 * narr),
        scratch_shapes=[
            pltpu.SemaphoreType.DMA((narr, nx)),
            pltpu.SemaphoreType.DMA((narr, nx)),
            pltpu.SemaphoreType.DMA((narr, nx)),
            pltpu.SemaphoreType.DMA((narr, nx)),
        ],
        compiler_params=pltpu.CompilerParams(collective_id=cid, has_side_effects=True,
                                             vmem_limit_bytes=64 * 1024 * 1024),
    )(*arrays, *weights)
    gathered = [o.reshape(n * rows, cols) for o in res[:narr]]
    products = [o.reshape(n * rows, width) for o in res[narr:]]
    return gathered, products


def _row_ids():
    me = lax.axis_index("row")
    y = me // 4
    z = me % 4
    k = lax.axis_index("col") % 2
    d = 1 - 2 * k
    return y, z, d


def _row_ag_kernel(ny, *refs):
    ins = refs[:2]
    weights = refs[2:4]
    outs = refs[4:6]
    terms = refs[6:8]
    sa, sb, rsem = refs[8:]

    def product(a, slot):
        if a == 0:
            value = jnp.dot(outs[a][slot], weights[a][...], preferred_element_type=jnp.float32)
        else:
            value = lax.dot_general(outs[a][slot], weights[a][...], (((1,), (1,)), ((), ())),
                                    preferred_element_type=jnp.float32)
        terms[a][slot] = value.astype(terms[a].dtype)

    col = lax.axis_index("col")
    y, z, d = _row_ids()
    me = y * 4 + z
    barrier = pltpu.get_barrier_semaphore()
    peers = (y * 4 + lax.rem(z + 4 + d, 4), y * 4 + lax.rem(z + 4 - d, 4),
             lax.rem(y + ny + d, ny) * 4 + z, lax.rem(y + ny - d, ny) * 4 + z)
    for p in peers:
        pl.semaphore_signal(barrier, inc=1, device_id=(p, col), device_id_type=MESH)
    pl.semaphore_wait(barrier, 4)
    geo = []
    for a in range(2):
        if a == 0:
            na, nb = 4, ny
            pos_a, pos_b = z, y
            slot_of = lambda pa, pb: pb * 4 + pa
        else:
            na, nb = ny, 4
            pos_a, pos_b = y, z
            slot_of = lambda pa, pb: pa * 4 + pb
        geo.append((na, nb, pos_a, pos_b, slot_of))
        outs[a][me] = ins[a][...]

    def dev(a, pa, pb):
        return (geo[a][4](pa, pb), col)

    def send(a, src, slot, target, sem):
        cp = pltpu.make_async_remote_copy(
            src_ref=src, dst_ref=outs[a].at[slot], send_sem=sem, recv_sem=rsem.at[a, slot],
            device_id=target, device_id_type=MESH)
        cp.start()
        return cp

    def wait_in(a, slot):
        pltpu.make_async_remote_copy(
            src_ref=ins[a], dst_ref=outs[a].at[slot], send_sem=sa.at[a, 0], recv_sem=rsem.at[a, slot],
            device_id=(peers[0], col), device_id_type=MESH).wait_recv()

    sends = []
    for a in range(2):
        na, nb, pa, pb, slot_of = geo[a]
        next_a = dev(a, lax.rem(pa + na + d, na), pb)
        next_b = dev(a, pa, lax.rem(pb + nb + d, nb))
        sends.append(send(a, ins[a], me, next_a, sa.at[a, 0]))
        sends.append(send(a, ins[a], me, next_b, sb.at[a, 0, 0]))
    for a in range(2):
        product(a, me)
    for s in range(1, 4):
        for a in range(2):
            na, nb, pa, pb, slot_of = geo[a]
            next_a = dev(a, lax.rem(pa + na + d, na), pb)
            next_b = dev(a, pa, lax.rem(pb + nb + d, nb))
            slot = slot_of(lax.rem(pa + 4 * na - d * s, na), pb)
            wait_in(a, slot)
            if s < na - 1:
                sends.append(send(a, outs[a].at[slot], slot, next_a, sa.at[a, s]))
            sends.append(send(a, outs[a].at[slot], slot, next_b, sb.at[a, 0, s]))
            product(a, slot)
    for t in range(1, 4):
        for j in range(4):
            for a in range(2):
                na, nb, pa, pb, slot_of = geo[a]
                next_b = dev(a, pa, lax.rem(pb + nb + d, nb))
                slot = slot_of(lax.rem(pa + 4 * na - d * j, na), lax.rem(pb + 4 * nb - d * t, nb))
                wait_in(a, slot)
                if t < nb - 1:
                    sends.append(send(a, outs[a].at[slot], slot, next_b, sb.at[a, t, j]))
                product(a, slot)
    for cp in sends:
        cp.wait_send()


def row_all_gather(first, second, w_first, w_second, cid):
    n = lax.axis_size("row")
    ny = n // 4
    rows, cols = first.shape
    width = w_first.shape[1]
    outs = pl.pallas_call(
        functools.partial(_row_ag_kernel, ny),
        out_shape=[jax.ShapeDtypeStruct((n, rows, cols), first.dtype)] * 2
        + [jax.ShapeDtypeStruct((n, rows, width), jnp.bfloat16)] * 2,
        in_specs=[pl.BlockSpec(memory_space=pltpu.VMEM)] * 4,
        out_specs=[pl.BlockSpec(memory_space=pltpu.VMEM)] * 4,
        scratch_shapes=[
            pltpu.SemaphoreType.DMA((2, 4)),
            pltpu.SemaphoreType.DMA((2, 4, 4)),
            pltpu.SemaphoreType.DMA((2, n)),
        ],
        compiler_params=pltpu.CompilerParams(collective_id=cid, has_side_effects=True,
                                             vmem_limit_bytes=64 * 1024 * 1024),
    )(first, second, w_first, w_second)
    return [o.reshape(n * rows, o.shape[2]) for o in outs]


def _row_rs_kernel(ny, *refs):
    ins = refs[:2]
    outs = refs[2:4]
    sb1, rb1, ssum, sb2, rb2, s1, r1, s2, r2 = refs[4:]
    col = lax.axis_index("col")
    y, z, d = _row_ids()
    barrier = pltpu.get_barrier_semaphore()
    peers = (y * 4 + lax.rem(z + 4 + d, 4), y * 4 + lax.rem(z + 4 - d, 4),
             lax.rem(y + ny + d, ny) * 4 + z, lax.rem(y + ny - d, ny) * 4 + z)
    for p in peers:
        pl.semaphore_signal(barrier, inc=1, device_id=(p, col), device_id_type=MESH)
    pl.semaphore_wait(barrier, 4)
    geo = [(4, ny, z, y, lambda pa, pb: pb * 4 + pa), (ny, 4, y, z, lambda pa, pb: pa * 4 + pb)]

    def dev(a, pa, pb):
        return (geo[a][4](pa, pb), col)

    def send(src, dst, ssem, rsem, target):
        cp = pltpu.make_async_remote_copy(src_ref=src, dst_ref=dst, send_sem=ssem, recv_sem=rsem,
                                          device_id=target, device_id_type=MESH)
        cp.start()
        return cp

    sends = []
    first = {}
    for s in range(4 - 1):
        for bq in range(4):
            for a in range(2):
                na, nb, pa, pb, slot_of = geo[a]
                slot = slot_of(lax.rem(pa + 4 * na - d * (s + 1), na), bq)
                if s == 0:
                    src = ins[a].at[slot]
                else:
                    first[(a, s - 1, bq)].wait_recv()
                    sb1[a, s, bq] = (rb1[a, s - 1, bq].astype(jnp.float32)
                                     + ins[a][slot].astype(jnp.float32)).astype(sb1.dtype)
                    src = sb1.at[a, s, bq]
                cp = send(src, rb1.at[a, s, bq], s1.at[a, s, bq], r1.at[a, s, bq],
                          dev(a, lax.rem(pa + na + d, na), pb))
                sends.append(cp)
                first[(a, s, bq)] = cp
    for bq in range(4):
        for a in range(2):
            na, nb, pa, pb, slot_of = geo[a]
            first[(a, 2, bq)].wait_recv()
            ssum[a, bq] = rb1[a, 2, bq].astype(jnp.float32) + ins[a][slot_of(pa, bq)].astype(jnp.float32)
    second = [[] for _ in range(2)]
    for t in range(4 - 1):
        for a in range(2):
            na, nb, pa, pb, slot_of = geo[a]
            pos = lax.rem(pb + 4 * nb - d * (t + 1), nb)
            if t == 0:
                sb2[a, t] = ssum[a, pos].astype(sb2.dtype)
            else:
                sb2[a, t] = (rb2[a, t - 1].astype(jnp.float32) + ssum[a, pos]).astype(sb2.dtype)
            cp = send(sb2.at[a, t], rb2.at[a, t], s2.at[a, t], r2.at[a, t],
                      dev(a, pa, lax.rem(pb + nb + d, nb)))
            sends.append(cp)
            second[a].append(cp)
        for a in range(2):
            second[a][t].wait_recv()
    for a in range(2):
        na, nb, pa, pb, slot_of = geo[a]
        outs[a][...] = rb2[a, 2].astype(jnp.float32) + ssum[a, pb]
    for cp in sends:
        cp.wait_send()


def row_reduce_scatter(first, second, cid):
    n = lax.axis_size("row")
    ny = n // 4
    rows, cols = first.shape[0] // n, first.shape[1]
    ins = [v.reshape(n, rows, cols) for v in (first, second)]
    return pl.pallas_call(
        functools.partial(_row_rs_kernel, ny),
        out_shape=[jax.ShapeDtypeStruct((rows, cols), jnp.float32)] * 2,
        in_specs=[pl.BlockSpec(memory_space=pltpu.VMEM)] * 2,
        out_specs=[pl.BlockSpec(memory_space=pltpu.VMEM)] * 2,
        scratch_shapes=[
            pltpu.VMEM((2, 3, 4, rows, cols), jnp.bfloat16),
            pltpu.VMEM((2, 3, 4, rows, cols), jnp.bfloat16),
            pltpu.VMEM((2, 4, rows, cols), jnp.float32),
            pltpu.VMEM((2, 3, rows, cols), jnp.bfloat16),
            pltpu.VMEM((2, 3, rows, cols), jnp.bfloat16),
            pltpu.SemaphoreType.DMA((2, 3, 4)),
            pltpu.SemaphoreType.DMA((2, 3, 4)),
            pltpu.SemaphoreType.DMA((2, 3)),
            pltpu.SemaphoreType.DMA((2, 3)),
        ],
        compiler_params=pltpu.CompilerParams(collective_id=cid, has_side_effects=True,
                                             vmem_limit_bytes=64 * 1024 * 1024),
    )(*ins)


def gelu_grad(value):
    cdf = 0.5 * (1.0 + jax.scipy.special.erf(value * 0.7071067811865476))
    pdf = jnp.exp(-0.5 * value * value) * 0.3989422804014327
    return cdf + value * pdf


def token_panel(local_rows):
    return lax.all_gather(local_rows, "row", axis=0, tiled=True)


def token_panel_a2a(local_rows):
    n = lax.axis_size("row")
    copies = jnp.broadcast_to(local_rows[None], (n,) + local_rows.shape)
    copies = copies.reshape(n * local_rows.shape[0], local_rows.shape[1])
    return lax.all_to_all(copies, "row", split_axis=0, concat_axis=0, tiled=True)


def hidden_panel(local_rows):
    return lax.all_gather(local_rows, "col", axis=0, tiled=True)


def contract_last(left, right):
    return lax.dot_general(
        left, right, (((1,), (1,)), ((), ())), preferred_element_type=jnp.float32
    )


def width_split(left_all, right, transposed):
    if transposed:
        term = contract_last(left_all, right)
    else:
        term = jnp.dot(left_all, right, preferred_element_type=jnp.float32)
    return lax.psum_scatter(
        term.astype(jnp.bfloat16), "col", scatter_dimension=0, tiled=True
    ).astype(jnp.float32)


def unit_sum(left_all, right, transposed):
    n = lax.axis_size("row")
    if transposed:
        term = contract_last(left_all, right)
    else:
        term = jnp.dot(left_all, right, preferred_element_type=jnp.float32)
    pieces = term.astype(jnp.bfloat16).reshape(n, term.shape[0] // n, term.shape[1])
    pieces = lax.all_to_all(pieces, "row", split_axis=0, concat_axis=0, tiled=True)
    return jnp.sum(pieces.astype(jnp.float32), axis=0)


def row_sum(term):
    n = lax.axis_size("row")
    pieces = term.reshape(n, term.shape[0] // n, term.shape[1])
    pieces = lax.all_to_all(pieces, "row", split_axis=0, concat_axis=0, tiled=True)
    return jnp.sum(pieces.astype(jnp.float32), axis=0)


def local(tokens, w_in, w_out, cotangent):
    tokens_all, upstream_all, pre_term, dact_term = row_all_gather(tokens, cotangent, w_in, w_out, 3)
    act, dpre = col_reduce_scatter([pre_term, dact_term], 1)
    (act_all, dpre_all), (mixed_term, back_term) = col_all_gather([act, dpre], [w_out, w_in.T], 2)
    mixed, back = row_reduce_scatter(mixed_term, back_term, 4)
    block_rows = (tokens.astype(jnp.float32) + mixed).astype(jnp.bfloat16)
    block_out = lax.all_to_all(block_rows, "col", split_axis=0, concat_axis=1, tiled=True)
    grad_out = lax.dot_general(
        act_all, upstream_all, (((0,), (0,)), ((), ())), preferred_element_type=jnp.float32
    )
    grad_in = lax.dot_general(
        tokens_all, dpre_all, (((0,), (0,)), ((), ())), preferred_element_type=jnp.float32
    )
    grad_tokens = (cotangent.astype(jnp.float32) + back).astype(jnp.bfloat16)
    return (block_out, grad_tokens, grad_in, grad_out)


def solution(mesh):
    in_specs = (P("row", "col"), P("col", "row"), P("row", "col"), P("row", "col"))
    out_specs = (P(("row", "col"), None), P("row", "col"), P("col", "row"), P("row", "col"))
    return jax.shard_map(local, mesh=mesh, in_specs=in_specs, out_specs=out_specs, check_vma=False)
```

```python
import jax
import jax.numpy as jnp
from jax import lax
from jax.sharding import PartitionSpec as P
import functools
from jax.experimental import pallas as pl
from jax.experimental.pallas import tpu as pltpu

MESH = pl.DeviceIdType.MESH


def _col_ids(nx):
    me = lax.axis_index("col")
    x = me // 2
    k = me % 2
    d = 1 - 2 * k
    nxt = lax.rem(x + nx + d, nx)
    prv = lax.rem(x + nx - d, nx)
    return x, k, d, nxt, prv


def _greet(row, k, x, nxt, prv):
    barrier = pltpu.get_barrier_semaphore()
    for peer in (2 * x + 1 - k, 2 * nxt + k, 2 * prv + k):
        pl.semaphore_signal(barrier, inc=1, device_id=(row, peer), device_id_type=MESH)
    pl.semaphore_wait(barrier, 3)


def _rs_kernel(nx, narr, *refs):
    parts = refs[:narr]
    outs = refs[narr:2 * narr]
    recv1, sendbuf, recv2, s1, r1, s2, r2 = refs[2 * narr:]
    row = lax.axis_index("row")
    x, k, d, nxt, prv = _col_ids(nx)
    _greet(row, k, x, nxt, prv)
    partner = (row, 2 * x + 1 - k)
    nextdev = (row, 2 * nxt + k)

    def order(j, sign):
        if j == nx - 1:
            return x
        return lax.rem(x + 4 * nx + sign * d * (j + 1), nx)

    first = []
    for j in range(nx):
        for a in range(narr):
            cp = pltpu.make_async_remote_copy(
                src_ref=parts[a].at[2 * order(j, 1) + 1 - k], dst_ref=recv1.at[a, j],
                send_sem=s1.at[a, j], recv_sem=r1.at[a, j],
                device_id=partner, device_id_type=MESH)
            cp.start()
            first.append(cp)

    def chip_sum(a, j):
        first[j * narr + a].wait_recv()
        own = parts[a][2 * order(j, -1) + k].astype(jnp.float32)
        return own + recv1[a, j].astype(jnp.float32)

    pieces = 4
    span = outs[0].shape[0] // pieces
    ring = {}
    for step in range(nx - 1):
        for a in range(narr):
            first[step * narr + a].wait_recv()
        for q in range(pieces):
            rows = pl.ds(q * span, span)
            for a in range(narr):
                value = (parts[a][2 * order(step, -1) + k, rows, :].astype(jnp.float32)
                         + recv1[a, step, rows, :].astype(jnp.float32))
                if step == 0:
                    sendbuf[a, step, rows, :] = value.astype(sendbuf.dtype)
                else:
                    ring[(a, step - 1, q)].wait_recv()
                    sendbuf[a, step, rows, :] = (recv2[a, step - 1, rows, :].astype(jnp.float32)
                                                 + value).astype(sendbuf.dtype)
                cp = pltpu.make_async_remote_copy(
                    src_ref=sendbuf.at[a, step, rows], dst_ref=recv2.at[a, step, rows],
                    send_sem=s2.at[a, step, q], recv_sem=r2.at[a, step, q],
                    device_id=nextdev, device_id_type=MESH)
                cp.start()
                ring[(a, step, q)] = cp
    for a in range(narr):
        first[(nx - 1) * narr + a].wait_recv()
    for q in range(pieces):
        rows = pl.ds(q * span, span)
        sums = []
        for a in range(narr):
            value = (parts[a][2 * x + k, rows, :].astype(jnp.float32)
                     + recv1[a, nx - 1, rows, :].astype(jnp.float32))
            ring[(a, nx - 2, q)].wait_recv()
            sums.append(recv2[a, nx - 2, rows, :].astype(jnp.float32) + value)
        pre, dact = sums
        cdf = 0.5 * (1.0 + jax.scipy.special.erf(pre * 0.7071067811865476))
        outs[0][rows, :] = (pre * cdf).astype(outs[0].dtype)
        outs[1][rows, :] = (dact * gelu_grad(pre)).astype(outs[1].dtype)
    for cp in first:
        cp.wait_send()
    for cp in ring.values():
        cp.wait_send()


def col_reduce_scatter(arrays, cid):
    n = lax.axis_size("col")
    nx = n // 2
    narr = len(arrays)
    rows = arrays[0].shape[0] // n
    cols = arrays[0].shape[1]
    parts = [a.reshape(n, rows, cols) for a in arrays]
    return pl.pallas_call(
        functools.partial(_rs_kernel, nx, narr),
        out_shape=[jax.ShapeDtypeStruct((rows, cols), jnp.bfloat16)] * narr,
        in_specs=[pl.BlockSpec(memory_space=pltpu.VMEM)] * narr,
        out_specs=[pl.BlockSpec(memory_space=pltpu.VMEM)] * narr,
        scratch_shapes=[
            pltpu.VMEM((narr, nx, rows, cols), jnp.bfloat16),
            pltpu.VMEM((narr, nx - 1, rows, cols), jnp.bfloat16),
            pltpu.VMEM((narr, nx - 1, rows, cols), jnp.bfloat16),
            pltpu.SemaphoreType.DMA((narr, nx)),
            pltpu.SemaphoreType.DMA((narr, nx)),
            pltpu.SemaphoreType.DMA((narr, nx - 1, 4)),
            pltpu.SemaphoreType.DMA((narr, nx - 1, 4)),
        ],
        compiler_params=pltpu.CompilerParams(collective_id=cid, has_side_effects=True,
                                             vmem_limit_bytes=64 * 1024 * 1024),
    )(*parts)


def _ag_kernel(nx, narr, *refs):
    chunks = refs[:narr]
    weights = refs[narr:2 * narr]
    outs = refs[2 * narr:3 * narr]
    prods = refs[3 * narr:4 * narr]
    sr, rr, sc, rc = refs[4 * narr:]
    row = lax.axis_index("row")
    x, k, d, nxt, prv = _col_ids(nx)
    _greet(row, k, x, nxt, prv)
    me = 2 * x + k
    partner = (row, 2 * x + 1 - k)
    nextdev = (row, 2 * nxt + k)

    def product(a, slot):
        if a == 0:
            value = jnp.dot(outs[a][slot], weights[a][...], preferred_element_type=jnp.float32)
        else:
            value = lax.dot_general(outs[a][slot], weights[a][...], (((1,), (1,)), ((), ())),
                                    preferred_element_type=jnp.float32)
        prods[a][slot] = value.astype(prods[a].dtype)

    for a in range(narr):
        outs[a][me] = chunks[a][...]
    ring, core = [], []
    for step in range(nx):
        for a in range(narr):
            src_x = lax.rem(x + 4 * nx - d * step, nx)
            slot = 2 * src_x + k
            if step > 0:
                ring[(step - 1) * narr + a].wait_recv()
            src = chunks[a] if step == 0 else outs[a].at[slot]
            if step < nx - 1:
                cp = pltpu.make_async_remote_copy(
                    src_ref=src, dst_ref=outs[a].at[slot],
                    send_sem=sr.at[a, step], recv_sem=rr.at[a, step],
                    device_id=nextdev, device_id_type=MESH)
                cp.start()
                ring.append(cp)
            cc = pltpu.make_async_remote_copy(
                src_ref=src, dst_ref=outs[a].at[slot],
                send_sem=sc.at[a, step], recv_sem=rc.at[a, step],
                device_id=partner, device_id_type=MESH)
            cc.start()
            core.append(cc)
        for a in range(narr):
            product(a, 2 * lax.rem(x + 4 * nx - d * step, nx) + k)
        if step > 0:
            for a in range(narr):
                core[(step - 1) * narr + a].wait()
            for a in range(narr):
                product(a, 2 * lax.rem(x + 4 * nx + d * (step - 1), nx) + 1 - k)
    for cp in ring:
        cp.wait_send()
    for a in range(narr):
        core[(nx - 1) * narr + a].wait()
    for a in range(narr):
        product(a, 2 * lax.rem(x + 4 * nx + d * (nx - 1), nx) + 1 - k)


def col_all_gather(arrays, weights, cid):
    n = lax.axis_size("col")
    nx = n // 2
    narr = len(arrays)
    rows, cols = arrays[0].shape
    width = weights[0].shape[1]
    res = pl.pallas_call(
        functools.partial(_ag_kernel, nx, narr),
        out_shape=[jax.ShapeDtypeStruct((n, rows, cols), arrays[0].dtype)] * narr
        + [jax.ShapeDtypeStruct((n, rows, width), jnp.bfloat16)] * narr,
        in_specs=[pl.BlockSpec(memory_space=pltpu.VMEM)] * (2 * narr),
        out_specs=[pl.BlockSpec(memory_space=pltpu.VMEM)] * (2 * narr),
        scratch_shapes=[
            pltpu.SemaphoreType.DMA((narr, nx)),
            pltpu.SemaphoreType.DMA((narr, nx)),
            pltpu.SemaphoreType.DMA((narr, nx)),
            pltpu.SemaphoreType.DMA((narr, nx)),
        ],
        compiler_params=pltpu.CompilerParams(collective_id=cid, has_side_effects=True,
                                             vmem_limit_bytes=64 * 1024 * 1024),
    )(*arrays, *weights)
    gathered = [o.reshape(n * rows, cols) for o in res[:narr]]
    products = [o.reshape(n * rows, width) for o in res[narr:]]
    return gathered, products


def _row_ids():
    me = lax.axis_index("row")
    y = me // 4
    z = me % 4
    k = lax.axis_index("col") % 2
    d = 1 - 2 * k
    return y, z, d


def _row_ag_kernel(ny, *refs):
    ins = refs[:2]
    weights = refs[2:4]
    outs = refs[4:6]
    terms = refs[6:8]
    sa, sb, rsem = refs[8:]

    def product(a, slot):
        if a == 0:
            value = jnp.dot(outs[a][slot], weights[a][...], preferred_element_type=jnp.float32)
        else:
            value = lax.dot_general(outs[a][slot], weights[a][...], (((1,), (1,)), ((), ())),
                                    preferred_element_type=jnp.float32)
        terms[a][slot] = value.astype(terms[a].dtype)

    col = lax.axis_index("col")
    y, z, d = _row_ids()
    me = y * 4 + z
    barrier = pltpu.get_barrier_semaphore()
    peers = (y * 4 + lax.rem(z + 4 + d, 4), y * 4 + lax.rem(z + 4 - d, 4),
             lax.rem(y + ny + d, ny) * 4 + z, lax.rem(y + ny - d, ny) * 4 + z)
    for p in peers:
        pl.semaphore_signal(barrier, inc=1, device_id=(p, col), device_id_type=MESH)
    pl.semaphore_wait(barrier, 4)
    geo = []
    for a in range(2):
        if a == 0:
            na, nb = 4, ny
            pos_a, pos_b = z, y
            slot_of = lambda pa, pb: pb * 4 + pa
        else:
            na, nb = ny, 4
            pos_a, pos_b = y, z
            slot_of = lambda pa, pb: pa * 4 + pb
        geo.append((na, nb, pos_a, pos_b, slot_of))
        outs[a][me] = ins[a][...]

    def dev(a, pa, pb):
        return (geo[a][4](pa, pb), col)

    def send(a, src, slot, target, sem):
        cp = pltpu.make_async_remote_copy(
            src_ref=src, dst_ref=outs[a].at[slot], send_sem=sem, recv_sem=rsem.at[a, slot],
            device_id=target, device_id_type=MESH)
        cp.start()
        return cp

    def wait_in(a, slot):
        pltpu.make_async_remote_copy(
            src_ref=ins[a], dst_ref=outs[a].at[slot], send_sem=sa.at[a, 0], recv_sem=rsem.at[a, slot],
            device_id=(peers[0], col), device_id_type=MESH).wait_recv()

    sends = []
    for a in range(2):
        na, nb, pa, pb, slot_of = geo[a]
        next_a = dev(a, lax.rem(pa + na + d, na), pb)
        next_b = dev(a, pa, lax.rem(pb + nb + d, nb))
        sends.append(send(a, ins[a], me, next_a, sa.at[a, 0]))
        sends.append(send(a, ins[a], me, next_b, sb.at[a, 0, 0]))
    for a in range(2):
        product(a, me)
    for s in range(1, 4):
        for a in range(2):
            na, nb, pa, pb, slot_of = geo[a]
            next_a = dev(a, lax.rem(pa + na + d, na), pb)
            next_b = dev(a, pa, lax.rem(pb + nb + d, nb))
            slot = slot_of(lax.rem(pa + 4 * na - d * s, na), pb)
            wait_in(a, slot)
            if s < na - 1:
                sends.append(send(a, outs[a].at[slot], slot, next_a, sa.at[a, s]))
            sends.append(send(a, outs[a].at[slot], slot, next_b, sb.at[a, 0, s]))
            product(a, slot)
    for t in range(1, 4):
        for j in range(4):
            for a in range(2):
                na, nb, pa, pb, slot_of = geo[a]
                next_b = dev(a, pa, lax.rem(pb + nb + d, nb))
                slot = slot_of(lax.rem(pa + 4 * na - d * j, na), lax.rem(pb + 4 * nb - d * t, nb))
                wait_in(a, slot)
                if t < nb - 1:
                    sends.append(send(a, outs[a].at[slot], slot, next_b, sb.at[a, t, j]))
                product(a, slot)
    for cp in sends:
        cp.wait_send()


def row_all_gather(first, second, w_first, w_second, cid):
    n = lax.axis_size("row")
    ny = n // 4
    rows, cols = first.shape
    width = w_first.shape[1]
    outs = pl.pallas_call(
        functools.partial(_row_ag_kernel, ny),
        out_shape=[jax.ShapeDtypeStruct((n, rows, cols), first.dtype)] * 2
        + [jax.ShapeDtypeStruct((n, rows, width), jnp.bfloat16)] * 2,
        in_specs=[pl.BlockSpec(memory_space=pltpu.VMEM)] * 4,
        out_specs=[pl.BlockSpec(memory_space=pltpu.VMEM)] * 4,
        scratch_shapes=[
            pltpu.SemaphoreType.DMA((2, 4)),
            pltpu.SemaphoreType.DMA((2, 4, 4)),
            pltpu.SemaphoreType.DMA((2, n)),
        ],
        compiler_params=pltpu.CompilerParams(collective_id=cid, has_side_effects=True,
                                             vmem_limit_bytes=64 * 1024 * 1024),
    )(first, second, w_first, w_second)
    return [o.reshape(n * rows, o.shape[2]) for o in outs]


def _row_rs_kernel(ny, *refs):
    ins = refs[:2]
    outs = refs[2:4]
    sb1, rb1, ssum, sb2, rb2, s1, r1, s2, r2 = refs[4:]
    col = lax.axis_index("col")
    y, z, d = _row_ids()
    barrier = pltpu.get_barrier_semaphore()
    peers = (y * 4 + lax.rem(z + 4 + d, 4), y * 4 + lax.rem(z + 4 - d, 4),
             lax.rem(y + ny + d, ny) * 4 + z, lax.rem(y + ny - d, ny) * 4 + z)
    for p in peers:
        pl.semaphore_signal(barrier, inc=1, device_id=(p, col), device_id_type=MESH)
    pl.semaphore_wait(barrier, 4)
    geo = [(4, ny, z, y, lambda pa, pb: pb * 4 + pa), (ny, 4, y, z, lambda pa, pb: pa * 4 + pb)]

    def dev(a, pa, pb):
        return (geo[a][4](pa, pb), col)

    def send(src, dst, ssem, rsem, target):
        cp = pltpu.make_async_remote_copy(src_ref=src, dst_ref=dst, send_sem=ssem, recv_sem=rsem,
                                          device_id=target, device_id_type=MESH)
        cp.start()
        return cp

    sends = []
    first = {}
    for s in range(4 - 1):
        for bq in range(4):
            for a in range(2):
                na, nb, pa, pb, slot_of = geo[a]
                slot = slot_of(lax.rem(pa + 4 * na - d * (s + 1), na), bq)
                if s == 0:
                    src = ins[a].at[slot]
                else:
                    first[(a, s - 1, bq)].wait_recv()
                    sb1[a, s, bq] = (rb1[a, s - 1, bq].astype(jnp.float32)
                                     + ins[a][slot].astype(jnp.float32)).astype(sb1.dtype)
                    src = sb1.at[a, s, bq]
                cp = send(src, rb1.at[a, s, bq], s1.at[a, s, bq], r1.at[a, s, bq],
                          dev(a, lax.rem(pa + na + d, na), pb))
                sends.append(cp)
                first[(a, s, bq)] = cp
    for bq in range(4):
        for a in range(2):
            na, nb, pa, pb, slot_of = geo[a]
            first[(a, 2, bq)].wait_recv()
            ssum[a, bq] = rb1[a, 2, bq].astype(jnp.float32) + ins[a][slot_of(pa, bq)].astype(jnp.float32)
    second = [[] for _ in range(2)]
    for t in range(4 - 1):
        for a in range(2):
            na, nb, pa, pb, slot_of = geo[a]
            pos = lax.rem(pb + 4 * nb - d * (t + 1), nb)
            if t == 0:
                sb2[a, t] = ssum[a, pos].astype(sb2.dtype)
            else:
                sb2[a, t] = (rb2[a, t - 1].astype(jnp.float32) + ssum[a, pos]).astype(sb2.dtype)
            cp = send(sb2.at[a, t], rb2.at[a, t], s2.at[a, t], r2.at[a, t],
                      dev(a, pa, lax.rem(pb + nb + d, nb)))
            sends.append(cp)
            second[a].append(cp)
        for a in range(2):
            second[a][t].wait_recv()
    for a in range(2):
        na, nb, pa, pb, slot_of = geo[a]
        outs[a][...] = rb2[a, 2].astype(jnp.float32) + ssum[a, pb]
    for cp in sends:
        cp.wait_send()


def row_reduce_scatter(first, second, cid):
    n = lax.axis_size("row")
    ny = n // 4
    rows, cols = first.shape[0] // n, first.shape[1]
    ins = [v.reshape(n, rows, cols) for v in (first, second)]
    return pl.pallas_call(
        functools.partial(_row_rs_kernel, ny),
        out_shape=[jax.ShapeDtypeStruct((rows, cols), jnp.float32)] * 2,
        in_specs=[pl.BlockSpec(memory_space=pltpu.VMEM)] * 2,
        out_specs=[pl.BlockSpec(memory_space=pltpu.VMEM)] * 2,
        scratch_shapes=[
            pltpu.VMEM((2, 3, 4, rows, cols), jnp.bfloat16),
            pltpu.VMEM((2, 3, 4, rows, cols), jnp.bfloat16),
            pltpu.VMEM((2, 4, rows, cols), jnp.float32),
            pltpu.VMEM((2, 3, rows, cols), jnp.bfloat16),
            pltpu.VMEM((2, 3, rows, cols), jnp.bfloat16),
            pltpu.SemaphoreType.DMA((2, 3, 4)),
            pltpu.SemaphoreType.DMA((2, 3, 4)),
            pltpu.SemaphoreType.DMA((2, 3)),
            pltpu.SemaphoreType.DMA((2, 3)),
        ],
        compiler_params=pltpu.CompilerParams(collective_id=cid, has_side_effects=True,
                                             vmem_limit_bytes=64 * 1024 * 1024),
    )(*ins)


def gelu_grad(value):
    cdf = 0.5 * (1.0 + jax.scipy.special.erf(value * 0.7071067811865476))
    pdf = jnp.exp(-0.5 * value * value) * 0.3989422804014327
    return cdf + value * pdf


def token_panel(local_rows):
    return lax.all_gather(local_rows, "row", axis=0, tiled=True)


def token_panel_a2a(local_rows):
    n = lax.axis_size("row")
    copies = jnp.broadcast_to(local_rows[None], (n,) + local_rows.shape)
    copies = copies.reshape(n * local_rows.shape[0], local_rows.shape[1])
    return lax.all_to_all(copies, "row", split_axis=0, concat_axis=0, tiled=True)


def hidden_panel(local_rows):
    return lax.all_gather(local_rows, "col", axis=0, tiled=True)


def contract_last(left, right):
    return lax.dot_general(
        left, right, (((1,), (1,)), ((), ())), preferred_element_type=jnp.float32
    )


def width_split(left_all, right, transposed):
    if transposed:
        term = contract_last(left_all, right)
    else:
        term = jnp.dot(left_all, right, preferred_element_type=jnp.float32)
    return lax.psum_scatter(
        term.astype(jnp.bfloat16), "col", scatter_dimension=0, tiled=True
    ).astype(jnp.float32)


def unit_sum(left_all, right, transposed):
    n = lax.axis_size("row")
    if transposed:
        term = contract_last(left_all, right)
    else:
        term = jnp.dot(left_all, right, preferred_element_type=jnp.float32)
    pieces = term.astype(jnp.bfloat16).reshape(n, term.shape[0] // n, term.shape[1])
    pieces = lax.all_to_all(pieces, "row", split_axis=0, concat_axis=0, tiled=True)
    return jnp.sum(pieces.astype(jnp.float32), axis=0)


def row_sum(term):
    n = lax.axis_size("row")
    pieces = term.reshape(n, term.shape[0] // n, term.shape[1])
    pieces = lax.all_to_all(pieces, "row", split_axis=0, concat_axis=0, tiled=True)
    return jnp.sum(pieces.astype(jnp.float32), axis=0)


def local(tokens, w_in, w_out, cotangent):
    tokens_all, upstream_all, pre_term, dact_term = row_all_gather(tokens, cotangent, w_in, w_out, 3)
    act, dpre = col_reduce_scatter([pre_term, dact_term], 1)
    (act_all, dpre_all), (mixed_term, back_term) = col_all_gather([act, dpre], [w_out, w_in], 2)
    mixed, back = row_reduce_scatter(mixed_term, back_term, 4)
    block_rows = (tokens.astype(jnp.float32) + mixed).astype(jnp.bfloat16)
    block_out = lax.all_to_all(block_rows, "col", split_axis=0, concat_axis=1, tiled=True)
    grad_out = lax.dot_general(
        act_all, upstream_all, (((0,), (0,)), ((), ())), preferred_element_type=jnp.float32
    )
    grad_in = lax.dot_general(
        tokens_all, dpre_all, (((0,), (0,)), ((), ())), preferred_element_type=jnp.float32
    )
    grad_tokens = (cotangent.astype(jnp.float32) + back).astype(jnp.bfloat16)
    return (block_out, grad_tokens, grad_in, grad_out)


def solution(mesh):
    in_specs = (P("row", "col"), P("col", "row"), P("row", "col"), P("row", "col"))
    out_specs = (P(("row", "col"), None), P("row", "col"), P("col", "row"), P("row", "col"))
    return jax.shard_map(local, mesh=mesh, in_specs=in_specs, out_specs=out_specs, check_vma=False)
```

```python
import jax
import jax.numpy as jnp
from jax import lax
from jax.sharding import PartitionSpec as P
import functools
from jax.experimental import pallas as pl
from jax.experimental.pallas import tpu as pltpu

MESH = pl.DeviceIdType.MESH


def _col_ids(nx):
    me = lax.axis_index("col")
    x = me // 2
    k = me % 2
    d = 1 - 2 * k
    nxt = lax.rem(x + nx + d, nx)
    prv = lax.rem(x + nx - d, nx)
    return x, k, d, nxt, prv


def _greet(row, k, x, nxt, prv):
    barrier = pltpu.get_barrier_semaphore()
    for peer in (2 * x + 1 - k, 2 * nxt + k, 2 * prv + k):
        pl.semaphore_signal(barrier, inc=1, device_id=(row, peer), device_id_type=MESH)
    pl.semaphore_wait(barrier, 3)


def _rs_body(nx, narr, parts, outs, recv1, sendbuf, recv2, s1, r1, s2, r2):
    row = lax.axis_index("row")
    x, k, d, nxt, prv = _col_ids(nx)
    partner = (row, 2 * x + 1 - k)
    nextdev = (row, 2 * nxt + k)

    def order(j, sign):
        if j == nx - 1:
            return x
        return lax.rem(x + 4 * nx + sign * d * (j + 1), nx)

    first = []
    for j in range(nx):
        for a in range(narr):
            cp = pltpu.make_async_remote_copy(
                src_ref=parts[a].at[2 * order(j, 1) + 1 - k], dst_ref=recv1.at[a, j],
                send_sem=s1.at[a, j], recv_sem=r1.at[a, j],
                device_id=partner, device_id_type=MESH)
            cp.start()
            first.append(cp)

    def chip_sum(a, j):
        first[j * narr + a].wait_recv()
        own = parts[a][2 * order(j, -1) + k].astype(jnp.float32)
        return own + recv1[a, j].astype(jnp.float32)

    pieces = 4
    span = outs[0].shape[0] // pieces
    ring = {}
    for step in range(nx - 1):
        for a in range(narr):
            first[step * narr + a].wait_recv()
        for q in range(pieces):
            rows = pl.ds(q * span, span)
            for a in range(narr):
                value = (parts[a][2 * order(step, -1) + k, rows, :].astype(jnp.float32)
                         + recv1[a, step, rows, :].astype(jnp.float32))
                if step == 0:
                    sendbuf[a, step, rows, :] = value.astype(sendbuf.dtype)
                else:
                    ring[(a, step - 1, q)].wait_recv()
                    sendbuf[a, step, rows, :] = (recv2[a, step - 1, rows, :].astype(jnp.float32)
                                                 + value).astype(sendbuf.dtype)
                cp = pltpu.make_async_remote_copy(
                    src_ref=sendbuf.at[a, step, rows], dst_ref=recv2.at[a, step, rows],
                    send_sem=s2.at[a, step, q], recv_sem=r2.at[a, step, q],
                    device_id=nextdev, device_id_type=MESH)
                cp.start()
                ring[(a, step, q)] = cp
    for a in range(narr):
        first[(nx - 1) * narr + a].wait_recv()
    for q in range(pieces):
        rows = pl.ds(q * span, span)
        sums = []
        for a in range(narr):
            value = (parts[a][2 * x + k, rows, :].astype(jnp.float32)
                     + recv1[a, nx - 1, rows, :].astype(jnp.float32))
            ring[(a, nx - 2, q)].wait_recv()
            sums.append(recv2[a, nx - 2, rows, :].astype(jnp.float32) + value)
        pre, dact = sums
        cdf = 0.5 * (1.0 + jax.scipy.special.erf(pre * 0.7071067811865476))
        outs[0][rows, :] = (pre * cdf).astype(outs[0].dtype)
        outs[1][rows, :] = (dact * gelu_grad(pre)).astype(outs[1].dtype)
    for cp in first:
        cp.wait_send()
    for cp in ring.values():
        cp.wait_send()


def _col_kernel(nx, narr, *refs):
    parts = refs[:narr]
    weights = refs[narr:2 * narr]
    outs = refs[2 * narr:3 * narr]
    prods = refs[3 * narr:4 * narr]
    scratch = refs[4 * narr:]
    row = lax.axis_index("row")
    x, k, d, nxt, prv = _col_ids(nx)
    _greet(row, k, x, nxt, prv)
    own = [o.at[2 * x + k] for o in outs]
    _rs_body(nx, narr, parts, own, *scratch[:7])
    _ag_body(nx, narr, own, weights, outs, prods, *scratch[7:])


def col_exchange(arrays, weights, cid):
    n = lax.axis_size("col")
    nx = n // 2
    narr = len(arrays)
    rows = arrays[0].shape[0] // n
    cols = arrays[0].shape[1]
    width = weights[0].shape[1]
    parts = [a.reshape(n, rows, cols) for a in arrays]
    res = pl.pallas_call(
        functools.partial(_col_kernel, nx, narr),
        out_shape=[jax.ShapeDtypeStruct((n, rows, cols), jnp.bfloat16)] * narr
        + [jax.ShapeDtypeStruct((n, rows, width), jnp.bfloat16)] * narr,
        in_specs=[pl.BlockSpec(memory_space=pltpu.VMEM)] * (2 * narr),
        out_specs=[pl.BlockSpec(memory_space=pltpu.VMEM)] * (2 * narr),
        scratch_shapes=[
            pltpu.VMEM((narr, nx, rows, cols), jnp.bfloat16),
            pltpu.VMEM((narr, nx - 1, rows, cols), jnp.bfloat16),
            pltpu.VMEM((narr, nx - 1, rows, cols), jnp.bfloat16),
            pltpu.SemaphoreType.DMA((narr, nx)),
            pltpu.SemaphoreType.DMA((narr, nx)),
            pltpu.SemaphoreType.DMA((narr, nx - 1, 4)),
            pltpu.SemaphoreType.DMA((narr, nx - 1, 4)),
            pltpu.SemaphoreType.DMA((narr, nx)),
            pltpu.SemaphoreType.DMA((narr, nx)),
            pltpu.SemaphoreType.DMA((narr, nx)),
            pltpu.SemaphoreType.DMA((narr, nx)),
        ],
        compiler_params=pltpu.CompilerParams(collective_id=cid, has_side_effects=True,
                                             vmem_limit_bytes=64 * 1024 * 1024),
    )(*parts, *weights)
    gathered = [o.reshape(n * rows, cols) for o in res[:narr]]
    products = [o.reshape(n * rows, width) for o in res[narr:]]
    return gathered, products


def _ag_body(nx, narr, chunks, weights, outs, prods, sr, rr, sc, rc):
    row = lax.axis_index("row")
    x, k, d, nxt, prv = _col_ids(nx)
    me = 2 * x + k
    partner = (row, 2 * x + 1 - k)
    nextdev = (row, 2 * nxt + k)

    def product(a, slot):
        if a == 0:
            value = jnp.dot(outs[a][slot], weights[a][...], preferred_element_type=jnp.float32)
        else:
            value = lax.dot_general(outs[a][slot], weights[a][...], (((1,), (1,)), ((), ())),
                                    preferred_element_type=jnp.float32)
        prods[a][slot] = value.astype(prods[a].dtype)

    ring, core = [], []
    for step in range(nx):
        for a in range(narr):
            src_x = lax.rem(x + 4 * nx - d * step, nx)
            slot = 2 * src_x + k
            if step > 0:
                ring[(step - 1) * narr + a].wait_recv()
            src = chunks[a] if step == 0 else outs[a].at[slot]
            if step < nx - 1:
                cp = pltpu.make_async_remote_copy(
                    src_ref=src, dst_ref=outs[a].at[slot],
                    send_sem=sr.at[a, step], recv_sem=rr.at[a, step],
                    device_id=nextdev, device_id_type=MESH)
                cp.start()
                ring.append(cp)
            cc = pltpu.make_async_remote_copy(
                src_ref=src, dst_ref=outs[a].at[slot],
                send_sem=sc.at[a, step], recv_sem=rc.at[a, step],
                device_id=partner, device_id_type=MESH)
            cc.start()
            core.append(cc)
        for a in range(narr):
            product(a, 2 * lax.rem(x + 4 * nx - d * step, nx) + k)
        if step > 0:
            for a in range(narr):
                core[(step - 1) * narr + a].wait()
            for a in range(narr):
                product(a, 2 * lax.rem(x + 4 * nx + d * (step - 1), nx) + 1 - k)
    for cp in ring:
        cp.wait_send()
    for a in range(narr):
        core[(nx - 1) * narr + a].wait()
    for a in range(narr):
        product(a, 2 * lax.rem(x + 4 * nx + d * (nx - 1), nx) + 1 - k)


def _row_ids():
    me = lax.axis_index("row")
    y = me // 4
    z = me % 4
    k = lax.axis_index("col") % 2
    d = 1 - 2 * k
    return y, z, d


def _row_ag_kernel(ny, *refs):
    ins = refs[:2]
    weights = refs[2:4]
    outs = refs[4:6]
    terms = refs[6:8]
    sa, sb, rsem = refs[8:]

    def product(a, slot):
        if a == 0:
            value = jnp.dot(outs[a][slot], weights[a][...], preferred_element_type=jnp.float32)
        else:
            value = lax.dot_general(outs[a][slot], weights[a][...], (((1,), (1,)), ((), ())),
                                    preferred_element_type=jnp.float32)
        terms[a][slot] = value.astype(terms[a].dtype)

    col = lax.axis_index("col")
    y, z, d = _row_ids()
    me = y * 4 + z
    barrier = pltpu.get_barrier_semaphore()
    peers = (y * 4 + lax.rem(z + 4 + d, 4), y * 4 + lax.rem(z + 4 - d, 4),
             lax.rem(y + ny + d, ny) * 4 + z, lax.rem(y + ny - d, ny) * 4 + z)
    for p in peers:
        pl.semaphore_signal(barrier, inc=1, device_id=(p, col), device_id_type=MESH)
    pl.semaphore_wait(barrier, 4)
    geo = []
    for a in range(2):
        if a == 0:
            na, nb = 4, ny
            pos_a, pos_b = z, y
            slot_of = lambda pa, pb: pb * 4 + pa
        else:
            na, nb = ny, 4
            pos_a, pos_b = y, z
            slot_of = lambda pa, pb: pa * 4 + pb
        geo.append((na, nb, pos_a, pos_b, slot_of))
        outs[a][me] = ins[a][...]

    def dev(a, pa, pb):
        return (geo[a][4](pa, pb), col)

    def send(a, src, slot, target, sem):
        cp = pltpu.make_async_remote_copy(
            src_ref=src, dst_ref=outs[a].at[slot], send_sem=sem, recv_sem=rsem.at[a, slot],
            device_id=target, device_id_type=MESH)
        cp.start()
        return cp

    def wait_in(a, slot):
        pltpu.make_async_remote_copy(
            src_ref=ins[a], dst_ref=outs[a].at[slot], send_sem=sa.at[a, 0], recv_sem=rsem.at[a, slot],
            device_id=(peers[0], col), device_id_type=MESH).wait_recv()

    sends = []
    for a in range(2):
        na, nb, pa, pb, slot_of = geo[a]
        next_a = dev(a, lax.rem(pa + na + d, na), pb)
        next_b = dev(a, pa, lax.rem(pb + nb + d, nb))
        sends.append(send(a, ins[a], me, next_a, sa.at[a, 0]))
        sends.append(send(a, ins[a], me, next_b, sb.at[a, 0, 0]))
    for a in range(2):
        product(a, me)
    for s in range(1, 4):
        for a in range(2):
            na, nb, pa, pb, slot_of = geo[a]
            next_a = dev(a, lax.rem(pa + na + d, na), pb)
            next_b = dev(a, pa, lax.rem(pb + nb + d, nb))
            slot = slot_of(lax.rem(pa + 4 * na - d * s, na), pb)
            wait_in(a, slot)
            if s < na - 1:
                sends.append(send(a, outs[a].at[slot], slot, next_a, sa.at[a, s]))
            sends.append(send(a, outs[a].at[slot], slot, next_b, sb.at[a, 0, s]))
            product(a, slot)
    for t in range(1, 4):
        for j in range(4):
            for a in range(2):
                na, nb, pa, pb, slot_of = geo[a]
                next_b = dev(a, pa, lax.rem(pb + nb + d, nb))
                slot = slot_of(lax.rem(pa + 4 * na - d * j, na), lax.rem(pb + 4 * nb - d * t, nb))
                wait_in(a, slot)
                if t < nb - 1:
                    sends.append(send(a, outs[a].at[slot], slot, next_b, sb.at[a, t, j]))
                product(a, slot)
    for cp in sends:
        cp.wait_send()


def row_all_gather(first, second, w_first, w_second, cid):
    n = lax.axis_size("row")
    ny = n // 4
    rows, cols = first.shape
    width = w_first.shape[1]
    outs = pl.pallas_call(
        functools.partial(_row_ag_kernel, ny),
        out_shape=[jax.ShapeDtypeStruct((n, rows, cols), first.dtype)] * 2
        + [jax.ShapeDtypeStruct((n, rows, width), jnp.bfloat16)] * 2,
        in_specs=[pl.BlockSpec(memory_space=pltpu.VMEM)] * 4,
        out_specs=[pl.BlockSpec(memory_space=pltpu.VMEM)] * 4,
        scratch_shapes=[
            pltpu.SemaphoreType.DMA((2, 4)),
            pltpu.SemaphoreType.DMA((2, 4, 4)),
            pltpu.SemaphoreType.DMA((2, n)),
        ],
        compiler_params=pltpu.CompilerParams(collective_id=cid, has_side_effects=True,
                                             vmem_limit_bytes=64 * 1024 * 1024),
    )(first, second, w_first, w_second)
    return [o.reshape(n * rows, o.shape[2]) for o in outs]


def _row_rs_kernel(ny, *refs):
    ins = refs[:2]
    outs = refs[2:4]
    sb1, rb1, ssum, sb2, rb2, s1, r1, s2, r2 = refs[4:]
    col = lax.axis_index("col")
    y, z, d = _row_ids()
    barrier = pltpu.get_barrier_semaphore()
    peers = (y * 4 + lax.rem(z + 4 + d, 4), y * 4 + lax.rem(z + 4 - d, 4),
             lax.rem(y + ny + d, ny) * 4 + z, lax.rem(y + ny - d, ny) * 4 + z)
    for p in peers:
        pl.semaphore_signal(barrier, inc=1, device_id=(p, col), device_id_type=MESH)
    pl.semaphore_wait(barrier, 4)
    geo = [(4, ny, z, y, lambda pa, pb: pb * 4 + pa), (ny, 4, y, z, lambda pa, pb: pa * 4 + pb)]

    def dev(a, pa, pb):
        return (geo[a][4](pa, pb), col)

    def send(src, dst, ssem, rsem, target):
        cp = pltpu.make_async_remote_copy(src_ref=src, dst_ref=dst, send_sem=ssem, recv_sem=rsem,
                                          device_id=target, device_id_type=MESH)
        cp.start()
        return cp

    sends = []
    first = {}
    for s in range(4 - 1):
        for bq in range(4):
            for a in range(2):
                na, nb, pa, pb, slot_of = geo[a]
                slot = slot_of(lax.rem(pa + 4 * na - d * (s + 1), na), bq)
                if s == 0:
                    src = ins[a].at[slot]
                else:
                    first[(a, s - 1, bq)].wait_recv()
                    sb1[a, s, bq] = (rb1[a, s - 1, bq].astype(jnp.float32)
                                     + ins[a][slot].astype(jnp.float32)).astype(sb1.dtype)
                    src = sb1.at[a, s, bq]
                cp = send(src, rb1.at[a, s, bq], s1.at[a, s, bq], r1.at[a, s, bq],
                          dev(a, lax.rem(pa + na + d, na), pb))
                sends.append(cp)
                first[(a, s, bq)] = cp
    for bq in range(4):
        for a in range(2):
            na, nb, pa, pb, slot_of = geo[a]
            first[(a, 2, bq)].wait_recv()
            ssum[a, bq] = rb1[a, 2, bq].astype(jnp.float32) + ins[a][slot_of(pa, bq)].astype(jnp.float32)
    second = [[] for _ in range(2)]
    for t in range(4 - 1):
        for a in range(2):
            na, nb, pa, pb, slot_of = geo[a]
            pos = lax.rem(pb + 4 * nb - d * (t + 1), nb)
            if t == 0:
                sb2[a, t] = ssum[a, pos].astype(sb2.dtype)
            else:
                sb2[a, t] = (rb2[a, t - 1].astype(jnp.float32) + ssum[a, pos]).astype(sb2.dtype)
            cp = send(sb2.at[a, t], rb2.at[a, t], s2.at[a, t], r2.at[a, t],
                      dev(a, pa, lax.rem(pb + nb + d, nb)))
            sends.append(cp)
            second[a].append(cp)
        for a in range(2):
            second[a][t].wait_recv()
    for a in range(2):
        na, nb, pa, pb, slot_of = geo[a]
        outs[a][...] = rb2[a, 2].astype(jnp.float32) + ssum[a, pb]
    for cp in sends:
        cp.wait_send()


def row_reduce_scatter(first, second, cid):
    n = lax.axis_size("row")
    ny = n // 4
    rows, cols = first.shape[0] // n, first.shape[1]
    ins = [v.reshape(n, rows, cols) for v in (first, second)]
    return pl.pallas_call(
        functools.partial(_row_rs_kernel, ny),
        out_shape=[jax.ShapeDtypeStruct((rows, cols), jnp.float32)] * 2,
        in_specs=[pl.BlockSpec(memory_space=pltpu.VMEM)] * 2,
        out_specs=[pl.BlockSpec(memory_space=pltpu.VMEM)] * 2,
        scratch_shapes=[
            pltpu.VMEM((2, 3, 4, rows, cols), jnp.bfloat16),
            pltpu.VMEM((2, 3, 4, rows, cols), jnp.bfloat16),
            pltpu.VMEM((2, 4, rows, cols), jnp.float32),
            pltpu.VMEM((2, 3, rows, cols), jnp.bfloat16),
            pltpu.VMEM((2, 3, rows, cols), jnp.bfloat16),
            pltpu.SemaphoreType.DMA((2, 3, 4)),
            pltpu.SemaphoreType.DMA((2, 3, 4)),
            pltpu.SemaphoreType.DMA((2, 3)),
            pltpu.SemaphoreType.DMA((2, 3)),
        ],
        compiler_params=pltpu.CompilerParams(collective_id=cid, has_side_effects=True,
                                             vmem_limit_bytes=64 * 1024 * 1024),
    )(*ins)


def gelu_grad(value):
    cdf = 0.5 * (1.0 + jax.scipy.special.erf(value * 0.7071067811865476))
    pdf = jnp.exp(-0.5 * value * value) * 0.3989422804014327
    return cdf + value * pdf


def token_panel(local_rows):
    return lax.all_gather(local_rows, "row", axis=0, tiled=True)


def token_panel_a2a(local_rows):
    n = lax.axis_size("row")
    copies = jnp.broadcast_to(local_rows[None], (n,) + local_rows.shape)
    copies = copies.reshape(n * local_rows.shape[0], local_rows.shape[1])
    return lax.all_to_all(copies, "row", split_axis=0, concat_axis=0, tiled=True)


def hidden_panel(local_rows):
    return lax.all_gather(local_rows, "col", axis=0, tiled=True)


def contract_last(left, right):
    return lax.dot_general(
        left, right, (((1,), (1,)), ((), ())), preferred_element_type=jnp.float32
    )


def width_split(left_all, right, transposed):
    if transposed:
        term = contract_last(left_all, right)
    else:
        term = jnp.dot(left_all, right, preferred_element_type=jnp.float32)
    return lax.psum_scatter(
        term.astype(jnp.bfloat16), "col", scatter_dimension=0, tiled=True
    ).astype(jnp.float32)


def unit_sum(left_all, right, transposed):
    n = lax.axis_size("row")
    if transposed:
        term = contract_last(left_all, right)
    else:
        term = jnp.dot(left_all, right, preferred_element_type=jnp.float32)
    pieces = term.astype(jnp.bfloat16).reshape(n, term.shape[0] // n, term.shape[1])
    pieces = lax.all_to_all(pieces, "row", split_axis=0, concat_axis=0, tiled=True)
    return jnp.sum(pieces.astype(jnp.float32), axis=0)


def row_sum(term):
    n = lax.axis_size("row")
    pieces = term.reshape(n, term.shape[0] // n, term.shape[1])
    pieces = lax.all_to_all(pieces, "row", split_axis=0, concat_axis=0, tiled=True)
    return jnp.sum(pieces.astype(jnp.float32), axis=0)


def local(tokens, w_in, w_out, cotangent):
    tokens_all, upstream_all, pre_term, dact_term = row_all_gather(tokens, cotangent, w_in, w_out, 3)
    (act_all, dpre_all), (mixed_term, back_term) = col_exchange([pre_term, dact_term], [w_out, w_in], 1)
    mixed, back = row_reduce_scatter(mixed_term, back_term, 4)
    block_rows = (tokens.astype(jnp.float32) + mixed).astype(jnp.bfloat16)
    block_out = lax.all_to_all(block_rows, "col", split_axis=0, concat_axis=1, tiled=True)
    grad_out = lax.dot_general(
        act_all, upstream_all, (((0,), (0,)), ((), ())), preferred_element_type=jnp.float32
    )
    grad_in = lax.dot_general(
        tokens_all, dpre_all, (((0,), (0,)), ((), ())), preferred_element_type=jnp.float32
    )
    grad_tokens = (cotangent.astype(jnp.float32) + back).astype(jnp.bfloat16)
    return (block_out, grad_tokens, grad_in, grad_out)


def solution(mesh):
    in_specs = (P("row", "col"), P("col", "row"), P("row", "col"), P("row", "col"))
    out_specs = (P(("row", "col"), None), P("row", "col"), P("col", "row"), P("row", "col"))
    return jax.shard_map(local, mesh=mesh, in_specs=in_specs, out_specs=out_specs, check_vma=False)
```

```python
import jax
import jax.numpy as jnp
from jax import lax
from jax.sharding import PartitionSpec as P
import functools
from jax.experimental import pallas as pl
from jax.experimental.pallas import tpu as pltpu

MESH = pl.DeviceIdType.MESH


def _col_ids(nx):
    me = lax.axis_index("col")
    x = me // 2
    k = me % 2
    d = 1 - 2 * k
    nxt = lax.rem(x + nx + d, nx)
    prv = lax.rem(x + nx - d, nx)
    return x, k, d, nxt, prv


def _greet(row, k, x, nxt, prv):
    barrier = pltpu.get_barrier_semaphore()
    for peer in (2 * x + 1 - k, 2 * nxt + k, 2 * prv + k):
        pl.semaphore_signal(barrier, inc=1, device_id=(row, peer), device_id_type=MESH)
    pl.semaphore_wait(barrier, 3)


def _rs_body(nx, narr, parts, outs, recv1, sendbuf, recv2, s1, r1, s2, r2):
    row = lax.axis_index("row")
    x, k, d, nxt, prv = _col_ids(nx)
    partner = (row, 2 * x + 1 - k)
    nextdev = (row, 2 * nxt + k)

    def order(j, sign):
        if j == nx - 1:
            return x
        return lax.rem(x + 4 * nx + sign * d * (j + 1), nx)

    first = []
    for j in range(nx):
        for a in range(narr):
            cp = pltpu.make_async_remote_copy(
                src_ref=parts[a].at[2 * order(j, 1) + 1 - k], dst_ref=recv1.at[a, j],
                send_sem=s1.at[a, j], recv_sem=r1.at[a, j],
                device_id=partner, device_id_type=MESH)
            cp.start()
            first.append(cp)

    def chip_sum(a, j):
        first[j * narr + a].wait_recv()
        own = parts[a][2 * order(j, -1) + k].astype(jnp.float32)
        return own + recv1[a, j].astype(jnp.float32)

    pieces = 4
    span = outs[0].shape[0] // pieces
    ring = {}
    for step in range(nx - 1):
        for a in range(narr):
            first[step * narr + a].wait_recv()
        for q in range(pieces):
            rows = pl.ds(q * span, span)
            for a in range(narr):
                value = (parts[a][2 * order(step, -1) + k, rows, :].astype(jnp.float32)
                         + recv1[a, step, rows, :].astype(jnp.float32))
                if step == 0:
                    sendbuf[a, step, rows, :] = value.astype(sendbuf.dtype)
                else:
                    ring[(a, step - 1, q)].wait_recv()
                    sendbuf[a, step, rows, :] = (recv2[a, step - 1, rows, :].astype(jnp.float32)
                                                 + value).astype(sendbuf.dtype)
                cp = pltpu.make_async_remote_copy(
                    src_ref=sendbuf.at[a, step, rows], dst_ref=recv2.at[a, step, rows],
                    send_sem=s2.at[a, step, q], recv_sem=r2.at[a, step, q],
                    device_id=nextdev, device_id_type=MESH)
                cp.start()
                ring[(a, step, q)] = cp
    for a in range(narr):
        first[(nx - 1) * narr + a].wait_recv()
    for q in range(pieces):
        rows = pl.ds(q * span, span)
        sums = []
        for a in range(narr):
            value = (parts[a][2 * x + k, rows, :].astype(jnp.float32)
                     + recv1[a, nx - 1, rows, :].astype(jnp.float32))
            ring[(a, nx - 2, q)].wait_recv()
            sums.append(recv2[a, nx - 2, rows, :].astype(jnp.float32) + value)
        pre, dact = sums
        cdf = 0.5 * (1.0 + jax.scipy.special.erf(pre * 0.7071067811865476))
        outs[0][rows, :] = (pre * cdf).astype(outs[0].dtype)
        outs[1][rows, :] = (dact * gelu_grad(pre)).astype(outs[1].dtype)
    for cp in first:
        cp.wait_send()
    for cp in ring.values():
        cp.wait_send()


def _col_kernel(nx, ny, narr, *refs):
    parts = refs[:narr]
    weights = refs[narr:2 * narr]
    outs = refs[2 * narr:3 * narr]
    sums = refs[3 * narr:4 * narr]
    prods = refs[4 * narr:5 * narr]
    scratch = refs[5 * narr:]
    row = lax.axis_index("row")
    x, k, d, nxt, prv = _col_ids(nx)
    barrier = pltpu.get_barrier_semaphore()
    for peer in (2 * x + 1 - k, 2 * nxt + k, 2 * prv + k):
        pl.semaphore_signal(barrier, inc=1, device_id=(row, peer), device_id_type=MESH)
    y, z, dr = _row_ids()
    for p in (y * 4 + lax.rem(z + 4 + dr, 4), y * 4 + lax.rem(z + 4 - dr, 4),
              lax.rem(y + ny + dr, ny) * 4 + z, lax.rem(y + ny - dr, ny) * 4 + z):
        pl.semaphore_signal(barrier, inc=1, device_id=(p, 2 * x + k), device_id_type=MESH)
    pl.semaphore_wait(barrier, 7)
    own = [o.at[2 * x + k] for o in outs]
    _rs_body(nx, narr, parts, own, *scratch[:7])
    _ag_body(nx, narr, own, weights, outs, prods, *scratch[7:11])
    _row_rs_body(ny, prods, sums, *scratch[11:])


def col_exchange(arrays, weights, cid):
    n = lax.axis_size("col")
    nx = n // 2
    narr = len(arrays)
    rows = arrays[0].shape[0] // n
    cols = arrays[0].shape[1]
    width = weights[0].shape[1]
    parts = [a.reshape(n, rows, cols) for a in arrays]
    nr = lax.axis_size("row")
    ny = nr // 4
    piece = n * rows // nr
    res = pl.pallas_call(
        functools.partial(_col_kernel, nx, ny, narr),
        out_shape=[jax.ShapeDtypeStruct((n, rows, cols), jnp.bfloat16)] * narr
        + [jax.ShapeDtypeStruct((piece, width), jnp.float32)] * narr,
        in_specs=[pl.BlockSpec(memory_space=pltpu.VMEM)] * (2 * narr),
        out_specs=[pl.BlockSpec(memory_space=pltpu.VMEM)] * (2 * narr),
        scratch_shapes=[pltpu.VMEM((n, rows, width), jnp.bfloat16)] * narr + [
            pltpu.VMEM((narr, nx, rows, cols), jnp.bfloat16),
            pltpu.VMEM((narr, nx - 1, rows, cols), jnp.bfloat16),
            pltpu.VMEM((narr, nx - 1, rows, cols), jnp.bfloat16),
            pltpu.SemaphoreType.DMA((narr, nx)),
            pltpu.SemaphoreType.DMA((narr, nx)),
            pltpu.SemaphoreType.DMA((narr, nx - 1, 4)),
            pltpu.SemaphoreType.DMA((narr, nx - 1, 4)),
            pltpu.SemaphoreType.DMA((narr, nx)),
            pltpu.SemaphoreType.DMA((narr, nx)),
            pltpu.SemaphoreType.DMA((narr, nx)),
            pltpu.SemaphoreType.DMA((narr, nx)),
            pltpu.VMEM((2, 3, 4, piece, width), jnp.bfloat16),
            pltpu.VMEM((2, 3, 4, piece, width), jnp.bfloat16),
            pltpu.VMEM((2, 4, piece, width), jnp.float32),
            pltpu.VMEM((2, 3, piece, width), jnp.bfloat16),
            pltpu.VMEM((2, 3, piece, width), jnp.bfloat16),
            pltpu.SemaphoreType.DMA((2, 3, 4)),
            pltpu.SemaphoreType.DMA((2, 3, 4)),
            pltpu.SemaphoreType.DMA((2, 3)),
            pltpu.SemaphoreType.DMA((2, 3)),
        ],
        compiler_params=pltpu.CompilerParams(collective_id=cid, has_side_effects=True,
                                             vmem_limit_bytes=64 * 1024 * 1024),
    )(*parts, *weights)
    gathered = [o.reshape(n * rows, cols) for o in res[:narr]]
    return gathered, res[narr:]


def _ag_body(nx, narr, chunks, weights, outs, prods, sr, rr, sc, rc):
    row = lax.axis_index("row")
    x, k, d, nxt, prv = _col_ids(nx)
    me = 2 * x + k
    partner = (row, 2 * x + 1 - k)
    nextdev = (row, 2 * nxt + k)

    def product(a, slot):
        if a == 0:
            value = jnp.dot(outs[a][slot], weights[a][...], preferred_element_type=jnp.float32)
        else:
            value = lax.dot_general(outs[a][slot], weights[a][...], (((1,), (1,)), ((), ())),
                                    preferred_element_type=jnp.float32)
        prods[a][slot] = value.astype(prods[a].dtype)

    ring, core = [], []
    for step in range(nx):
        for a in range(narr):
            src_x = lax.rem(x + 4 * nx - d * step, nx)
            slot = 2 * src_x + k
            if step > 0:
                ring[(step - 1) * narr + a].wait_recv()
            src = chunks[a] if step == 0 else outs[a].at[slot]
            if step < nx - 1:
                cp = pltpu.make_async_remote_copy(
                    src_ref=src, dst_ref=outs[a].at[slot],
                    send_sem=sr.at[a, step], recv_sem=rr.at[a, step],
                    device_id=nextdev, device_id_type=MESH)
                cp.start()
                ring.append(cp)
            cc = pltpu.make_async_remote_copy(
                src_ref=src, dst_ref=outs[a].at[slot],
                send_sem=sc.at[a, step], recv_sem=rc.at[a, step],
                device_id=partner, device_id_type=MESH)
            cc.start()
            core.append(cc)
        for a in range(narr):
            product(a, 2 * lax.rem(x + 4 * nx - d * step, nx) + k)
        if step > 0:
            for a in range(narr):
                core[(step - 1) * narr + a].wait()
            for a in range(narr):
                product(a, 2 * lax.rem(x + 4 * nx + d * (step - 1), nx) + 1 - k)
    for cp in ring:
        cp.wait_send()
    for a in range(narr):
        core[(nx - 1) * narr + a].wait()
    for a in range(narr):
        product(a, 2 * lax.rem(x + 4 * nx + d * (nx - 1), nx) + 1 - k)


def _row_ids():
    me = lax.axis_index("row")
    y = me // 4
    z = me % 4
    k = lax.axis_index("col") % 2
    d = 1 - 2 * k
    return y, z, d


def _row_ag_kernel(ny, *refs):
    ins = refs[:2]
    weights = refs[2:4]
    outs = refs[4:6]
    terms = refs[6:8]
    sa, sb, rsem = refs[8:]

    def product(a, slot):
        if a == 0:
            value = jnp.dot(outs[a][slot], weights[a][...], preferred_element_type=jnp.float32)
        else:
            value = lax.dot_general(outs[a][slot], weights[a][...], (((1,), (1,)), ((), ())),
                                    preferred_element_type=jnp.float32)
        terms[a][slot] = value.astype(terms[a].dtype)

    col = lax.axis_index("col")
    y, z, d = _row_ids()
    me = y * 4 + z
    barrier = pltpu.get_barrier_semaphore()
    peers = (y * 4 + lax.rem(z + 4 + d, 4), y * 4 + lax.rem(z + 4 - d, 4),
             lax.rem(y + ny + d, ny) * 4 + z, lax.rem(y + ny - d, ny) * 4 + z)
    for p in peers:
        pl.semaphore_signal(barrier, inc=1, device_id=(p, col), device_id_type=MESH)
    pl.semaphore_wait(barrier, 4)
    geo = []
    for a in range(2):
        if a == 0:
            na, nb = 4, ny
            pos_a, pos_b = z, y
            slot_of = lambda pa, pb: pb * 4 + pa
        else:
            na, nb = ny, 4
            pos_a, pos_b = y, z
            slot_of = lambda pa, pb: pa * 4 + pb
        geo.append((na, nb, pos_a, pos_b, slot_of))
        outs[a][me] = ins[a][...]

    def dev(a, pa, pb):
        return (geo[a][4](pa, pb), col)

    def send(a, src, slot, target, sem):
        cp = pltpu.make_async_remote_copy(
            src_ref=src, dst_ref=outs[a].at[slot], send_sem=sem, recv_sem=rsem.at[a, slot],
            device_id=target, device_id_type=MESH)
        cp.start()
        return cp

    def wait_in(a, slot):
        pltpu.make_async_remote_copy(
            src_ref=ins[a], dst_ref=outs[a].at[slot], send_sem=sa.at[a, 0], recv_sem=rsem.at[a, slot],
            device_id=(peers[0], col), device_id_type=MESH).wait_recv()

    sends = []
    for a in range(2):
        na, nb, pa, pb, slot_of = geo[a]
        next_a = dev(a, lax.rem(pa + na + d, na), pb)
        next_b = dev(a, pa, lax.rem(pb + nb + d, nb))
        sends.append(send(a, ins[a], me, next_a, sa.at[a, 0]))
        sends.append(send(a, ins[a], me, next_b, sb.at[a, 0, 0]))
    for a in range(2):
        product(a, me)
    for s in range(1, 4):
        for a in range(2):
            na, nb, pa, pb, slot_of = geo[a]
            next_a = dev(a, lax.rem(pa + na + d, na), pb)
            next_b = dev(a, pa, lax.rem(pb + nb + d, nb))
            slot = slot_of(lax.rem(pa + 4 * na - d * s, na), pb)
            wait_in(a, slot)
            if s < na - 1:
                sends.append(send(a, outs[a].at[slot], slot, next_a, sa.at[a, s]))
            sends.append(send(a, outs[a].at[slot], slot, next_b, sb.at[a, 0, s]))
            product(a, slot)
    for t in range(1, 4):
        for j in range(4):
            for a in range(2):
                na, nb, pa, pb, slot_of = geo[a]
                next_b = dev(a, pa, lax.rem(pb + nb + d, nb))
                slot = slot_of(lax.rem(pa + 4 * na - d * j, na), lax.rem(pb + 4 * nb - d * t, nb))
                wait_in(a, slot)
                if t < nb - 1:
                    sends.append(send(a, outs[a].at[slot], slot, next_b, sb.at[a, t, j]))
                product(a, slot)
    for cp in sends:
        cp.wait_send()


def row_all_gather(first, second, w_first, w_second, cid):
    n = lax.axis_size("row")
    ny = n // 4
    rows, cols = first.shape
    width = w_first.shape[1]
    outs = pl.pallas_call(
        functools.partial(_row_ag_kernel, ny),
        out_shape=[jax.ShapeDtypeStruct((n, rows, cols), first.dtype)] * 2
        + [jax.ShapeDtypeStruct((n, rows, width), jnp.bfloat16)] * 2,
        in_specs=[pl.BlockSpec(memory_space=pltpu.VMEM)] * 4,
        out_specs=[pl.BlockSpec(memory_space=pltpu.VMEM)] * 4,
        scratch_shapes=[
            pltpu.SemaphoreType.DMA((2, 4)),
            pltpu.SemaphoreType.DMA((2, 4, 4)),
            pltpu.SemaphoreType.DMA((2, n)),
        ],
        compiler_params=pltpu.CompilerParams(collective_id=cid, has_side_effects=True,
                                             vmem_limit_bytes=64 * 1024 * 1024),
    )(first, second, w_first, w_second)
    return [o.reshape(n * rows, o.shape[2]) for o in outs]


def _piece(ref, slot):
    half = ref.shape[1] // 2
    return ref.at[slot // 2, pl.ds(pl.multiple_of((slot % 2) * half, half), half)]


def _row_rs_body(ny, ins, outs, sb1, rb1, ssum, sb2, rb2, s1, r1, s2, r2):
    col = lax.axis_index("col")
    y, z, d = _row_ids()
    geo = [(4, ny, z, y, lambda pa, pb: pb * 4 + pa), (ny, 4, y, z, lambda pa, pb: pa * 4 + pb)]

    def dev(a, pa, pb):
        return (geo[a][4](pa, pb), col)

    def send(src, dst, ssem, rsem, target):
        cp = pltpu.make_async_remote_copy(src_ref=src, dst_ref=dst, send_sem=ssem, recv_sem=rsem,
                                          device_id=target, device_id_type=MESH)
        cp.start()
        return cp

    sends = []
    first = {}
    for s in range(4 - 1):
        for bq in range(4):
            for a in range(2):
                na, nb, pa, pb, slot_of = geo[a]
                slot = slot_of(lax.rem(pa + 4 * na - d * (s + 1), na), bq)
                if s == 0:
                    src = _piece(ins[a], slot)
                else:
                    first[(a, s - 1, bq)].wait_recv()
                    sb1[a, s, bq] = (rb1[a, s - 1, bq].astype(jnp.float32)
                                     + _piece(ins[a], slot)[...].astype(jnp.float32)).astype(sb1.dtype)
                    src = sb1.at[a, s, bq]
                cp = send(src, rb1.at[a, s, bq], s1.at[a, s, bq], r1.at[a, s, bq],
                          dev(a, lax.rem(pa + na + d, na), pb))
                sends.append(cp)
                first[(a, s, bq)] = cp
    for bq in range(4):
        for a in range(2):
            na, nb, pa, pb, slot_of = geo[a]
            first[(a, 2, bq)].wait_recv()
            ssum[a, bq] = rb1[a, 2, bq].astype(jnp.float32) + _piece(ins[a], slot_of(pa, bq))[...].astype(jnp.float32)
    second = [[] for _ in range(2)]
    for t in range(4 - 1):
        for a in range(2):
            na, nb, pa, pb, slot_of = geo[a]
            pos = lax.rem(pb + 4 * nb - d * (t + 1), nb)
            if t == 0:
                sb2[a, t] = ssum[a, pos].astype(sb2.dtype)
            else:
                sb2[a, t] = (rb2[a, t - 1].astype(jnp.float32) + ssum[a, pos]).astype(sb2.dtype)
            cp = send(sb2.at[a, t], rb2.at[a, t], s2.at[a, t], r2.at[a, t],
                      dev(a, pa, lax.rem(pb + nb + d, nb)))
            sends.append(cp)
            second[a].append(cp)
        for a in range(2):
            second[a][t].wait_recv()
    for a in range(2):
        na, nb, pa, pb, slot_of = geo[a]
        outs[a][...] = rb2[a, 2].astype(jnp.float32) + ssum[a, pb]
    for cp in sends:
        cp.wait_send()


def gelu_grad(value):
    cdf = 0.5 * (1.0 + jax.scipy.special.erf(value * 0.7071067811865476))
    pdf = jnp.exp(-0.5 * value * value) * 0.3989422804014327
    return cdf + value * pdf


def token_panel(local_rows):
    return lax.all_gather(local_rows, "row", axis=0, tiled=True)


def token_panel_a2a(local_rows):
    n = lax.axis_size("row")
    copies = jnp.broadcast_to(local_rows[None], (n,) + local_rows.shape)
    copies = copies.reshape(n * local_rows.shape[0], local_rows.shape[1])
    return lax.all_to_all(copies, "row", split_axis=0, concat_axis=0, tiled=True)


def hidden_panel(local_rows):
    return lax.all_gather(local_rows, "col", axis=0, tiled=True)


def contract_last(left, right):
    return lax.dot_general(
        left, right, (((1,), (1,)), ((), ())), preferred_element_type=jnp.float32
    )


def width_split(left_all, right, transposed):
    if transposed:
        term = contract_last(left_all, right)
    else:
        term = jnp.dot(left_all, right, preferred_element_type=jnp.float32)
    return lax.psum_scatter(
        term.astype(jnp.bfloat16), "col", scatter_dimension=0, tiled=True
    ).astype(jnp.float32)


def unit_sum(left_all, right, transposed):
    n = lax.axis_size("row")
    if transposed:
        term = contract_last(left_all, right)
    else:
        term = jnp.dot(left_all, right, preferred_element_type=jnp.float32)
    pieces = term.astype(jnp.bfloat16).reshape(n, term.shape[0] // n, term.shape[1])
    pieces = lax.all_to_all(pieces, "row", split_axis=0, concat_axis=0, tiled=True)
    return jnp.sum(pieces.astype(jnp.float32), axis=0)


def row_sum(term):
    n = lax.axis_size("row")
    pieces = term.reshape(n, term.shape[0] // n, term.shape[1])
    pieces = lax.all_to_all(pieces, "row", split_axis=0, concat_axis=0, tiled=True)
    return jnp.sum(pieces.astype(jnp.float32), axis=0)


def local(tokens, w_in, w_out, cotangent):
    tokens_all, upstream_all, pre_term, dact_term = row_all_gather(tokens, cotangent, w_in, w_out, 3)
    (act_all, dpre_all), (mixed, back) = col_exchange([pre_term, dact_term], [w_out, w_in], 1)
    block_rows = (tokens.astype(jnp.float32) + mixed).astype(jnp.bfloat16)
    block_out = lax.all_to_all(block_rows, "col", split_axis=0, concat_axis=1, tiled=True)
    grad_out = lax.dot_general(
        act_all, upstream_all, (((0,), (0,)), ((), ())), preferred_element_type=jnp.float32
    )
    grad_in = lax.dot_general(
        tokens_all, dpre_all, (((0,), (0,)), ((), ())), preferred_element_type=jnp.float32
    )
    grad_tokens = (cotangent.astype(jnp.float32) + back).astype(jnp.bfloat16)
    return (block_out, grad_tokens, grad_in, grad_out)


def solution(mesh):
    in_specs = (P("row", "col"), P("col", "row"), P("row", "col"), P("row", "col"))
    out_specs = (P(("row", "col"), None), P("row", "col"), P("col", "row"), P("row", "col"))
    return jax.shard_map(local, mesh=mesh, in_specs=in_specs, out_specs=out_specs, check_vma=False)
```

```python
import jax
import jax.numpy as jnp
from jax import lax
from jax.sharding import PartitionSpec as P
import functools
from jax.experimental import pallas as pl
from jax.experimental.pallas import tpu as pltpu

MESH = pl.DeviceIdType.MESH


def _col_ids(nx):
    me = lax.axis_index("col")
    x = me // 2
    k = me % 2
    d = 1 - 2 * k
    nxt = lax.rem(x + nx + d, nx)
    prv = lax.rem(x + nx - d, nx)
    return x, k, d, nxt, prv


def _greet(row, k, x, nxt, prv):
    barrier = pltpu.get_barrier_semaphore()
    for peer in (2 * x + 1 - k, 2 * nxt + k, 2 * prv + k):
        pl.semaphore_signal(barrier, inc=1, device_id=(row, peer), device_id_type=MESH)
    pl.semaphore_wait(barrier, 3)


def _rs_body(nx, narr, parts, outs, recv1, sendbuf, recv2, s1, r1, s2, r2):
    row = lax.axis_index("row")
    x, k, d, nxt, prv = _col_ids(nx)
    partner = (row, 2 * x + 1 - k)
    nextdev = (row, 2 * nxt + k)

    def order(j, sign):
        if j == nx - 1:
            return x
        return lax.rem(x + 4 * nx + sign * d * (j + 1), nx)

    first = []
    for j in range(nx):
        for a in range(narr):
            cp = pltpu.make_async_remote_copy(
                src_ref=parts[a].at[2 * order(j, 1) + 1 - k], dst_ref=recv1.at[a, j],
                send_sem=s1.at[a, j], recv_sem=r1.at[a, j],
                device_id=partner, device_id_type=MESH)
            cp.start()
            first.append(cp)

    def chip_sum(a, j):
        first[j * narr + a].wait_recv()
        own = parts[a][2 * order(j, -1) + k].astype(jnp.float32)
        return own + recv1[a, j].astype(jnp.float32)

    pieces = 4
    span = outs[0].shape[0] // pieces
    ring = {}
    for step in range(nx - 1):
        for a in range(narr):
            first[step * narr + a].wait_recv()
        for q in range(pieces):
            rows = pl.ds(q * span, span)
            for a in range(narr):
                value = (parts[a][2 * order(step, -1) + k, rows, :].astype(jnp.float32)
                         + recv1[a, step, rows, :].astype(jnp.float32))
                if step == 0:
                    sendbuf[a, step, rows, :] = value.astype(sendbuf.dtype)
                else:
                    ring[(a, step - 1, q)].wait_recv()
                    sendbuf[a, step, rows, :] = (recv2[a, step - 1, rows, :].astype(jnp.float32)
                                                 + value).astype(sendbuf.dtype)
                cp = pltpu.make_async_remote_copy(
                    src_ref=sendbuf.at[a, step, rows], dst_ref=recv2.at[a, step, rows],
                    send_sem=s2.at[a, step, q], recv_sem=r2.at[a, step, q],
                    device_id=nextdev, device_id_type=MESH)
                cp.start()
                ring[(a, step, q)] = cp
    for a in range(narr):
        first[(nx - 1) * narr + a].wait_recv()
    for q in range(pieces):
        rows = pl.ds(q * span, span)
        sums = []
        for a in range(narr):
            value = (parts[a][2 * x + k, rows, :].astype(jnp.float32)
                     + recv1[a, nx - 1, rows, :].astype(jnp.float32))
            ring[(a, nx - 2, q)].wait_recv()
            sums.append(recv2[a, nx - 2, rows, :].astype(jnp.float32) + value)
        pre, dact = sums
        cdf = 0.5 * (1.0 + jax.scipy.special.erf(pre * 0.7071067811865476))
        outs[0][rows, :] = (pre * cdf).astype(outs[0].dtype)
        outs[1][rows, :] = (dact * gelu_grad(pre)).astype(outs[1].dtype)
    for cp in first:
        cp.wait_send()
    for cp in ring.values():
        cp.wait_send()


def _col_kernel(nx, ny, narr, *refs):
    tokens, cot, w_in, w_out = refs[:4]
    panels = refs[4:6]
    outs = refs[6:8]
    sums = refs[8:10]
    parts = refs[10:12]
    prods = refs[12:14]
    scratch = refs[14:]
    weights = [w_out, w_in]
    row = lax.axis_index("row")
    x, k, d, nxt, prv = _col_ids(nx)
    barrier = pltpu.get_barrier_semaphore()
    for peer in (2 * x + 1 - k, 2 * nxt + k, 2 * prv + k):
        pl.semaphore_signal(barrier, inc=1, device_id=(row, peer), device_id_type=MESH)
    y, z, dr = _row_ids()
    for p in (y * 4 + lax.rem(z + 4 + dr, 4), y * 4 + lax.rem(z + 4 - dr, 4),
              lax.rem(y + ny + dr, ny) * 4 + z, lax.rem(y + ny - dr, ny) * 4 + z):
        pl.semaphore_signal(barrier, inc=1, device_id=(p, 2 * x + k), device_id_type=MESH)
    pl.semaphore_wait(barrier, 7)
    _row_ag_body(ny, [tokens, cot], [w_in, w_out], panels, parts, *scratch[20:23])
    own = [o.at[2 * x + k] for o in outs]
    _rs_body(nx, narr, parts, own, *scratch[:7])
    _ag_body(nx, narr, own, weights, outs, prods, *scratch[7:11])
    _row_rs_body(ny, prods, sums, *scratch[11:20])


def fused_block(tokens, cotangent, w_in, w_out, cid):
    n = lax.axis_size("col")
    nx = n // 2
    narr = 2
    nr = lax.axis_size("row")
    ny = nr // 4
    piece, model = tokens.shape
    hidden = w_in.shape[1]
    rows = piece * nr // n
    cols = hidden
    width = model
    res = pl.pallas_call(
        functools.partial(_col_kernel, nx, ny, narr),
        out_shape=[jax.ShapeDtypeStruct((nr, piece, model), jnp.bfloat16)] * 2
        + [jax.ShapeDtypeStruct((n, rows, cols), jnp.bfloat16)] * narr
        + [jax.ShapeDtypeStruct((piece, width), jnp.float32)] * narr,
        in_specs=[pl.BlockSpec(memory_space=pltpu.VMEM)] * 4,
        out_specs=[pl.BlockSpec(memory_space=pltpu.VMEM)] * 6,
        scratch_shapes=[pltpu.VMEM((n, rows, cols), jnp.bfloat16)] * narr
        + [pltpu.VMEM((n, rows, width), jnp.bfloat16)] * narr + [
            pltpu.VMEM((narr, nx, rows, cols), jnp.bfloat16),
            pltpu.VMEM((narr, nx - 1, rows, cols), jnp.bfloat16),
            pltpu.VMEM((narr, nx - 1, rows, cols), jnp.bfloat16),
            pltpu.SemaphoreType.DMA((narr, nx)),
            pltpu.SemaphoreType.DMA((narr, nx)),
            pltpu.SemaphoreType.DMA((narr, nx - 1, 4)),
            pltpu.SemaphoreType.DMA((narr, nx - 1, 4)),
            pltpu.SemaphoreType.DMA((narr, nx)),
            pltpu.SemaphoreType.DMA((narr, nx)),
            pltpu.SemaphoreType.DMA((narr, nx)),
            pltpu.SemaphoreType.DMA((narr, nx)),
            pltpu.VMEM((2, 3, 4, piece, width), jnp.bfloat16),
            pltpu.VMEM((2, 3, 4, piece, width), jnp.bfloat16),
            pltpu.VMEM((2, 4, piece, width), jnp.float32),
            pltpu.VMEM((2, 3, piece, width), jnp.bfloat16),
            pltpu.VMEM((2, 3, piece, width), jnp.bfloat16),
            pltpu.SemaphoreType.DMA((2, 3, 4)),
            pltpu.SemaphoreType.DMA((2, 3, 4)),
            pltpu.SemaphoreType.DMA((2, 3)),
            pltpu.SemaphoreType.DMA((2, 3)),
            pltpu.SemaphoreType.DMA((2, 4)),
            pltpu.SemaphoreType.DMA((2, 4, 4)),
            pltpu.SemaphoreType.DMA((2, nr)),
        ],
        compiler_params=pltpu.CompilerParams(collective_id=cid, has_side_effects=True,
                                             vmem_limit_bytes=64 * 1024 * 1024),
    )(tokens, cotangent, w_in, w_out)
    return ([o.reshape(nr * piece, model) for o in res[:2]]
            + [o.reshape(n * rows, cols) for o in res[2:4]] + list(res[4:]))


def _ag_body(nx, narr, chunks, weights, outs, prods, sr, rr, sc, rc):
    row = lax.axis_index("row")
    x, k, d, nxt, prv = _col_ids(nx)
    me = 2 * x + k
    partner = (row, 2 * x + 1 - k)
    nextdev = (row, 2 * nxt + k)

    def product(a, slot):
        if a == 0:
            value = jnp.dot(outs[a][slot], weights[a][...], preferred_element_type=jnp.float32)
        else:
            value = lax.dot_general(outs[a][slot], weights[a][...], (((1,), (1,)), ((), ())),
                                    preferred_element_type=jnp.float32)
        prods[a][slot] = value.astype(prods[a].dtype)

    ring, core = [], []
    for step in range(nx):
        for a in range(narr):
            src_x = lax.rem(x + 4 * nx - d * step, nx)
            slot = 2 * src_x + k
            if step > 0:
                ring[(step - 1) * narr + a].wait_recv()
            src = chunks[a] if step == 0 else outs[a].at[slot]
            if step < nx - 1:
                cp = pltpu.make_async_remote_copy(
                    src_ref=src, dst_ref=outs[a].at[slot],
                    send_sem=sr.at[a, step], recv_sem=rr.at[a, step],
                    device_id=nextdev, device_id_type=MESH)
                cp.start()
                ring.append(cp)
            cc = pltpu.make_async_remote_copy(
                src_ref=src, dst_ref=outs[a].at[slot],
                send_sem=sc.at[a, step], recv_sem=rc.at[a, step],
                device_id=partner, device_id_type=MESH)
            cc.start()
            core.append(cc)
        for a in range(narr):
            product(a, 2 * lax.rem(x + 4 * nx - d * step, nx) + k)
        if step > 0:
            for a in range(narr):
                core[(step - 1) * narr + a].wait()
            for a in range(narr):
                product(a, 2 * lax.rem(x + 4 * nx + d * (step - 1), nx) + 1 - k)
    for cp in ring:
        cp.wait_send()
    for a in range(narr):
        core[(nx - 1) * narr + a].wait()
    for a in range(narr):
        product(a, 2 * lax.rem(x + 4 * nx + d * (nx - 1), nx) + 1 - k)


def _row_ids():
    me = lax.axis_index("row")
    y = me // 4
    z = me % 4
    k = lax.axis_index("col") % 2
    d = 1 - 2 * k
    return y, z, d


def _row_ag_body(ny, ins, weights, outs, terms, sa, sb, rsem):

    def product(a, slot):
        if a == 0:
            value = jnp.dot(outs[a][slot], weights[a][...], preferred_element_type=jnp.float32)
        else:
            value = lax.dot_general(outs[a][slot], weights[a][...], (((1,), (1,)), ((), ())),
                                    preferred_element_type=jnp.float32)
        _piece(terms[a], slot)[...] = value.astype(terms[a].dtype)

    col = lax.axis_index("col")
    y, z, d = _row_ids()
    me = y * 4 + z
    peers = (y * 4 + lax.rem(z + 4 + d, 4), y * 4 + lax.rem(z + 4 - d, 4),
             lax.rem(y + ny + d, ny) * 4 + z, lax.rem(y + ny - d, ny) * 4 + z)
    geo = []
    for a in range(2):
        if a == 0:
            na, nb = 4, ny
            pos_a, pos_b = z, y
            slot_of = lambda pa, pb: pb * 4 + pa
        else:
            na, nb = ny, 4
            pos_a, pos_b = y, z
            slot_of = lambda pa, pb: pa * 4 + pb
        geo.append((na, nb, pos_a, pos_b, slot_of))
        outs[a][me] = ins[a][...]

    def dev(a, pa, pb):
        return (geo[a][4](pa, pb), col)

    def send(a, src, slot, target, sem):
        cp = pltpu.make_async_remote_copy(
            src_ref=src, dst_ref=outs[a].at[slot], send_sem=sem, recv_sem=rsem.at[a, slot],
            device_id=target, device_id_type=MESH)
        cp.start()
        return cp

    def wait_in(a, slot):
        pltpu.make_async_remote_copy(
            src_ref=ins[a], dst_ref=outs[a].at[slot], send_sem=sa.at[a, 0], recv_sem=rsem.at[a, slot],
            device_id=(peers[0], col), device_id_type=MESH).wait_recv()

    sends = []
    for a in range(2):
        na, nb, pa, pb, slot_of = geo[a]
        next_a = dev(a, lax.rem(pa + na + d, na), pb)
        next_b = dev(a, pa, lax.rem(pb + nb + d, nb))
        sends.append(send(a, ins[a], me, next_a, sa.at[a, 0]))
        sends.append(send(a, ins[a], me, next_b, sb.at[a, 0, 0]))
    for a in range(2):
        product(a, me)
    for s in range(1, 4):
        for a in range(2):
            na, nb, pa, pb, slot_of = geo[a]
            next_a = dev(a, lax.rem(pa + na + d, na), pb)
            next_b = dev(a, pa, lax.rem(pb + nb + d, nb))
            slot = slot_of(lax.rem(pa + 4 * na - d * s, na), pb)
            wait_in(a, slot)
            if s < na - 1:
                sends.append(send(a, outs[a].at[slot], slot, next_a, sa.at[a, s]))
            sends.append(send(a, outs[a].at[slot], slot, next_b, sb.at[a, 0, s]))
            product(a, slot)
    for t in range(1, 4):
        for j in range(4):
            for a in range(2):
                na, nb, pa, pb, slot_of = geo[a]
                next_b = dev(a, pa, lax.rem(pb + nb + d, nb))
                slot = slot_of(lax.rem(pa + 4 * na - d * j, na), lax.rem(pb + 4 * nb - d * t, nb))
                wait_in(a, slot)
                if t < nb - 1:
                    sends.append(send(a, outs[a].at[slot], slot, next_b, sb.at[a, t, j]))
                product(a, slot)
    for cp in sends:
        cp.wait_send()


def _piece(ref, slot):
    half = ref.shape[1] // 2
    return ref.at[slot // 2, pl.ds(pl.multiple_of((slot % 2) * half, half), half)]


def _row_rs_body(ny, ins, outs, sb1, rb1, ssum, sb2, rb2, s1, r1, s2, r2):
    col = lax.axis_index("col")
    y, z, d = _row_ids()
    geo = [(4, ny, z, y, lambda pa, pb: pb * 4 + pa), (ny, 4, y, z, lambda pa, pb: pa * 4 + pb)]

    def dev(a, pa, pb):
        return (geo[a][4](pa, pb), col)

    def send(src, dst, ssem, rsem, target):
        cp = pltpu.make_async_remote_copy(src_ref=src, dst_ref=dst, send_sem=ssem, recv_sem=rsem,
                                          device_id=target, device_id_type=MESH)
        cp.start()
        return cp

    sends = []
    first = {}
    for s in range(4 - 1):
        for bq in range(4):
            for a in range(2):
                na, nb, pa, pb, slot_of = geo[a]
                slot = slot_of(lax.rem(pa + 4 * na - d * (s + 1), na), bq)
                if s == 0:
                    src = _piece(ins[a], slot)
                else:
                    first[(a, s - 1, bq)].wait_recv()
                    sb1[a, s, bq] = (rb1[a, s - 1, bq].astype(jnp.float32)
                                     + _piece(ins[a], slot)[...].astype(jnp.float32)).astype(sb1.dtype)
                    src = sb1.at[a, s, bq]
                cp = send(src, rb1.at[a, s, bq], s1.at[a, s, bq], r1.at[a, s, bq],
                          dev(a, lax.rem(pa + na + d, na), pb))
                sends.append(cp)
                first[(a, s, bq)] = cp
    for bq in range(4):
        for a in range(2):
            na, nb, pa, pb, slot_of = geo[a]
            first[(a, 2, bq)].wait_recv()
            ssum[a, bq] = rb1[a, 2, bq].astype(jnp.float32) + _piece(ins[a], slot_of(pa, bq))[...].astype(jnp.float32)
    second = [[] for _ in range(2)]
    for t in range(4 - 1):
        for a in range(2):
            na, nb, pa, pb, slot_of = geo[a]
            pos = lax.rem(pb + 4 * nb - d * (t + 1), nb)
            if t == 0:
                sb2[a, t] = ssum[a, pos].astype(sb2.dtype)
            else:
                sb2[a, t] = (rb2[a, t - 1].astype(jnp.float32) + ssum[a, pos]).astype(sb2.dtype)
            cp = send(sb2.at[a, t], rb2.at[a, t], s2.at[a, t], r2.at[a, t],
                      dev(a, pa, lax.rem(pb + nb + d, nb)))
            sends.append(cp)
            second[a].append(cp)
        for a in range(2):
            second[a][t].wait_recv()
    for a in range(2):
        na, nb, pa, pb, slot_of = geo[a]
        outs[a][...] = rb2[a, 2].astype(jnp.float32) + ssum[a, pb]
    for cp in sends:
        cp.wait_send()


def gelu_grad(value):
    cdf = 0.5 * (1.0 + jax.scipy.special.erf(value * 0.7071067811865476))
    pdf = jnp.exp(-0.5 * value * value) * 0.3989422804014327
    return cdf + value * pdf


def token_panel(local_rows):
    return lax.all_gather(local_rows, "row", axis=0, tiled=True)


def token_panel_a2a(local_rows):
    n = lax.axis_size("row")
    copies = jnp.broadcast_to(local_rows[None], (n,) + local_rows.shape)
    copies = copies.reshape(n * local_rows.shape[0], local_rows.shape[1])
    return lax.all_to_all(copies, "row", split_axis=0, concat_axis=0, tiled=True)


def hidden_panel(local_rows):
    return lax.all_gather(local_rows, "col", axis=0, tiled=True)


def contract_last(left, right):
    return lax.dot_general(
        left, right, (((1,), (1,)), ((), ())), preferred_element_type=jnp.float32
    )


def width_split(left_all, right, transposed):
    if transposed:
        term = contract_last(left_all, right)
    else:
        term = jnp.dot(left_all, right, preferred_element_type=jnp.float32)
    return lax.psum_scatter(
        term.astype(jnp.bfloat16), "col", scatter_dimension=0, tiled=True
    ).astype(jnp.float32)


def unit_sum(left_all, right, transposed):
    n = lax.axis_size("row")
    if transposed:
        term = contract_last(left_all, right)
    else:
        term = jnp.dot(left_all, right, preferred_element_type=jnp.float32)
    pieces = term.astype(jnp.bfloat16).reshape(n, term.shape[0] // n, term.shape[1])
    pieces = lax.all_to_all(pieces, "row", split_axis=0, concat_axis=0, tiled=True)
    return jnp.sum(pieces.astype(jnp.float32), axis=0)


def row_sum(term):
    n = lax.axis_size("row")
    pieces = term.reshape(n, term.shape[0] // n, term.shape[1])
    pieces = lax.all_to_all(pieces, "row", split_axis=0, concat_axis=0, tiled=True)
    return jnp.sum(pieces.astype(jnp.float32), axis=0)


def local(tokens, w_in, w_out, cotangent):
    tokens_all, upstream_all, act_all, dpre_all, mixed, back = fused_block(tokens, cotangent, w_in, w_out, 1)
    block_rows = (tokens.astype(jnp.float32) + mixed).astype(jnp.bfloat16)
    block_out = lax.all_to_all(block_rows, "col", split_axis=0, concat_axis=1, tiled=True)
    grad_out = lax.dot_general(
        act_all, upstream_all, (((0,), (0,)), ((), ())), preferred_element_type=jnp.float32
    )
    grad_in = lax.dot_general(
        tokens_all, dpre_all, (((0,), (0,)), ((), ())), preferred_element_type=jnp.float32
    )
    grad_tokens = (cotangent.astype(jnp.float32) + back).astype(jnp.bfloat16)
    return (block_out, grad_tokens, grad_in, grad_out)


def solution(mesh):
    in_specs = (P("row", "col"), P("col", "row"), P("row", "col"), P("row", "col"))
    out_specs = (P(("row", "col"), None), P("row", "col"), P("col", "row"), P("row", "col"))
    return jax.shard_map(local, mesh=mesh, in_specs=in_specs, out_specs=out_specs, check_vma=False)
```

```python
import jax
import jax.numpy as jnp
from jax import lax
from jax.sharding import PartitionSpec as P
import functools
from jax.experimental import pallas as pl
from jax.experimental.pallas import tpu as pltpu

MESH = pl.DeviceIdType.MESH


def _col_ids(nx):
    me = lax.axis_index("col")
    x = me // 2
    k = me % 2
    d = 1 - 2 * k
    nxt = lax.rem(x + nx + d, nx)
    prv = lax.rem(x + nx - d, nx)
    return x, k, d, nxt, prv


def _greet(row, k, x, nxt, prv):
    barrier = pltpu.get_barrier_semaphore()
    for peer in (2 * x + 1 - k, 2 * nxt + k, 2 * prv + k):
        pl.semaphore_signal(barrier, inc=1, device_id=(row, peer), device_id_type=MESH)
    pl.semaphore_wait(barrier, 3)


def _rs_body(nx, narr, parts, outs, recv1, sendbuf, recv2, s1, r1, s2, r2):
    row = lax.axis_index("row")
    x, k, d, nxt, prv = _col_ids(nx)
    partner = (row, 2 * x + 1 - k)
    nextdev = (row, 2 * nxt + k)

    def order(j, sign):
        if j == nx - 1:
            return x
        return lax.rem(x + 4 * nx + sign * d * (j + 1), nx)

    first = []
    for j in range(nx):
        for a in range(narr):
            cp = pltpu.make_async_remote_copy(
                src_ref=parts[a].at[2 * order(j, 1) + 1 - k], dst_ref=recv1.at[a, j],
                send_sem=s1.at[a, j], recv_sem=r1.at[a, j],
                device_id=partner, device_id_type=MESH)
            cp.start()
            first.append(cp)

    def chip_sum(a, j):
        first[j * narr + a].wait_recv()
        own = parts[a][2 * order(j, -1) + k].astype(jnp.float32)
        return own + recv1[a, j].astype(jnp.float32)

    pieces = 4
    span = outs[0].shape[0] // pieces
    ring = {}
    for step in range(nx - 1):
        for a in range(narr):
            first[step * narr + a].wait_recv()
        for q in range(pieces):
            rows = pl.ds(q * span, span)
            for a in range(narr):
                value = (parts[a][2 * order(step, -1) + k, rows, :].astype(jnp.float32)
                         + recv1[a, step, rows, :].astype(jnp.float32))
                if step == 0:
                    sendbuf[a, step, rows, :] = value.astype(sendbuf.dtype)
                else:
                    ring[(a, step - 1, q)].wait_recv()
                    sendbuf[a, step, rows, :] = (recv2[a, step - 1, rows, :].astype(jnp.float32)
                                                 + value).astype(sendbuf.dtype)
                cp = pltpu.make_async_remote_copy(
                    src_ref=sendbuf.at[a, step, rows], dst_ref=recv2.at[a, step, rows],
                    send_sem=s2.at[a, step, q], recv_sem=r2.at[a, step, q],
                    device_id=nextdev, device_id_type=MESH)
                cp.start()
                ring[(a, step, q)] = cp
    for a in range(narr):
        first[(nx - 1) * narr + a].wait_recv()
    for q in range(pieces):
        rows = pl.ds(q * span, span)
        sums = []
        for a in range(narr):
            value = (parts[a][2 * x + k, rows, :].astype(jnp.float32)
                     + recv1[a, nx - 1, rows, :].astype(jnp.float32))
            ring[(a, nx - 2, q)].wait_recv()
            sums.append(recv2[a, nx - 2, rows, :].astype(jnp.float32) + value)
        pre, dact = sums
        cdf = 0.5 * (1.0 + jax.scipy.special.erf(pre * 0.7071067811865476))
        outs[0][rows, :] = (pre * cdf).astype(outs[0].dtype)
        outs[1][rows, :] = (dact * gelu_grad(pre)).astype(outs[1].dtype)
    for cp in first:
        cp.wait_send()
    for cp in ring.values():
        cp.wait_send()


def _col_kernel(nx, ny, narr, *refs):
    tokens, cot, w_in, w_out = refs[:4]
    panels = refs[4:6]
    outs = refs[6:8]
    sums = refs[8:10]
    parts = refs[10:12]
    prods = refs[12:14]
    scratch = refs[14:]
    weights = [w_out, w_in]
    row = lax.axis_index("row")
    x, k, d, nxt, prv = _col_ids(nx)
    barrier = pltpu.get_barrier_semaphore()
    for peer in (2 * x + 1 - k, 2 * nxt + k, 2 * prv + k):
        pl.semaphore_signal(barrier, inc=1, device_id=(row, peer), device_id_type=MESH)
    y, z, dr = _row_ids()
    for p in (y * 4 + lax.rem(z + 4 + dr, 4), y * 4 + lax.rem(z + 4 - dr, 4),
              lax.rem(y + ny + dr, ny) * 4 + z, lax.rem(y + ny - dr, ny) * 4 + z):
        pl.semaphore_signal(barrier, inc=1, device_id=(p, 2 * x + k), device_id_type=MESH)
    pl.semaphore_wait(barrier, 7)
    _row_ag_body(ny, [tokens, cot], [w_in, w_out], panels, parts, *scratch[20:23])
    own = [o.at[2 * x + k] for o in outs]
    _rs_body(nx, narr, parts, own, *scratch[:7])
    _ag_body(nx, narr, own, weights, outs, prods, *scratch[7:11])
    _row_rs_body(ny, prods, sums, [tokens, cot], *scratch[11:20])


def fused_block(tokens, cotangent, w_in, w_out, cid):
    n = lax.axis_size("col")
    nx = n // 2
    narr = 2
    nr = lax.axis_size("row")
    ny = nr // 4
    piece, model = tokens.shape
    hidden = w_in.shape[1]
    rows = piece * nr // n
    cols = hidden
    width = model
    res = pl.pallas_call(
        functools.partial(_col_kernel, nx, ny, narr),
        out_shape=[jax.ShapeDtypeStruct((nr, piece, model), jnp.bfloat16)] * 2
        + [jax.ShapeDtypeStruct((n, rows, cols), jnp.bfloat16)] * narr
        + [jax.ShapeDtypeStruct((piece, width), jnp.bfloat16)] * narr,
        in_specs=[pl.BlockSpec(memory_space=pltpu.VMEM)] * 4,
        out_specs=[pl.BlockSpec(memory_space=pltpu.VMEM)] * 6,
        scratch_shapes=[pltpu.VMEM((n, rows, cols), jnp.bfloat16)] * narr
        + [pltpu.VMEM((n, rows, width), jnp.bfloat16)] * narr + [
            pltpu.VMEM((narr, nx, rows, cols), jnp.bfloat16),
            pltpu.VMEM((narr, nx - 1, rows, cols), jnp.bfloat16),
            pltpu.VMEM((narr, nx - 1, rows, cols), jnp.bfloat16),
            pltpu.SemaphoreType.DMA((narr, nx)),
            pltpu.SemaphoreType.DMA((narr, nx)),
            pltpu.SemaphoreType.DMA((narr, nx - 1, 4)),
            pltpu.SemaphoreType.DMA((narr, nx - 1, 4)),
            pltpu.SemaphoreType.DMA((narr, nx)),
            pltpu.SemaphoreType.DMA((narr, nx)),
            pltpu.SemaphoreType.DMA((narr, nx)),
            pltpu.SemaphoreType.DMA((narr, nx)),
            pltpu.VMEM((2, 3, 4, piece, width), jnp.bfloat16),
            pltpu.VMEM((2, 3, 4, piece, width), jnp.bfloat16),
            pltpu.VMEM((2, 4, piece, width), jnp.float32),
            pltpu.VMEM((2, 3, piece, width), jnp.bfloat16),
            pltpu.VMEM((2, 3, piece, width), jnp.bfloat16),
            pltpu.SemaphoreType.DMA((2, 3, 4)),
            pltpu.SemaphoreType.DMA((2, 3, 4)),
            pltpu.SemaphoreType.DMA((2, 3)),
            pltpu.SemaphoreType.DMA((2, 3)),
            pltpu.SemaphoreType.DMA((2, 4)),
            pltpu.SemaphoreType.DMA((2, 4, 4)),
            pltpu.SemaphoreType.DMA((2, nr)),
        ],
        compiler_params=pltpu.CompilerParams(collective_id=cid, has_side_effects=True,
                                             vmem_limit_bytes=64 * 1024 * 1024),
    )(tokens, cotangent, w_in, w_out)
    return ([o.reshape(nr * piece, model) for o in res[:2]]
            + [o.reshape(n * rows, cols) for o in res[2:4]] + list(res[4:]))


def _ag_body(nx, narr, chunks, weights, outs, prods, sr, rr, sc, rc):
    row = lax.axis_index("row")
    x, k, d, nxt, prv = _col_ids(nx)
    me = 2 * x + k
    partner = (row, 2 * x + 1 - k)
    nextdev = (row, 2 * nxt + k)

    def product(a, slot):
        if a == 0:
            value = jnp.dot(outs[a][slot], weights[a][...], preferred_element_type=jnp.float32)
        else:
            value = lax.dot_general(outs[a][slot], weights[a][...], (((1,), (1,)), ((), ())),
                                    preferred_element_type=jnp.float32)
        prods[a][slot] = value.astype(prods[a].dtype)

    ring, core = [], []
    for step in range(nx):
        for a in range(narr):
            src_x = lax.rem(x + 4 * nx - d * step, nx)
            slot = 2 * src_x + k
            if step > 0:
                ring[(step - 1) * narr + a].wait_recv()
            src = chunks[a] if step == 0 else outs[a].at[slot]
            if step < nx - 1:
                cp = pltpu.make_async_remote_copy(
                    src_ref=src, dst_ref=outs[a].at[slot],
                    send_sem=sr.at[a, step], recv_sem=rr.at[a, step],
                    device_id=nextdev, device_id_type=MESH)
                cp.start()
                ring.append(cp)
            cc = pltpu.make_async_remote_copy(
                src_ref=src, dst_ref=outs[a].at[slot],
                send_sem=sc.at[a, step], recv_sem=rc.at[a, step],
                device_id=partner, device_id_type=MESH)
            cc.start()
            core.append(cc)
        for a in range(narr):
            product(a, 2 * lax.rem(x + 4 * nx - d * step, nx) + k)
        if step > 0:
            for a in range(narr):
                core[(step - 1) * narr + a].wait()
            for a in range(narr):
                product(a, 2 * lax.rem(x + 4 * nx + d * (step - 1), nx) + 1 - k)
    for cp in ring:
        cp.wait_send()
    for a in range(narr):
        core[(nx - 1) * narr + a].wait()
    for a in range(narr):
        product(a, 2 * lax.rem(x + 4 * nx + d * (nx - 1), nx) + 1 - k)


def _row_ids():
    me = lax.axis_index("row")
    y = me // 4
    z = me % 4
    k = lax.axis_index("col") % 2
    d = 1 - 2 * k
    return y, z, d


def _row_ag_body(ny, ins, weights, outs, terms, sa, sb, rsem):

    def product(a, slot):
        if a == 0:
            value = jnp.dot(outs[a][slot], weights[a][...], preferred_element_type=jnp.float32)
        else:
            value = lax.dot_general(outs[a][slot], weights[a][...], (((1,), (1,)), ((), ())),
                                    preferred_element_type=jnp.float32)
        _piece(terms[a], slot)[...] = value.astype(terms[a].dtype)

    col = lax.axis_index("col")
    y, z, d = _row_ids()
    me = y * 4 + z
    peers = (y * 4 + lax.rem(z + 4 + d, 4), y * 4 + lax.rem(z + 4 - d, 4),
             lax.rem(y + ny + d, ny) * 4 + z, lax.rem(y + ny - d, ny) * 4 + z)
    geo = []
    for a in range(2):
        if a == 0:
            na, nb = 4, ny
            pos_a, pos_b = z, y
            slot_of = lambda pa, pb: pb * 4 + pa
        else:
            na, nb = ny, 4
            pos_a, pos_b = y, z
            slot_of = lambda pa, pb: pa * 4 + pb
        geo.append((na, nb, pos_a, pos_b, slot_of))
        outs[a][me] = ins[a][...]

    def dev(a, pa, pb):
        return (geo[a][4](pa, pb), col)

    def send(a, src, slot, target, sem):
        cp = pltpu.make_async_remote_copy(
            src_ref=src, dst_ref=outs[a].at[slot], send_sem=sem, recv_sem=rsem.at[a, slot],
            device_id=target, device_id_type=MESH)
        cp.start()
        return cp

    def wait_in(a, slot):
        pltpu.make_async_remote_copy(
            src_ref=ins[a], dst_ref=outs[a].at[slot], send_sem=sa.at[a, 0], recv_sem=rsem.at[a, slot],
            device_id=(peers[0], col), device_id_type=MESH).wait_recv()

    sends = []
    for a in range(2):
        na, nb, pa, pb, slot_of = geo[a]
        next_a = dev(a, lax.rem(pa + na + d, na), pb)
        next_b = dev(a, pa, lax.rem(pb + nb + d, nb))
        sends.append(send(a, ins[a], me, next_a, sa.at[a, 0]))
        sends.append(send(a, ins[a], me, next_b, sb.at[a, 0, 0]))
    for a in range(2):
        product(a, me)
    for s in range(1, 4):
        for a in range(2):
            na, nb, pa, pb, slot_of = geo[a]
            next_a = dev(a, lax.rem(pa + na + d, na), pb)
            next_b = dev(a, pa, lax.rem(pb + nb + d, nb))
            slot = slot_of(lax.rem(pa + 4 * na - d * s, na), pb)
            wait_in(a, slot)
            if s < na - 1:
                sends.append(send(a, outs[a].at[slot], slot, next_a, sa.at[a, s]))
            sends.append(send(a, outs[a].at[slot], slot, next_b, sb.at[a, 0, s]))
            product(a, slot)
    for t in range(1, 4):
        for j in range(4):
            for a in range(2):
                na, nb, pa, pb, slot_of = geo[a]
                next_b = dev(a, pa, lax.rem(pb + nb + d, nb))
                slot = slot_of(lax.rem(pa + 4 * na - d * j, na), lax.rem(pb + 4 * nb - d * t, nb))
                wait_in(a, slot)
                if t < nb - 1:
                    sends.append(send(a, outs[a].at[slot], slot, next_b, sb.at[a, t, j]))
                product(a, slot)
    for cp in sends:
        cp.wait_send()


def _piece(ref, slot):
    half = ref.shape[1] // 2
    return ref.at[slot // 2, pl.ds(pl.multiple_of((slot % 2) * half, half), half)]


def _row_rs_body(ny, ins, outs, addends, sb1, rb1, ssum, sb2, rb2, s1, r1, s2, r2):
    col = lax.axis_index("col")
    y, z, d = _row_ids()
    geo = [(4, ny, z, y, lambda pa, pb: pb * 4 + pa), (ny, 4, y, z, lambda pa, pb: pa * 4 + pb)]

    def dev(a, pa, pb):
        return (geo[a][4](pa, pb), col)

    def send(src, dst, ssem, rsem, target):
        cp = pltpu.make_async_remote_copy(src_ref=src, dst_ref=dst, send_sem=ssem, recv_sem=rsem,
                                          device_id=target, device_id_type=MESH)
        cp.start()
        return cp

    sends = []
    first = {}
    for s in range(4 - 1):
        for bq in range(4):
            for a in range(2):
                na, nb, pa, pb, slot_of = geo[a]
                slot = slot_of(lax.rem(pa + 4 * na - d * (s + 1), na), bq)
                if s == 0:
                    src = _piece(ins[a], slot)
                else:
                    first[(a, s - 1, bq)].wait_recv()
                    sb1[a, s, bq] = (rb1[a, s - 1, bq].astype(jnp.float32)
                                     + _piece(ins[a], slot)[...].astype(jnp.float32)).astype(sb1.dtype)
                    src = sb1.at[a, s, bq]
                cp = send(src, rb1.at[a, s, bq], s1.at[a, s, bq], r1.at[a, s, bq],
                          dev(a, lax.rem(pa + na + d, na), pb))
                sends.append(cp)
                first[(a, s, bq)] = cp
    for bq in range(4):
        for a in range(2):
            na, nb, pa, pb, slot_of = geo[a]
            first[(a, 2, bq)].wait_recv()
            ssum[a, bq] = rb1[a, 2, bq].astype(jnp.float32) + _piece(ins[a], slot_of(pa, bq))[...].astype(jnp.float32)
    second = [[] for _ in range(2)]
    for t in range(4 - 1):
        for a in range(2):
            na, nb, pa, pb, slot_of = geo[a]
            pos = lax.rem(pb + 4 * nb - d * (t + 1), nb)
            if t == 0:
                sb2[a, t] = ssum[a, pos].astype(sb2.dtype)
            else:
                sb2[a, t] = (rb2[a, t - 1].astype(jnp.float32) + ssum[a, pos]).astype(sb2.dtype)
            cp = send(sb2.at[a, t], rb2.at[a, t], s2.at[a, t], r2.at[a, t],
                      dev(a, pa, lax.rem(pb + nb + d, nb)))
            sends.append(cp)
            second[a].append(cp)
        for a in range(2):
            second[a][t].wait_recv()
    for a in range(2):
        na, nb, pa, pb, slot_of = geo[a]
        outs[a][...] = (addends[a][...].astype(jnp.float32) + rb2[a, 2].astype(jnp.float32)
                        + ssum[a, pb]).astype(outs[a].dtype)
    for cp in sends:
        cp.wait_send()


def gelu_grad(value):
    cdf = 0.5 * (1.0 + jax.scipy.special.erf(value * 0.7071067811865476))
    pdf = jnp.exp(-0.5 * value * value) * 0.3989422804014327
    return cdf + value * pdf


def token_panel(local_rows):
    return lax.all_gather(local_rows, "row", axis=0, tiled=True)


def token_panel_a2a(local_rows):
    n = lax.axis_size("row")
    copies = jnp.broadcast_to(local_rows[None], (n,) + local_rows.shape)
    copies = copies.reshape(n * local_rows.shape[0], local_rows.shape[1])
    return lax.all_to_all(copies, "row", split_axis=0, concat_axis=0, tiled=True)


def hidden_panel(local_rows):
    return lax.all_gather(local_rows, "col", axis=0, tiled=True)


def contract_last(left, right):
    return lax.dot_general(
        left, right, (((1,), (1,)), ((), ())), preferred_element_type=jnp.float32
    )


def width_split(left_all, right, transposed):
    if transposed:
        term = contract_last(left_all, right)
    else:
        term = jnp.dot(left_all, right, preferred_element_type=jnp.float32)
    return lax.psum_scatter(
        term.astype(jnp.bfloat16), "col", scatter_dimension=0, tiled=True
    ).astype(jnp.float32)


def unit_sum(left_all, right, transposed):
    n = lax.axis_size("row")
    if transposed:
        term = contract_last(left_all, right)
    else:
        term = jnp.dot(left_all, right, preferred_element_type=jnp.float32)
    pieces = term.astype(jnp.bfloat16).reshape(n, term.shape[0] // n, term.shape[1])
    pieces = lax.all_to_all(pieces, "row", split_axis=0, concat_axis=0, tiled=True)
    return jnp.sum(pieces.astype(jnp.float32), axis=0)


def row_sum(term):
    n = lax.axis_size("row")
    pieces = term.reshape(n, term.shape[0] // n, term.shape[1])
    pieces = lax.all_to_all(pieces, "row", split_axis=0, concat_axis=0, tiled=True)
    return jnp.sum(pieces.astype(jnp.float32), axis=0)


def local(tokens, w_in, w_out, cotangent):
    tokens_all, upstream_all, act_all, dpre_all, block_rows, grad_tokens = fused_block(
        tokens, cotangent, w_in, w_out, 1)
    block_out = lax.all_to_all(block_rows, "col", split_axis=0, concat_axis=1, tiled=True)
    grad_out = lax.dot_general(
        act_all, upstream_all, (((0,), (0,)), ((), ())), preferred_element_type=jnp.float32
    )
    grad_in = lax.dot_general(
        tokens_all, dpre_all, (((0,), (0,)), ((), ())), preferred_element_type=jnp.float32
    )
    return (block_out, grad_tokens, grad_in, grad_out)


def solution(mesh):
    in_specs = (P("row", "col"), P("col", "row"), P("row", "col"), P("row", "col"))
    out_specs = (P(("row", "col"), None), P("row", "col"), P("col", "row"), P("row", "col"))
    return jax.shard_map(local, mesh=mesh, in_specs=in_specs, out_specs=out_specs, check_vma=False)
```

```python
import jax
import jax.numpy as jnp
from jax import lax
from jax.sharding import PartitionSpec as P
import functools
from jax.experimental import pallas as pl
from jax.experimental.pallas import tpu as pltpu

MESH = pl.DeviceIdType.MESH


def _col_ids(nx):
    me = lax.axis_index("col")
    x = me // 2
    k = me % 2
    d = 1 - 2 * k
    nxt = lax.rem(x + nx + d, nx)
    prv = lax.rem(x + nx - d, nx)
    return x, k, d, nxt, prv


def _greet(row, k, x, nxt, prv):
    barrier = pltpu.get_barrier_semaphore()
    me_c = 2 * x + k
    for o in range(1, 2 * nx):
        pl.semaphore_signal(barrier, inc=1, device_id=(row, lax.rem(me_c + o, 2 * nx)), device_id_type=MESH)
    pl.semaphore_wait(barrier, 3)


def _rs_body(nx, narr, parts, outs, recv1, sendbuf, recv2, s1, r1, s2, r2):
    row = lax.axis_index("row")
    x, k, d, nxt, prv = _col_ids(nx)
    partner = (row, 2 * x + 1 - k)
    nextdev = (row, 2 * nxt + k)

    def order(j, sign):
        if j == nx - 1:
            return x
        return lax.rem(x + 4 * nx + sign * d * (j + 1), nx)

    first = []
    for j in range(nx):
        for a in range(narr):
            cp = pltpu.make_async_remote_copy(
                src_ref=parts[a].at[2 * order(j, 1) + 1 - k], dst_ref=recv1.at[a, j],
                send_sem=s1.at[a, j], recv_sem=r1.at[a, j],
                device_id=partner, device_id_type=MESH)
            cp.start()
            first.append(cp)

    def chip_sum(a, j):
        first[j * narr + a].wait_recv()
        own = parts[a][2 * order(j, -1) + k].astype(jnp.float32)
        return own + recv1[a, j].astype(jnp.float32)

    pieces = 4
    span = outs[0].shape[0] // pieces
    ring = {}
    for step in range(nx - 1):
        for a in range(narr):
            first[step * narr + a].wait_recv()
        for q in range(pieces):
            rows = pl.ds(q * span, span)
            for a in range(narr):
                value = (parts[a][2 * order(step, -1) + k, rows, :].astype(jnp.float32)
                         + recv1[a, step, rows, :].astype(jnp.float32))
                if step == 0:
                    sendbuf[a, step, rows, :] = value.astype(sendbuf.dtype)
                else:
                    ring[(a, step - 1, q)].wait_recv()
                    sendbuf[a, step, rows, :] = (recv2[a, step - 1, rows, :].astype(jnp.float32)
                                                 + value).astype(sendbuf.dtype)
                cp = pltpu.make_async_remote_copy(
                    src_ref=sendbuf.at[a, step, rows], dst_ref=recv2.at[a, step, rows],
                    send_sem=s2.at[a, step, q], recv_sem=r2.at[a, step, q],
                    device_id=nextdev, device_id_type=MESH)
                cp.start()
                ring[(a, step, q)] = cp
    for a in range(narr):
        first[(nx - 1) * narr + a].wait_recv()
    for q in range(pieces):
        rows = pl.ds(q * span, span)
        sums = []
        for a in range(narr):
            value = (parts[a][2 * x + k, rows, :].astype(jnp.float32)
                     + recv1[a, nx - 1, rows, :].astype(jnp.float32))
            ring[(a, nx - 2, q)].wait_recv()
            sums.append(recv2[a, nx - 2, rows, :].astype(jnp.float32) + value)
        pre, dact = sums
        cdf = 0.5 * (1.0 + jax.scipy.special.erf(pre * 0.7071067811865476))
        outs[0][rows, :] = (pre * cdf).astype(outs[0].dtype)
        outs[1][rows, :] = (dact * gelu_grad(pre)).astype(outs[1].dtype)
    for cp in first:
        cp.wait_send()
    for cp in ring.values():
        cp.wait_send()


def _col_kernel(nx, ny, narr, *refs):
    tokens, cot, w_in, w_out = refs[:4]
    panels = refs[4:6]
    outs = refs[6:8]
    sums = refs[8:10]
    final = refs[10]
    parts = refs[11:13]
    prods = refs[13:15]
    scratch = refs[15:]
    weights = [w_out, w_in]
    row = lax.axis_index("row")
    x, k, d, nxt, prv = _col_ids(nx)
    barrier = pltpu.get_barrier_semaphore()
    me_c = 2 * x + k
    for o in range(1, 2 * nx):
        pl.semaphore_signal(barrier, inc=1, device_id=(row, lax.rem(me_c + o, 2 * nx)), device_id_type=MESH)
    y, z, dr = _row_ids()
    for p in (y * 4 + lax.rem(z + 4 + dr, 4), y * 4 + lax.rem(z + 4 - dr, 4),
              lax.rem(y + ny + dr, ny) * 4 + z, lax.rem(y + ny - dr, ny) * 4 + z):
        pl.semaphore_signal(barrier, inc=1, device_id=(p, 2 * x + k), device_id_type=MESH)
    pl.semaphore_wait(barrier, 2 * nx - 1 + 4)
    _row_ag_body(ny, [tokens, cot], [w_in, w_out], panels, parts, *scratch[20:23])
    own = [o.at[2 * x + k] for o in outs]
    _rs_body(nx, narr, parts, own, *scratch[:7])
    _ag_body(nx, narr, own, weights, outs, prods, *scratch[7:11])
    _row_rs_body(ny, prods, sums, [tokens, cot], *scratch[11:20])
    span = final.shape[0]
    width = sums[0].shape[1]
    final[:, pl.ds(pl.multiple_of(me_c * width, width), width)] = sums[0][pl.ds(pl.multiple_of(me_c * span, span), span), :]
    spread = []
    for o in range(1, 2 * nx):
        peer = lax.rem(me_c + o, 2 * nx)
        cp = pltpu.make_async_remote_copy(
            src_ref=sums[0].at[pl.ds(pl.multiple_of(peer * span, span), span)],
            dst_ref=final.at[:, pl.ds(pl.multiple_of(me_c * width, width), width)],
            send_sem=scratch[23].at[o], recv_sem=scratch[24].at[o],
            device_id=(row, peer), device_id_type=MESH)
        cp.start()
        spread.append(cp)
    for cp in spread:
        cp.wait()


def fused_block(tokens, cotangent, w_in, w_out, cid):
    n = lax.axis_size("col")
    nx = n // 2
    narr = 2
    nr = lax.axis_size("row")
    ny = nr // 4
    piece, model = tokens.shape
    hidden = w_in.shape[1]
    rows = piece * nr // n
    cols = hidden
    width = model
    res = pl.pallas_call(
        functools.partial(_col_kernel, nx, ny, narr),
        out_shape=[jax.ShapeDtypeStruct((nr, piece, model), jnp.bfloat16)] * 2
        + [jax.ShapeDtypeStruct((n, rows, cols), jnp.bfloat16)] * narr
        + [jax.ShapeDtypeStruct((piece, width), jnp.bfloat16)] * narr
        + [jax.ShapeDtypeStruct((piece // n, width * n), jnp.bfloat16)],
        in_specs=[pl.BlockSpec(memory_space=pltpu.VMEM)] * 4,
        out_specs=[pl.BlockSpec(memory_space=pltpu.VMEM)] * 7,
        scratch_shapes=[pltpu.VMEM((n, rows, cols), jnp.bfloat16)] * narr
        + [pltpu.VMEM((n, rows, width), jnp.bfloat16)] * narr + [
            pltpu.VMEM((narr, nx, rows, cols), jnp.bfloat16),
            pltpu.VMEM((narr, nx - 1, rows, cols), jnp.bfloat16),
            pltpu.VMEM((narr, nx - 1, rows, cols), jnp.bfloat16),
            pltpu.SemaphoreType.DMA((narr, nx)),
            pltpu.SemaphoreType.DMA((narr, nx)),
            pltpu.SemaphoreType.DMA((narr, nx - 1, 4)),
            pltpu.SemaphoreType.DMA((narr, nx - 1, 4)),
            pltpu.SemaphoreType.DMA((narr, nx)),
            pltpu.SemaphoreType.DMA((narr, nx)),
            pltpu.SemaphoreType.DMA((narr, nx)),
            pltpu.SemaphoreType.DMA((narr, nx)),
            pltpu.VMEM((2, 3, 4, piece, width), jnp.bfloat16),
            pltpu.VMEM((2, 3, 4, piece, width), jnp.bfloat16),
            pltpu.VMEM((2, 4, piece, width), jnp.float32),
            pltpu.VMEM((2, 3, piece, width), jnp.bfloat16),
            pltpu.VMEM((2, 3, piece, width), jnp.bfloat16),
            pltpu.SemaphoreType.DMA((2, 3, 4)),
            pltpu.SemaphoreType.DMA((2, 3, 4)),
            pltpu.SemaphoreType.DMA((2, 3)),
            pltpu.SemaphoreType.DMA((2, 3)),
            pltpu.SemaphoreType.DMA((2, 4)),
            pltpu.SemaphoreType.DMA((2, 4, 4)),
            pltpu.SemaphoreType.DMA((2, nr)),
            pltpu.SemaphoreType.DMA((n,)),
            pltpu.SemaphoreType.DMA((n,)),
        ],
        compiler_params=pltpu.CompilerParams(collective_id=cid, has_side_effects=True,
                                             vmem_limit_bytes=64 * 1024 * 1024),
    )(tokens, cotangent, w_in, w_out)
    return ([o.reshape(nr * piece, model) for o in res[:2]]
            + [o.reshape(n * rows, cols) for o in res[2:4]] + list(res[4:]))


def _ag_body(nx, narr, chunks, weights, outs, prods, sr, rr, sc, rc):
    row = lax.axis_index("row")
    x, k, d, nxt, prv = _col_ids(nx)
    me = 2 * x + k
    partner = (row, 2 * x + 1 - k)
    nextdev = (row, 2 * nxt + k)

    def product(a, slot):
        if a == 0:
            value = jnp.dot(outs[a][slot], weights[a][...], preferred_element_type=jnp.float32)
        else:
            value = lax.dot_general(outs[a][slot], weights[a][...], (((1,), (1,)), ((), ())),
                                    preferred_element_type=jnp.float32)
        prods[a][slot] = value.astype(prods[a].dtype)

    ring, core = [], []
    for step in range(nx):
        for a in range(narr):
            src_x = lax.rem(x + 4 * nx - d * step, nx)
            slot = 2 * src_x + k
            if step > 0:
                ring[(step - 1) * narr + a].wait_recv()
            src = chunks[a] if step == 0 else outs[a].at[slot]
            if step < nx - 1:
                cp = pltpu.make_async_remote_copy(
                    src_ref=src, dst_ref=outs[a].at[slot],
                    send_sem=sr.at[a, step], recv_sem=rr.at[a, step],
                    device_id=nextdev, device_id_type=MESH)
                cp.start()
                ring.append(cp)
            cc = pltpu.make_async_remote_copy(
                src_ref=src, dst_ref=outs[a].at[slot],
                send_sem=sc.at[a, step], recv_sem=rc.at[a, step],
                device_id=partner, device_id_type=MESH)
            cc.start()
            core.append(cc)
        for a in range(narr):
            product(a, 2 * lax.rem(x + 4 * nx - d * step, nx) + k)
        if step > 0:
            for a in range(narr):
                core[(step - 1) * narr + a].wait()
            for a in range(narr):
                product(a, 2 * lax.rem(x + 4 * nx + d * (step - 1), nx) + 1 - k)
    for cp in ring:
        cp.wait_send()
    for a in range(narr):
        core[(nx - 1) * narr + a].wait()
    for a in range(narr):
        product(a, 2 * lax.rem(x + 4 * nx + d * (nx - 1), nx) + 1 - k)


def _row_ids():
    me = lax.axis_index("row")
    y = me // 4
    z = me % 4
    k = lax.axis_index("col") % 2
    d = 1 - 2 * k
    return y, z, d


def _row_ag_body(ny, ins, weights, outs, terms, sa, sb, rsem):

    def product(a, slot):
        if a == 0:
            value = jnp.dot(outs[a][slot], weights[a][...], preferred_element_type=jnp.float32)
        else:
            value = lax.dot_general(outs[a][slot], weights[a][...], (((1,), (1,)), ((), ())),
                                    preferred_element_type=jnp.float32)
        _piece(terms[a], slot)[...] = value.astype(terms[a].dtype)

    col = lax.axis_index("col")
    y, z, d = _row_ids()
    me = y * 4 + z
    peers = (y * 4 + lax.rem(z + 4 + d, 4), y * 4 + lax.rem(z + 4 - d, 4),
             lax.rem(y + ny + d, ny) * 4 + z, lax.rem(y + ny - d, ny) * 4 + z)
    geo = []
    for a in range(2):
        if a == 0:
            na, nb = 4, ny
            pos_a, pos_b = z, y
            slot_of = lambda pa, pb: pb * 4 + pa
        else:
            na, nb = ny, 4
            pos_a, pos_b = y, z
            slot_of = lambda pa, pb: pa * 4 + pb
        geo.append((na, nb, pos_a, pos_b, slot_of))
        outs[a][me] = ins[a][...]

    def dev(a, pa, pb):
        return (geo[a][4](pa, pb), col)

    def send(a, src, slot, target, sem):
        cp = pltpu.make_async_remote_copy(
            src_ref=src, dst_ref=outs[a].at[slot], send_sem=sem, recv_sem=rsem.at[a, slot],
            device_id=target, device_id_type=MESH)
        cp.start()
        return cp

    def wait_in(a, slot):
        pltpu.make_async_remote_copy(
            src_ref=ins[a], dst_ref=outs[a].at[slot], send_sem=sa.at[a, 0], recv_sem=rsem.at[a, slot],
            device_id=(peers[0], col), device_id_type=MESH).wait_recv()

    sends = []
    for a in range(2):
        na, nb, pa, pb, slot_of = geo[a]
        next_a = dev(a, lax.rem(pa + na + d, na), pb)
        next_b = dev(a, pa, lax.rem(pb + nb + d, nb))
        sends.append(send(a, ins[a], me, next_a, sa.at[a, 0]))
        sends.append(send(a, ins[a], me, next_b, sb.at[a, 0, 0]))
    for a in range(2):
        product(a, me)
    for s in range(1, 4):
        for a in range(2):
            na, nb, pa, pb, slot_of = geo[a]
            next_a = dev(a, lax.rem(pa + na + d, na), pb)
            next_b = dev(a, pa, lax.rem(pb + nb + d, nb))
            slot = slot_of(lax.rem(pa + 4 * na - d * s, na), pb)
            wait_in(a, slot)
            if s < na - 1:
                sends.append(send(a, outs[a].at[slot], slot, next_a, sa.at[a, s]))
            sends.append(send(a, outs[a].at[slot], slot, next_b, sb.at[a, 0, s]))
            product(a, slot)
    for t in range(1, 4):
        for j in range(4):
            for a in range(2):
                na, nb, pa, pb, slot_of = geo[a]
                next_b = dev(a, pa, lax.rem(pb + nb + d, nb))
                slot = slot_of(lax.rem(pa + 4 * na - d * j, na), lax.rem(pb + 4 * nb - d * t, nb))
                wait_in(a, slot)
                if t < nb - 1:
                    sends.append(send(a, outs[a].at[slot], slot, next_b, sb.at[a, t, j]))
                product(a, slot)
    for cp in sends:
        cp.wait_send()


def _piece(ref, slot):
    half = ref.shape[1] // 2
    return ref.at[slot // 2, pl.ds(pl.multiple_of((slot % 2) * half, half), half)]


def _row_rs_body(ny, ins, outs, addends, sb1, rb1, ssum, sb2, rb2, s1, r1, s2, r2):
    col = lax.axis_index("col")
    y, z, d = _row_ids()
    geo = [(4, ny, z, y, lambda pa, pb: pb * 4 + pa), (ny, 4, y, z, lambda pa, pb: pa * 4 + pb)]

    def dev(a, pa, pb):
        return (geo[a][4](pa, pb), col)

    def send(src, dst, ssem, rsem, target):
        cp = pltpu.make_async_remote_copy(src_ref=src, dst_ref=dst, send_sem=ssem, recv_sem=rsem,
                                          device_id=target, device_id_type=MESH)
        cp.start()
        return cp

    sends = []
    first = {}
    for s in range(4 - 1):
        for bq in range(4):
            for a in range(2):
                na, nb, pa, pb, slot_of = geo[a]
                slot = slot_of(lax.rem(pa + 4 * na - d * (s + 1), na), bq)
                if s == 0:
                    src = _piece(ins[a], slot)
                else:
                    first[(a, s - 1, bq)].wait_recv()
                    sb1[a, s, bq] = (rb1[a, s - 1, bq].astype(jnp.float32)
                                     + _piece(ins[a], slot)[...].astype(jnp.float32)).astype(sb1.dtype)
                    src = sb1.at[a, s, bq]
                cp = send(src, rb1.at[a, s, bq], s1.at[a, s, bq], r1.at[a, s, bq],
                          dev(a, lax.rem(pa + na + d, na), pb))
                sends.append(cp)
                first[(a, s, bq)] = cp
    for bq in range(4):
        for a in range(2):
            na, nb, pa, pb, slot_of = geo[a]
            first[(a, 2, bq)].wait_recv()
            ssum[a, bq] = rb1[a, 2, bq].astype(jnp.float32) + _piece(ins[a], slot_of(pa, bq))[...].astype(jnp.float32)
    second = [[] for _ in range(2)]
    for t in range(4 - 1):
        for a in range(2):
            na, nb, pa, pb, slot_of = geo[a]
            pos = lax.rem(pb + 4 * nb - d * (t + 1), nb)
            if t == 0:
                sb2[a, t] = ssum[a, pos].astype(sb2.dtype)
            else:
                sb2[a, t] = (rb2[a, t - 1].astype(jnp.float32) + ssum[a, pos]).astype(sb2.dtype)
            cp = send(sb2.at[a, t], rb2.at[a, t], s2.at[a, t], r2.at[a, t],
                      dev(a, pa, lax.rem(pb + nb + d, nb)))
            sends.append(cp)
            second[a].append(cp)
        for a in range(2):
            second[a][t].wait_recv()
    for a in range(2):
        na, nb, pa, pb, slot_of = geo[a]
        outs[a][...] = (addends[a][...].astype(jnp.float32) + rb2[a, 2].astype(jnp.float32)
                        + ssum[a, pb]).astype(outs[a].dtype)
    for cp in sends:
        cp.wait_send()


def gelu_grad(value):
    cdf = 0.5 * (1.0 + jax.scipy.special.erf(value * 0.7071067811865476))
    pdf = jnp.exp(-0.5 * value * value) * 0.3989422804014327
    return cdf + value * pdf


def token_panel(local_rows):
    return lax.all_gather(local_rows, "row", axis=0, tiled=True)


def token_panel_a2a(local_rows):
    n = lax.axis_size("row")
    copies = jnp.broadcast_to(local_rows[None], (n,) + local_rows.shape)
    copies = copies.reshape(n * local_rows.shape[0], local_rows.shape[1])
    return lax.all_to_all(copies, "row", split_axis=0, concat_axis=0, tiled=True)


def hidden_panel(local_rows):
    return lax.all_gather(local_rows, "col", axis=0, tiled=True)


def contract_last(left, right):
    return lax.dot_general(
        left, right, (((1,), (1,)), ((), ())), preferred_element_type=jnp.float32
    )


def width_split(left_all, right, transposed):
    if transposed:
        term = contract_last(left_all, right)
    else:
        term = jnp.dot(left_all, right, preferred_element_type=jnp.float32)
    return lax.psum_scatter(
        term.astype(jnp.bfloat16), "col", scatter_dimension=0, tiled=True
    ).astype(jnp.float32)


def unit_sum(left_all, right, transposed):
    n = lax.axis_size("row")
    if transposed:
        term = contract_last(left_all, right)
    else:
        term = jnp.dot(left_all, right, preferred_element_type=jnp.float32)
    pieces = term.astype(jnp.bfloat16).reshape(n, term.shape[0] // n, term.shape[1])
    pieces = lax.all_to_all(pieces, "row", split_axis=0, concat_axis=0, tiled=True)
    return jnp.sum(pieces.astype(jnp.float32), axis=0)


def row_sum(term):
    n = lax.axis_size("row")
    pieces = term.reshape(n, term.shape[0] // n, term.shape[1])
    pieces = lax.all_to_all(pieces, "row", split_axis=0, concat_axis=0, tiled=True)
    return jnp.sum(pieces.astype(jnp.float32), axis=0)


def local(tokens, w_in, w_out, cotangent):
    tokens_all, upstream_all, act_all, dpre_all, block_rows, grad_tokens, block_out = fused_block(
        tokens, cotangent, w_in, w_out, 1)
    grad_out = lax.dot_general(
        act_all, upstream_all, (((0,), (0,)), ((), ())), preferred_element_type=jnp.float32
    )
    grad_in = lax.dot_general(
        tokens_all, dpre_all, (((0,), (0,)), ((), ())), preferred_element_type=jnp.float32
    )
    return (block_out, grad_tokens, grad_in, grad_out)


def solution(mesh):
    in_specs = (P("row", "col"), P("col", "row"), P("row", "col"), P("row", "col"))
    out_specs = (P(("row", "col"), None), P("row", "col"), P("col", "row"), P("row", "col"))
    return jax.shard_map(local, mesh=mesh, in_specs=in_specs, out_specs=out_specs, check_vma=False)
```
